32 devices in a mesh: parts: 2 (over x), tm: 16 (over z, y, core).
Axes of the slice: x: 2, y: 2, z: 4, core: 2. Of those that a mesh axis runs over, the one named last changes fastest.
Arguments:
- query_states: bfloat16 [32, 384, 768], P(('parts', 'tm')), parts along dimension 0, may hold values from -88 to 88
- key_states: bfloat16 [32, 384, 768], P(('parts', 'tm')), parts along dimension 0, may hold values from -4 to 4
- value_states: bfloat16 [32, 384, 768], P(('parts', 'tm')), parts along dimension 0, may hold values from -40 to 40
- out_weight: bfloat16 [1536, 3072], replicated, may hold values from -0.15625 to 0.15625
Outputs:
- mixed: bfloat16 [6144, 3072], P(('parts', 'tm')), parts along dimension 0
The draws below stay inside these ranges and needn't reach their ends.
There are 2 independent parts, one for each index of `parts`. The reference program is written for one: setup_inputs(seed, part) draws one part's arguments, and reference() takes and returns one part's arrays. A program takes and returns all parts, laid end to end along the dimension named above; an argument that names none is the same for every part. Nothing has to cross between parts.
All inputs are finite; a program needn't handle non-finite values.
Results may differ from the reference program's by a relative error of at most 0.0058.
Values may be sent and summed in bfloat16 or wider, within the bound.
A program may use at most 128 MiB of HBM per device.

```python
import jax
import jax.numpy as jnp
from jax import lax

TCOLS = 4
HEADS = 12
HD = 128
D = 3072
TOK_DEV = 384
TILES = 8
T_TILES = 2
TOKENS = 3072


def to_blocks(grid):
    half_width = grid.shape[2] // 2
    return grid.reshape(TILES, TOK_DEV, 2, half_width).transpose(0, 2, 1, 3).reshape(2 * TILES, TOK_DEV, half_width)


def key_grid(key):
    normal_draw = jax.random.normal(jax.random.fold_in(key, 7), (TILES, TOK_DEV, HEADS * HD), jnp.float32)
    values_out = jnp.clip(normal_draw, -4.0, 4.0)
    sign_draw = jnp.where(jax.random.bernoulli(jax.random.fold_in(key, 13), 0.5, (TILES,)), 4.0, -4.0)
    last_col = HEADS * HD - 1
    pick_row = 5 % TOK_DEV
    values_out = values_out.at[:, pick_row, last_col].set(sign_draw)
    values_out = values_out.at[:, pick_row, last_col - 1].set(-sign_draw)
    return values_out


def draw_key_states(key, part):
    values_out = key_grid(key)
    return to_blocks(values_out).astype(jnp.bfloat16)


def draw_query_states(key, part):
    normal_draw = jax.random.normal(jax.random.fold_in(key, 3), (TILES, TOK_DEV, HEADS * HD), jnp.float32)
    values_out = jnp.clip(normal_draw, -4.0, 4.0)
    return to_blocks(values_out).astype(jnp.bfloat16)


def shard_levels(stream_key, shape, cuts, low, high):
    level = 1.0
    for position, blocks in cuts:
        draws = jax.random.uniform(jax.random.fold_in(jax.random.fold_in(stream_key, 6), position), (blocks,), jnp.float32, low / len(cuts), high / len(cuts))
        level = level * jnp.repeat(jnp.exp(draws), shape[position] // blocks).reshape((-1,) + (1,) * (len(shape) - 1 - position))
    return level


def gaussian(key, dims, scale, most, cuts=(), held_as=jnp.bfloat16):
    loudness = shard_levels(key, dims, cuts, -0.22, 0.18) if cuts else 1.0
    values = jax.random.normal(key, dims, jnp.float32) * scale * loudness
    return jnp.minimum(jnp.maximum(values, -most), most).astype(held_as)


def setup_inputs(seed: int = 0, part: int = 0) -> dict:
    seeds = jax.random.split(jax.random.key(seed), 5)
    own_keys = jax.random.split(jax.random.fold_in(seeds[4], part), 5)
    query_states = draw_query_states(jax.random.fold_in(jax.random.fold_in(seeds[4], part), 71), part)
    key_states = draw_key_states(jax.random.fold_in(jax.random.fold_in(seeds[4], part), 71), part)
    value_states = gaussian(own_keys[2], (2 * TILES, TOK_DEV, HEADS * HD // 2), 8.0, 40.0, ((0, 16),))
    out_weight = gaussian(seeds[3], (HEADS * HD, D), (HEADS * HD) ** -0.5, 0.15625)
    return {"query_states": query_states, "key_states": key_states, "value_states": value_states, "out_weight": out_weight}


masked_score = -1e30


def to_tiles(blocks):
    tile_count = blocks.shape[0] // 2
    half_width = blocks.shape[2]
    return blocks.reshape(tile_count, 2, TOK_DEV, half_width).transpose(0, 2, 1, 3).reshape(tile_count, TOK_DEV, 2 * half_width)


def tile_attention(query_tile, key_window, value_window, key_ok):
    score_scale = HD ** -0.5
    pieces = []
    for head_index in range(HEADS):
        first_col = head_index * HD
        query_head = query_tile[:, first_col:first_col + HD]
        key_head = key_window[:, first_col:first_col + HD]
        value_head = value_window[:, first_col:first_col + HD]
        scores = lax.dot_general(query_head, key_head, (((1,), (1,)), ((), ())), preferred_element_type=jnp.float32) * score_scale
        scores = jnp.where(key_ok[None, :], scores, masked_score)
        row_max = jnp.max(scores, axis=1, keepdims=True)
        exp_scores = jnp.exp(scores - row_max)
        denominator = jnp.sum(exp_scores, axis=1, keepdims=True)
        weights = (exp_scores / denominator).astype(jnp.bfloat16)
        pieces.append(jnp.dot(weights, value_head, preferred_element_type=jnp.float32).astype(jnp.bfloat16))
    return jnp.concatenate(pieces, axis=1)


def reference(query_states, key_states, value_states, out_weight):
    width_all = HEADS * HD
    query_tiles = to_tiles(query_states)
    key_layout = to_tiles(key_states).reshape(T_TILES, TCOLS, TOK_DEV, width_all)
    value_layout = to_tiles(value_states).reshape(T_TILES, TCOLS, TOK_DEV, width_all)
    border = ((1, 1), (1, 1), (0, 0), (0, 0))
    key_padded = jnp.pad(key_layout, border)
    value_padded = jnp.pad(value_layout, border)
    tile_steps = jnp.arange(3, dtype=jnp.int32) - 1
    zero_index = jnp.zeros((), jnp.int32)

    def one_tile(tile_index):
        time_tile = (tile_index // TCOLS).astype(jnp.int32)
        col_tile = (tile_index % TCOLS).astype(jnp.int32)
        starts = (time_tile, col_tile, zero_index, zero_index)
        window_shape = (3, 3, TOK_DEV, width_all)
        key_window = lax.dynamic_slice(key_padded, starts, window_shape).reshape(9 * TOK_DEV, width_all)
        value_window = lax.dynamic_slice(value_padded, starts, window_shape).reshape(9 * TOK_DEV, width_all)
        time_ok = (time_tile + tile_steps >= 0) & (time_tile + tile_steps < T_TILES)
        col_ok = (col_tile + tile_steps >= 0) & (col_tile + tile_steps < TCOLS)
        tile_ok = (time_ok[:, None] & col_ok[None, :]).reshape(9)
        key_ok = jnp.repeat(tile_ok, TOK_DEV)
        query_tile = lax.dynamic_index_in_dim(query_tiles, tile_index, 0, keepdims=False)
        return tile_attention(query_tile, key_window, value_window, key_ok)

    attended = lax.map(one_tile, jnp.arange(TILES, dtype=jnp.int32)).reshape(TOKENS, width_all)
    mixed_rows = jnp.dot(attended, out_weight, preferred_element_type=jnp.float32)
    return mixed_rows.astype(jnp.bfloat16)
```

```python
import functools

import jax
import jax.numpy as jnp
from jax import lax
from jax.experimental import pallas as pl
from jax.experimental.pallas import tpu as pltpu
from jax.sharding import PartitionSpec as P

TCOLS = 4
HD = 128
MESH = pl.DeviceIdType.MESH
LOG2E = 1.4426950408889634

DIRECT_OWN = 2
DIRECT_CORNER = 1
AHEAD = 2
LAG_TIME = 2
LAG_CORNER = 3
LAG_MIDDLE = 5


def slot_of(time_step, col_step):
    return (time_step + 1) * 3 + col_step + 1


def general_kernel(
    time_count,
    heads,
    q_hbm,
    k_hbm,
    v_hbm,
    w_hbm,
    out_ref,
    q_s,
    kv,
    w_s,
    m_s,
    l_s,
    acc_s,
    outgoing,
    attended,
    load_sem,
    w_sem,
    send_sem,
    recv_sem,
    att_send_sem,
    att_recv_sem,
):
    rows = q_s.shape[1]
    half = rows // 2
    me = lax.axis_index("tm")
    group = lax.rem(me, 2)
    tile = lax.div(me, 2)
    col = lax.rem(tile, TCOLS)
    time = lax.div(tile, TCOLS)
    has_time = {-1: time > 0, 1: time < time_count - 1}
    has_col = {-1: col > 0, 1: col < TCOLS - 1}
    outer = 1 - 2 * lax.rem(col, 2)
    is_edge = jnp.logical_or(col == 0, col == TCOLS - 1)
    is_middle = jnp.logical_not(is_edge)
    outer_device = me + 2 * outer
    middle_device = me - 2 * outer
    relay_device = me + 4 * outer
    other_core = me + 1 - 2 * group
    own_slot = slot_of(0, 0)
    stride = TCOLS
    has_hop = {-1: tile >= stride // 2, 1: tile + stride // 2 < time_count * TCOLS}
    is_hop = jnp.logical_and(has_hop[-1], has_hop[1])

    def hop_slot(step):
        return 9 if step < 0 else 10

    def load(h):
        columns = pl.ds(pl.multiple_of(h * HD, HD), HD)
        return (
            pltpu.make_async_copy(k_hbm.at[0, :, columns], kv.at[own_slot, h, 0], load_sem.at[0, h]),
            pltpu.make_async_copy(v_hbm.at[0, :, columns], kv.at[own_slot, h, 1], load_sem.at[1, h]),
            pltpu.make_async_copy(q_hbm.at[0, :, columns], q_s.at[h], load_sem.at[2, h]),
        )

    for h in range(heads):
        for copy in load(jnp.int32(h)):
            copy.start()
    w_copy = pltpu.make_async_copy(w_hbm, w_s, w_sem)
    w_copy.start()

    barrier = pltpu.get_barrier_semaphore()

    def greet(device):
        pl.semaphore_signal(barrier, inc=1, device_id={"tm": device}, device_id_type=MESH)

    greetings = jnp.int32(2)
    greet(other_core)
    greet(outer_device)
    for step in (-1, 1):
        pl.when(has_hop[step])(lambda step=step: greet(me + stride * step))
        greetings = greetings + has_hop[step].astype(jnp.int32)
    pl.when(is_middle)(lambda: greet(middle_device))
    greetings = greetings + is_middle.astype(jnp.int32)
    pl.semaphore_wait(barrier, greetings)

    def transfer(kind, h, source, target, device):
        return pltpu.make_async_remote_copy(
            src_ref=kv.at[source, h],
            dst_ref=kv.at[target, h],
            send_sem=send_sem.at[kind, h],
            recv_sem=recv_sem.at[target, h],
            device_id={"tm": device},
            device_id_type=MESH,
        )

    def arrive(slot, h):
        transfer(0, h, slot, slot, other_core).wait_recv()

    def send_time(step, h):
        return transfer(0 if step < 0 else 1, h, own_slot, hop_slot(step), me + stride * step)

    def send_hop(step, h):
        return transfer(11 if step < 0 else 12, h, hop_slot(step), slot_of(-step, 0), me + stride * step)

    def send_outer(step, h):
        return transfer(3 + step, h, slot_of(step, 0), slot_of(step, 0) - outer, outer_device)

    def send_middle(step, h):
        return transfer(6 + step, h, slot_of(step, 0), slot_of(step, 0) + outer, middle_device)

    def send_relay(step, h):
        return transfer(9 + step, h, slot_of(step, 0) + outer, slot_of(step, 0) - outer, relay_device)

    def straight(step, h):
        return h >= heads - (DIRECT_OWN if step == 0 else DIRECT_CORNER)

    def send_att(h):
        return pltpu.make_async_remote_copy(
            src_ref=outgoing.at[h],
            dst_ref=attended.at[group, h],
            send_sem=att_send_sem.at[h],
            recv_sem=att_recv_sem.at[h],
            device_id={"tm": other_core},
            device_id_type=MESH,
        )

    def recv_att(h):
        return pltpu.make_async_remote_copy(
            src_ref=outgoing.at[h],
            dst_ref=attended.at[1 - group, h],
            send_sem=att_send_sem.at[h],
            recv_sem=att_recv_sem.at[h],
            device_id={"tm": other_core},
            device_id_type=MESH,
        )

    def send_own(h):
        for copy in load(h):
            copy.wait()
        for step in (-1, 1):
            pl.when(has_time[step])(lambda step=step: send_time(step, h).start())
        send_outer(0, h).start()
        if DIRECT_OWN:
            pl.when(jnp.logical_and(is_middle, straight(0, h)))(lambda: send_middle(0, h).start())

    for h in range(AHEAD):
        send_own(jnp.int32(h))

    exponent_scale = (HD ** (-0.5)) * LOG2E

    def attend(slot, h, first=False):
        scores = lax.dot_general(
            q_s[h], kv[slot, h, 0], (((1,), (1,)), ((), ())), preferred_element_type=jnp.float32
        )
        row_max = jnp.max(scores, axis=1, keepdims=True)
        if not first:
            old_max = m_s[h][:, :1]
            row_max = jnp.maximum(row_max, old_max)
        weights = jnp.exp2((scores - row_max) * exponent_scale)
        total = jnp.sum(weights, axis=1, keepdims=True)
        result = jnp.dot(weights.astype(jnp.bfloat16), kv[slot, h, 1], preferred_element_type=jnp.float32)
        if not first:
            keep = jnp.exp2((old_max - row_max) * exponent_scale)
            total = total + keep * l_s[h][:, :1]
            result = result + keep * acc_s[h]
        m_s[h] = jnp.broadcast_to(row_max, (rows, HD))
        l_s[h] = jnp.broadcast_to(total, (rows, HD))
        acc_s[h] = result

    def finish(h):
        acc_s[h] = acc_s[h] / l_s[h]
        attended[group, h] = acc_s[h, pl.ds(pl.multiple_of(group * half, 16), half), :].astype(jnp.bfloat16)
        outgoing[h] = acc_s[h, pl.ds(pl.multiple_of((1 - group) * half, 16), half), :].astype(jnp.bfloat16)

    def ready(h):
        return jnp.logical_and(h >= 0, h < heads)

    @pl.loop(0, heads + LAG_MIDDLE)
    def _(i):
        pl.when(i + AHEAD < heads)(lambda: send_own(i + AHEAD))

        @pl.when(jnp.logical_and(i < heads, is_edge))
        def _():
            arrive(own_slot + outer, i)
            pl.when(jnp.logical_not(straight(0, i)))(lambda: send_relay(0, i).start())

        @pl.when(jnp.logical_and(i < heads, is_hop))
        def _():
            for step in (-1, 1):
                arrive(hop_slot(step), i)
                send_hop(step, i).start()

        crossed = i - LAG_TIME

        @pl.when(ready(crossed))
        def _():
            for step in (-1, 1):

                @pl.when(has_time[step])
                def _():
                    arrive(slot_of(step, 0), crossed)
                    send_outer(step, crossed).start()
                    if DIRECT_CORNER:
                        pl.when(jnp.logical_and(is_middle, straight(step, crossed)))(
                            lambda: send_middle(step, crossed).start()
                        )

        back = i - LAG_CORNER

        @pl.when(jnp.logical_and(ready(back), is_edge))
        def _():
            for step in (-1, 1):

                @pl.when(has_time[step])
                def _():
                    arrive(slot_of(step, 0) + outer, back)
                    pl.when(jnp.logical_not(straight(step, back)))(lambda: send_relay(step, back).start())

        pl.when(i < heads)(lambda: attend(own_slot, i, first=True))

        @pl.when(ready(crossed))
        def _():
            for step in (-1, 1):
                pl.when(has_time[step])(lambda: attend(slot_of(step, 0), crossed))

        @pl.when(ready(back))
        def _():
            pl.when(is_middle)(lambda: arrive(own_slot + outer, back))
            attend(own_slot + outer, back)
            for step in (-1, 1):

                @pl.when(has_time[step])
                def _():
                    pl.when(is_middle)(lambda: arrive(slot_of(step, 0) + outer, back))
                    attend(slot_of(step, 0) + outer, back)

        last = i - LAG_MIDDLE

        @pl.when(last >= 1)
        def _():
            send_att(last - 1).start()

        @pl.when(last >= 0)
        def _():
            @pl.when(is_middle)
            def _():
                arrive(own_slot - outer, last)
                attend(own_slot - outer, last)
                for step in (-1, 1):

                    @pl.when(has_time[step])
                    def _():
                        arrive(slot_of(step, 0) - outer, last)
                        attend(slot_of(step, 0) - outer, last)

            finish(last)

    send_att(heads - 1).start()
    w_copy.wait()

    for h in range(heads):
        recv_att(h).wait_recv()

    width = out_ref.shape[1]
    chunk = 512
    lhs = jnp.concatenate([attended[part, h] for part in range(2) for h in range(heads)], axis=1)

    @pl.loop(0, width // chunk, unroll=True)
    def _(n):
        columns = pl.ds(pl.multiple_of(n * chunk, chunk), chunk)
        out_ref[:, columns] = jnp.dot(lhs, w_s[:, columns], preferred_element_type=jnp.float32).astype(
            out_ref.dtype
        )

    @pl.loop(0, heads)
    def _(h):
        send_att(h).wait_send()
        send_outer(0, h).wait_send()

        @pl.when(is_hop)
        def _():
            for step in (-1, 1):
                send_hop(step, h).wait_send()

        if DIRECT_OWN:
            pl.when(jnp.logical_and(is_middle, straight(0, h)))(lambda: send_middle(0, h).wait_send())
        pl.when(jnp.logical_and(is_edge, jnp.logical_not(straight(0, h))))(
            lambda: send_relay(0, h).wait_send()
        )
        for step in (-1, 1):

            @pl.when(has_time[step])
            def _():
                send_time(step, h).wait_send()
                send_outer(step, h).wait_send()
                if DIRECT_CORNER:
                    pl.when(jnp.logical_and(is_middle, straight(step, h)))(
                        lambda: send_middle(step, h).wait_send()
                    )
                pl.when(jnp.logical_and(is_edge, jnp.logical_not(straight(step, h))))(
                    lambda: send_relay(step, h).wait_send()
                )


def balanced_kernel(
    tiles,
    q_hbm,
    k_hbm,
    v_hbm,
    w_hbm,
    out_ref,
    q_s,
    guest_q,
    kv,
    w_s,
    m_s,
    l_s,
    acc_s,
    mixed_s,
    done_s,
    other_s,
    share_out,
    share_in,
    stat_out,
    stat_in,
    load_sem,
    w_sem,
    send_sem,
    recv_sem,
    q_send_sem,
    q_recv_sem,
    share_send_sem,
    share_recv_sem,
    att_send_sem,
    att_recv_sem,
):
    heads, rows = q_s.shape[:2]
    half = rows // 2
    last = heads - 1
    me = lax.axis_index("tm")
    group = lax.rem(me, 2)
    tile = lax.div(me, 2)
    lower = tile < tiles // 2
    role = jnp.where(lower, tile, tiles - 1 - tile)
    side = lax.rem(role, 2)
    is_cut_row = role >= 2
    is_outer_row = jnp.logical_not(is_cut_row)
    is_corner = role == 1
    is_host = role == 3
    pal = role + 1 - 2 * side
    row_base = role - side
    swapped = 5 - side
    straight = 4 + side
    far = 6 + side
    pal_far = 7 - side
    other_core = me + 1 - 2 * group

    def device_of(slot):
        return 2 * jnp.where(lower, slot, tiles - 1 - slot) + group

    pal_device = device_of(pal)
    up_down_device = device_of(jnp.where(is_cut_row, role - 2, role + 2))
    cut_device = device_of(role + 2)

    def load(h):
        columns = pl.ds(pl.multiple_of(h * HD, HD), HD)
        return (
            pltpu.make_async_copy(k_hbm.at[0, :, columns], kv.at[role, h, 0], load_sem.at[0, h]),
            pltpu.make_async_copy(v_hbm.at[0, :, columns], kv.at[role, h, 1], load_sem.at[1, h]),
            pltpu.make_async_copy(q_hbm.at[0, :, columns], q_s.at[h], load_sem.at[2, h]),
        )

    def load_w(h, which):
        owner = group if which == 0 else 1 - group
        source = pl.ds(pl.multiple_of((owner * heads + h) * HD, HD), HD)
        target = pl.ds(pl.multiple_of((2 * h + which) * HD, HD), HD)
        return pltpu.make_async_copy(w_hbm.at[source], w_s.at[target], w_sem.at[h, which])

    for h in (last, *range(last)):
        for copy in load(jnp.int32(h)):
            copy.start()

    barrier = pltpu.get_barrier_semaphore()

    def greet(device):
        pl.semaphore_signal(barrier, inc=1, device_id={"tm": device}, device_id_type=MESH)

    greet(other_core)
    greet(pal_device)
    greet(up_down_device)
    pl.when(is_cut_row)(lambda: greet(cut_device))
    pl.semaphore_wait(barrier, 3 + is_cut_row.astype(jnp.int32))

    def transfer(way, slot, h, target, device):
        return pltpu.make_async_remote_copy(
            src_ref=kv.at[slot, h],
            dst_ref=kv.at[target, h],
            send_sem=send_sem.at[way, slot, h],
            recv_sem=recv_sem.at[target, h],
            device_id={"tm": device},
            device_id_type=MESH,
        )

    def arrive(slot, h):
        transfer(0, slot, h, slot, pal_device).wait_recv()

    def to_pal(slot, h):
        return transfer(0, slot, h, slot, pal_device)

    def up_down(slot, h):
        return transfer(1, slot, h, slot, up_down_device)

    def cross(slot, h):
        return transfer(1, slot, h, tiles - 1 - slot, cut_device)

    def send_q(h):
        return pltpu.make_async_remote_copy(
            src_ref=q_s.at[h],
            dst_ref=guest_q.at[h],
            send_sem=q_send_sem.at[h],
            recv_sem=q_recv_sem.at[h],
            device_id={"tm": up_down_device},
            device_id_type=MESH,
        )

    def send_share(h):
        return tuple(
            pltpu.make_async_remote_copy(
                src_ref=source.at[h],
                dst_ref=target.at[h],
                send_sem=share_send_sem.at[which, h],
                recv_sem=share_recv_sem.at[which, h],
                device_id={"tm": up_down_device},
                device_id_type=MESH,
            )
            for which, (source, target) in enumerate(((share_out, share_in), (stat_out, stat_in)))
        )

    own_half = pl.ds(pl.multiple_of(group * half, 16), half)
    their_half = pl.ds(pl.multiple_of((1 - group) * half, 16), half)

    def send_att(h):
        return pltpu.make_async_remote_copy(
            src_ref=done_s.at[h, their_half],
            dst_ref=other_s.at[h],
            send_sem=att_send_sem.at[h],
            recv_sem=att_recv_sem.at[h],
            device_id={"tm": other_core},
            device_id_type=MESH,
        )

    def send_own(h):
        to_pal(role, h).start()
        pl.when(is_outer_row)(lambda: up_down(role, h).start())

    for h in (last, *range(last)):
        for copy in load(jnp.int32(h)):
            copy.wait()
        if h == last:
            pl.when(is_cut_row)(lambda: cross(role, jnp.int32(last)).start())
        else:
            send_own(jnp.int32(h))
    send_own(jnp.int32(last))
    for h in range(heads):
        pl.when(is_corner)(lambda: send_q(jnp.int32(h)).start())
    for h in range(heads):
        for which in range(2):
            load_w(h, which).start()

    exponent_scale = (HD ** (-0.5)) * LOG2E

    def attend(queries, slots, h, old_max=None):
        scores = [
            lax.dot_general(queries, kv[slot, h, 0], (((1,), (1,)), ((), ())), preferred_element_type=jnp.float32)
            for slot in slots
        ]
        row_max = functools.reduce(jnp.maximum, [jnp.max(s, axis=1, keepdims=True) for s in scores])
        if old_max is not None:
            row_max = jnp.maximum(row_max, old_max)
        weights = [jnp.exp2((s - row_max) * exponent_scale) for s in scores]
        total = sum(jnp.sum(w, axis=1, keepdims=True) for w in weights)
        result = sum(
            jnp.dot(w.astype(jnp.bfloat16), kv[slot, h, 1], preferred_element_type=jnp.float32)
            for w, slot in zip(weights, slots)
        )
        return row_max, total, result

    def attend_more(slots, h):
        old_max = m_s[h][:, :1]
        row_max, total, result = attend(q_s[h], slots, h, old_max)
        keep = jnp.exp2((old_max - row_max) * exponent_scale)
        return row_max, total + keep * l_s[h][:, :1], result + keep * acc_s[h]

    def hold(h, row_max, total, result):
        m_s[h] = jnp.broadcast_to(row_max, (rows, HD))
        l_s[h] = jnp.broadcast_to(total, (rows, HD))
        acc_s[h] = result

    def finish(h, row_max, total, result):
        done_s[h] = (result / total).astype(jnp.bfloat16)

    def share(h):
        row_max, total, result = attend(guest_q[h], (2, 6), h)
        share_out[h] = (result / total).astype(jnp.bfloat16)
        lane = lax.broadcasted_iota(jnp.int32, (rows, HD), 1)
        stats = jnp.where(lax.rem(lane, 8) < 4, row_max, total)
        stat_out[h] = jnp.transpose(stats)[:8]

    def merge(h):
        row_max, total, result = m_s[h], l_s[h], acc_s[h]
        their_max = jnp.transpose(jnp.broadcast_to(stat_in[h, 0:1, :], (HD, rows)))
        their_total = jnp.transpose(jnp.broadcast_to(stat_in[h, 4:5, :], (HD, rows)))
        top = jnp.maximum(row_max, their_max)
        keep = jnp.exp2((row_max - top) * exponent_scale)
        weight = their_total * jnp.exp2((their_max - top) * exponent_scale)
        finish(h, None, keep * total + weight, keep * result + weight * share_in[h].astype(jnp.float32))

    width = out_ref.shape[1]
    chunk = 512

    def mix(first, stop):
        lhs = jnp.concatenate(
            [part for h in range(first, stop) for part in (done_s[h, own_half, :], other_s[h])], axis=1
        )
        depth = slice(2 * first * HD, 2 * stop * HD)

        def product(n):
            columns = pl.ds(n * chunk, chunk)
            return columns, jnp.dot(lhs, w_s[depth, columns], preferred_element_type=jnp.float32)

        return (product(n) for n in range(width // chunk))

    early_heads = heads - 2

    def ready(h):
        return jnp.logical_and(h >= 0, h < heads)

    @pl.loop(0, 2 * heads + 2)
    def _(i):
        settled = i - heads - jnp.where(is_cut_row, 2, 3)
        pl.when(ready(settled))(lambda: send_att(settled).start())

        @pl.when(i == 2 * heads)
        def _():
            for h in range(heads):
                for which in range(2):
                    load_w(h, which).wait()
            for h in range(early_heads):
                send_att(h).wait_recv()
            for columns, value in mix(0, early_heads):
                mixed_s[:, columns] = value

        @pl.when(i < heads)
        def _():
            arrive(pal, i)
            pl.when(role == 0)(lambda: up_down(pal, i).start())
            pl.when(jnp.logical_and(is_cut_row, i < last))(lambda: cross(pal, i).start())

        @pl.when(is_cut_row)
        def _():
            @pl.when(i == 0)
            def _():
                arrive(side, i)
                cross(side, i).start()
                arrive(straight, jnp.int32(last))
                up_down(straight, jnp.int32(last)).start()
                pl.when(is_host)(lambda: to_pal(straight, jnp.int32(last)).start())

            relayed = i - 2

            @pl.when(jnp.logical_and(relayed >= 0, relayed < last))
            def _():
                arrive(swapped, relayed)
                up_down(swapped, relayed).start()

            crossed = jnp.where(i == 2, 0, i - heads)

            @pl.when(jnp.logical_or(i == 2, jnp.logical_and(crossed >= 1, crossed < heads)))
            def _():
                arrive(far, crossed)
                to_pal(far, crossed).start()

            def pass_on(h, first):
                @pl.when(jnp.logical_and(h >= first, h < heads))
                def _():
                    arrive(side, h)
                    cross(side, h).start()

            pass_on(jnp.where(i == heads - 2, 1, 2 * (i - heads) + 4), 1)
            pass_on(2 * (i - heads) + 5, 2)

        @pl.when(is_outer_row)
        def _():
            @pl.when(i == 1)
            def _():
                arrive(straight, jnp.int32(last))
                to_pal(straight, jnp.int32(last)).start()

            relayed = i - 3

            @pl.when(jnp.logical_and(relayed >= 0, relayed < last))
            def _():
                arrive(swapped, relayed)
                to_pal(swapped, relayed).start()

        @pl.when(i < heads)
        def _():
            hold(i, *attend(q_s[i], (row_base, row_base + 1), i))

        @pl.when(is_outer_row)
        def _():
            h = jnp.where(i == heads, last, i - heads - 1)

            @pl.when(jnp.logical_and(i >= heads, i < 2 * heads))
            def _():
                arrive(jnp.where(h == last, swapped, straight), h)
                hold(h, *attend_more((4, 5), h))

            ending = i - heads - 2

            @pl.when(jnp.logical_and(ready(ending), role == 0))
            def _():
                finish(ending, None, l_s[ending], acc_s[ending])

            @pl.when(jnp.logical_and(ready(ending), is_corner))
            def _():
                for copy in send_share(ending):
                    copy.wait_recv()
                merge(ending)

        ending = i - heads - 1

        @pl.when(jnp.logical_and(ready(ending), role == 2))
        def _():
            arrive(1, ending)
            pl.when(ending == last)(lambda: arrive(5, ending))
            arrive(pal_far, ending)
            finish(ending, *attend_more((1, 5, 6, 7), ending))

        @pl.when(jnp.logical_and(ready(ending), is_host))
        def _():
            send_q(ending).wait_recv()
            arrive(pal_far, ending)
            share(ending)
            for copy in send_share(ending):
                copy.start()
            finish(ending, *attend_more((6, 7), ending))

    pl.when(is_outer_row)(lambda: send_att(last).start())
    for h in range(early_heads, heads):
        send_att(h).wait_recv()
    for columns, value in mix(early_heads, heads):
        out_ref[:, columns] = (mixed_s[:, columns] + value).astype(out_ref.dtype)

    @pl.loop(0, heads)
    def _(h):
        send_att(h).wait_send()
        to_pal(role, h).wait_send()

        @pl.when(is_cut_row)
        def _():
            to_pal(far, h).wait_send()
            pl.when(jnp.logical_and(is_host, h == last))(lambda: to_pal(straight, h).wait_send())
            up_down(jnp.where(h == last, straight, swapped), h).wait_send()
            cross(jnp.where(h == last, role, pal), h).wait_send()
            cross(side, h).wait_send()

            @pl.when(is_host)
            def _():
                for copy in send_share(h):
                    copy.wait_send()

        @pl.when(is_outer_row)
        def _():
            to_pal(jnp.where(h == last, straight, swapped), h).wait_send()
            up_down(role, h).wait_send()
            pl.when(role == 0)(lambda: up_down(pal, h).wait_send())
            pl.when(is_corner)(lambda: send_q(h).wait_send())


def balanced_call(query_states, key_states, value_states, out_weight):
    rows, half_width = query_states.shape[1:]
    heads = half_width // HD
    depth, width = out_weight.shape
    tiles = lax.axis_size("tm") // 2
    dma = pltpu.SemaphoreType.DMA
    return pl.pallas_call(
        functools.partial(balanced_kernel, tiles),
        out_shape=jax.ShapeDtypeStruct((rows // 2, width), jnp.bfloat16),
        in_specs=[pl.BlockSpec(memory_space=pl.ANY)] * 4,
        out_specs=pl.BlockSpec(memory_space=pltpu.VMEM),
        scratch_shapes=[
            pltpu.VMEM((heads, rows, HD), jnp.bfloat16),
            pltpu.VMEM((heads, rows, HD), jnp.bfloat16),
            pltpu.VMEM((tiles, heads, 2, rows, HD), jnp.bfloat16),
            pltpu.VMEM((depth, width), jnp.bfloat16),
            pltpu.VMEM((heads, rows, HD), jnp.float32),
            pltpu.VMEM((heads, rows, HD), jnp.float32),
            pltpu.VMEM((heads, rows, HD), jnp.float32),
            pltpu.VMEM((rows // 2, width), jnp.float32),
            pltpu.VMEM((heads, rows, HD), jnp.bfloat16),
            pltpu.VMEM((heads, rows // 2, HD), jnp.bfloat16),
            pltpu.VMEM((heads, rows, HD), jnp.bfloat16),
            pltpu.VMEM((heads, rows, HD), jnp.bfloat16),
            pltpu.VMEM((heads, 8, rows), jnp.float32),
            pltpu.VMEM((heads, 8, rows), jnp.float32),
            dma((3, heads)),
            dma((heads, 2)),
            dma((2, tiles, heads)),
            dma((tiles, heads)),
            dma((heads,)),
            dma((heads,)),
            dma((2, heads)),
            dma((2, heads)),
            dma((heads,)),
            dma((heads,)),
        ],
        compiler_params=pltpu.CompilerParams(
            collective_id=0, has_side_effects=True, vmem_limit_bytes=56 * 1024 * 1024
        ),
    )(query_states, key_states, value_states, out_weight)


def general_call(query_states, key_states, value_states, out_weight):
    rows, half_width = query_states.shape[1:]
    heads = half_width // HD
    depth, width = out_weight.shape
    time_count = lax.axis_size("tm") // (2 * TCOLS)
    return pl.pallas_call(
        functools.partial(general_kernel, time_count, heads),
        out_shape=jax.ShapeDtypeStruct((rows // 2, width), jnp.bfloat16),
        in_specs=[pl.BlockSpec(memory_space=pl.ANY)] * 4,
        out_specs=pl.BlockSpec(memory_space=pltpu.VMEM),
        scratch_shapes=[
            pltpu.VMEM((heads, rows, HD), jnp.bfloat16),
            pltpu.VMEM((11, heads, 2, rows, HD), jnp.bfloat16),
            pltpu.VMEM((depth, width), jnp.bfloat16),
            pltpu.VMEM((heads, rows, HD), jnp.float32),
            pltpu.VMEM((heads, rows, HD), jnp.float32),
            pltpu.VMEM((heads, rows, HD), jnp.float32),
            pltpu.VMEM((heads, rows // 2, HD), jnp.bfloat16),
            pltpu.VMEM((2, heads, rows // 2, HD), jnp.bfloat16),
            pltpu.SemaphoreType.DMA((3, heads)),
            pltpu.SemaphoreType.DMA,
            pltpu.SemaphoreType.DMA((13, heads)),
            pltpu.SemaphoreType.DMA((11, heads)),
            pltpu.SemaphoreType.DMA((heads,)),
            pltpu.SemaphoreType.DMA((heads,)),
        ],
        compiler_params=pltpu.CompilerParams(
            collective_id=0, has_side_effects=True, vmem_limit_bytes=56 * 1024 * 1024
        ),
    )(query_states, key_states, value_states, out_weight)


def per_device(query_states, key_states, value_states, out_weight):
    call = balanced_call if lax.axis_size("tm") == 4 * TCOLS else general_call
    return call(query_states, key_states, value_states, out_weight)


def solution(mesh):
    in_specs = (
        P(("parts", "tm"), None, None),
        P(("parts", "tm"), None, None),
        P(("parts", "tm"), None, None),
        P(),
    )
    out_specs = P(("parts", "tm"), None)
    return jax.shard_map(
        per_device, mesh=mesh, in_specs=in_specs, out_specs=out_specs, check_vma=False
    )
```

```python
import functools

import jax
import jax.numpy as jnp
from jax import lax
from jax.experimental import pallas as pl
from jax.experimental.pallas import tpu as pltpu
from jax.sharding import PartitionSpec as P

TCOLS = 4
HD = 128
MESH = pl.DeviceIdType.MESH
LOG2E = 1.4426950408889634

DIRECT_OWN = 2
DIRECT_CORNER = 1
AHEAD = 2
LAG_TIME = 2
LAG_CORNER = 3
LAG_MIDDLE = 5


def slot_of(time_step, col_step):
    return (time_step + 1) * 3 + col_step + 1


def general_kernel(
    time_count,
    heads,
    q_hbm,
    k_hbm,
    v_hbm,
    w_hbm,
    out_ref,
    q_s,
    kv,
    w_s,
    m_s,
    l_s,
    acc_s,
    outgoing,
    attended,
    load_sem,
    w_sem,
    send_sem,
    recv_sem,
    att_send_sem,
    att_recv_sem,
):
    rows = q_s.shape[1]
    half = rows // 2
    me = lax.axis_index("tm")
    group = lax.rem(me, 2)
    tile = lax.div(me, 2)
    col = lax.rem(tile, TCOLS)
    time = lax.div(tile, TCOLS)
    has_time = {-1: time > 0, 1: time < time_count - 1}
    has_col = {-1: col > 0, 1: col < TCOLS - 1}
    outer = 1 - 2 * lax.rem(col, 2)
    is_edge = jnp.logical_or(col == 0, col == TCOLS - 1)
    is_middle = jnp.logical_not(is_edge)
    outer_device = me + 2 * outer
    middle_device = me - 2 * outer
    relay_device = me + 4 * outer
    other_core = me + 1 - 2 * group
    own_slot = slot_of(0, 0)
    stride = TCOLS
    has_hop = {-1: tile >= stride // 2, 1: tile + stride // 2 < time_count * TCOLS}
    is_hop = jnp.logical_and(has_hop[-1], has_hop[1])

    def hop_slot(step):
        return 9 if step < 0 else 10

    def load(h):
        columns = pl.ds(pl.multiple_of(h * HD, HD), HD)
        return (
            pltpu.make_async_copy(k_hbm.at[0, :, columns], kv.at[own_slot, h, 0], load_sem.at[0, h]),
            pltpu.make_async_copy(v_hbm.at[0, :, columns], kv.at[own_slot, h, 1], load_sem.at[1, h]),
            pltpu.make_async_copy(q_hbm.at[0, :, columns], q_s.at[h], load_sem.at[2, h]),
        )

    for h in range(heads):
        for copy in load(jnp.int32(h)):
            copy.start()
    w_copy = pltpu.make_async_copy(w_hbm, w_s, w_sem)
    w_copy.start()

    barrier = pltpu.get_barrier_semaphore()

    def greet(device):
        pl.semaphore_signal(barrier, inc=1, device_id={"tm": device}, device_id_type=MESH)

    greetings = jnp.int32(2)
    greet(other_core)
    greet(outer_device)
    for step in (-1, 1):
        pl.when(has_hop[step])(lambda step=step: greet(me + stride * step))
        greetings = greetings + has_hop[step].astype(jnp.int32)
    pl.when(is_middle)(lambda: greet(middle_device))
    greetings = greetings + is_middle.astype(jnp.int32)
    pl.semaphore_wait(barrier, greetings)

    def transfer(kind, h, source, target, device):
        return pltpu.make_async_remote_copy(
            src_ref=kv.at[source, h],
            dst_ref=kv.at[target, h],
            send_sem=send_sem.at[kind, h],
            recv_sem=recv_sem.at[target, h],
            device_id={"tm": device},
            device_id_type=MESH,
        )

    def arrive(slot, h):
        transfer(0, h, slot, slot, other_core).wait_recv()

    def send_time(step, h):
        return transfer(0 if step < 0 else 1, h, own_slot, hop_slot(step), me + stride * step)

    def send_hop(step, h):
        return transfer(11 if step < 0 else 12, h, hop_slot(step), slot_of(-step, 0), me + stride * step)

    def send_outer(step, h):
        return transfer(3 + step, h, slot_of(step, 0), slot_of(step, 0) - outer, outer_device)

    def send_middle(step, h):
        return transfer(6 + step, h, slot_of(step, 0), slot_of(step, 0) + outer, middle_device)

    def send_relay(step, h):
        return transfer(9 + step, h, slot_of(step, 0) + outer, slot_of(step, 0) - outer, relay_device)

    def straight(step, h):
        return h >= heads - (DIRECT_OWN if step == 0 else DIRECT_CORNER)

    def send_att(h):
        return pltpu.make_async_remote_copy(
            src_ref=outgoing.at[h],
            dst_ref=attended.at[group, h],
            send_sem=att_send_sem.at[h],
            recv_sem=att_recv_sem.at[h],
            device_id={"tm": other_core},
            device_id_type=MESH,
        )

    def recv_att(h):
        return pltpu.make_async_remote_copy(
            src_ref=outgoing.at[h],
            dst_ref=attended.at[1 - group, h],
            send_sem=att_send_sem.at[h],
            recv_sem=att_recv_sem.at[h],
            device_id={"tm": other_core},
            device_id_type=MESH,
        )

    def send_own(h):
        for copy in load(h):
            copy.wait()
        for step in (-1, 1):
            pl.when(has_time[step])(lambda step=step: send_time(step, h).start())
        send_outer(0, h).start()
        if DIRECT_OWN:
            pl.when(jnp.logical_and(is_middle, straight(0, h)))(lambda: send_middle(0, h).start())

    for h in range(AHEAD):
        send_own(jnp.int32(h))

    exponent_scale = (HD ** (-0.5)) * LOG2E

    def attend(slot, h, first=False):
        scores = lax.dot_general(
            q_s[h], kv[slot, h, 0], (((1,), (1,)), ((), ())), preferred_element_type=jnp.float32
        )
        row_max = jnp.max(scores, axis=1, keepdims=True)
        if not first:
            old_max = m_s[h][:, :1]
            row_max = jnp.maximum(row_max, old_max)
        weights = jnp.exp2((scores - row_max) * exponent_scale)
        total = jnp.sum(weights, axis=1, keepdims=True)
        result = jnp.dot(weights.astype(jnp.bfloat16), kv[slot, h, 1], preferred_element_type=jnp.float32)
        if not first:
            keep = jnp.exp2((old_max - row_max) * exponent_scale)
            total = total + keep * l_s[h][:, :1]
            result = result + keep * acc_s[h]
        m_s[h] = jnp.broadcast_to(row_max, (rows, HD))
        l_s[h] = jnp.broadcast_to(total, (rows, HD))
        acc_s[h] = result

    def finish(h):
        acc_s[h] = acc_s[h] / l_s[h]
        attended[group, h] = acc_s[h, pl.ds(pl.multiple_of(group * half, 16), half), :].astype(jnp.bfloat16)
        outgoing[h] = acc_s[h, pl.ds(pl.multiple_of((1 - group) * half, 16), half), :].astype(jnp.bfloat16)

    def ready(h):
        return jnp.logical_and(h >= 0, h < heads)

    @pl.loop(0, heads + LAG_MIDDLE)
    def _(i):
        pl.when(i + AHEAD < heads)(lambda: send_own(i + AHEAD))

        @pl.when(jnp.logical_and(i < heads, is_edge))
        def _():
            arrive(own_slot + outer, i)
            pl.when(jnp.logical_not(straight(0, i)))(lambda: send_relay(0, i).start())

        @pl.when(jnp.logical_and(i < heads, is_hop))
        def _():
            for step in (-1, 1):
                arrive(hop_slot(step), i)
                send_hop(step, i).start()

        crossed = i - LAG_TIME

        @pl.when(ready(crossed))
        def _():
            for step in (-1, 1):

                @pl.when(has_time[step])
                def _():
                    arrive(slot_of(step, 0), crossed)
                    send_outer(step, crossed).start()
                    if DIRECT_CORNER:
                        pl.when(jnp.logical_and(is_middle, straight(step, crossed)))(
                            lambda: send_middle(step, crossed).start()
                        )

        back = i - LAG_CORNER

        @pl.when(jnp.logical_and(ready(back), is_edge))
        def _():
            for step in (-1, 1):

                @pl.when(has_time[step])
                def _():
                    arrive(slot_of(step, 0) + outer, back)
                    pl.when(jnp.logical_not(straight(step, back)))(lambda: send_relay(step, back).start())

        pl.when(i < heads)(lambda: attend(own_slot, i, first=True))

        @pl.when(ready(crossed))
        def _():
            for step in (-1, 1):
                pl.when(has_time[step])(lambda: attend(slot_of(step, 0), crossed))

        @pl.when(ready(back))
        def _():
            pl.when(is_middle)(lambda: arrive(own_slot + outer, back))
            attend(own_slot + outer, back)
            for step in (-1, 1):

                @pl.when(has_time[step])
                def _():
                    pl.when(is_middle)(lambda: arrive(slot_of(step, 0) + outer, back))
                    attend(slot_of(step, 0) + outer, back)

        last = i - LAG_MIDDLE

        @pl.when(last >= 1)
        def _():
            send_att(last - 1).start()

        @pl.when(last >= 0)
        def _():
            @pl.when(is_middle)
            def _():
                arrive(own_slot - outer, last)
                attend(own_slot - outer, last)
                for step in (-1, 1):

                    @pl.when(has_time[step])
                    def _():
                        arrive(slot_of(step, 0) - outer, last)
                        attend(slot_of(step, 0) - outer, last)

            finish(last)

    send_att(heads - 1).start()
    w_copy.wait()

    for h in range(heads):
        recv_att(h).wait_recv()

    width = out_ref.shape[1]
    chunk = 512
    lhs = jnp.concatenate([attended[part, h] for part in range(2) for h in range(heads)], axis=1)

    @pl.loop(0, width // chunk, unroll=True)
    def _(n):
        columns = pl.ds(pl.multiple_of(n * chunk, chunk), chunk)
        out_ref[:, columns] = jnp.dot(lhs, w_s[:, columns], preferred_element_type=jnp.float32).astype(
            out_ref.dtype
        )

    @pl.loop(0, heads)
    def _(h):
        send_att(h).wait_send()
        send_outer(0, h).wait_send()

        @pl.when(is_hop)
        def _():
            for step in (-1, 1):
                send_hop(step, h).wait_send()

        if DIRECT_OWN:
            pl.when(jnp.logical_and(is_middle, straight(0, h)))(lambda: send_middle(0, h).wait_send())
        pl.when(jnp.logical_and(is_edge, jnp.logical_not(straight(0, h))))(
            lambda: send_relay(0, h).wait_send()
        )
        for step in (-1, 1):

            @pl.when(has_time[step])
            def _():
                send_time(step, h).wait_send()
                send_outer(step, h).wait_send()
                if DIRECT_CORNER:
                    pl.when(jnp.logical_and(is_middle, straight(step, h)))(
                        lambda: send_middle(step, h).wait_send()
                    )
                pl.when(jnp.logical_and(is_edge, jnp.logical_not(straight(step, h))))(
                    lambda: send_relay(step, h).wait_send()
                )


def balanced_kernel(
    tiles,
    q_hbm,
    k_hbm,
    v_hbm,
    w_hbm,
    out_ref,
    q_s,
    guest_q,
    kv,
    w_s,
    m_s,
    l_s,
    acc_s,
    mixed_s,
    done_s,
    other_s,
    share_out,
    share_in,
    stat_out,
    stat_in,
    load_sem,
    w_sem,
    send_sem,
    recv_sem,
    q_send_sem,
    q_recv_sem,
    share_send_sem,
    share_recv_sem,
    att_send_sem,
    att_recv_sem,
):
    heads, rows = q_s.shape[:2]
    half = rows // 2
    last = heads - 1
    me = lax.axis_index("tm")
    group = lax.rem(me, 2)
    tile = lax.div(me, 2)
    lower = tile < tiles // 2
    role = jnp.where(lower, tile, tiles - 1 - tile)
    side = lax.rem(role, 2)
    is_cut_row = role >= 2
    is_outer_row = jnp.logical_not(is_cut_row)
    is_corner = role == 1
    is_host = role == 3
    pal = role + 1 - 2 * side
    row_base = role - side
    swapped = 5 - side
    straight = 4 + side
    far = 6 + side
    pal_far = 7 - side
    other_core = me + 1 - 2 * group

    def device_of(slot):
        return 2 * jnp.where(lower, slot, tiles - 1 - slot) + group

    pal_device = device_of(pal)
    up_down_device = device_of(jnp.where(is_cut_row, role - 2, role + 2))
    cut_device = device_of(role + 2)

    def load(h):
        columns = pl.ds(pl.multiple_of(h * HD, HD), HD)
        return (
            pltpu.make_async_copy(k_hbm.at[0, :, columns], kv.at[role, h, 0], load_sem.at[0, h]),
            pltpu.make_async_copy(v_hbm.at[0, :, columns], kv.at[role, h, 1], load_sem.at[1, h]),
            pltpu.make_async_copy(q_hbm.at[0, :, columns], q_s.at[h], load_sem.at[2, h]),
        )

    def load_w(h, which):
        owner = group if which == 0 else 1 - group
        source = pl.ds(pl.multiple_of((owner * heads + h) * HD, HD), HD)
        target = pl.ds(pl.multiple_of((2 * h + which) * HD, HD), HD)
        return pltpu.make_async_copy(w_hbm.at[source], w_s.at[target], w_sem.at[h, which])

    for h in (last, *range(last)):
        for copy in load(jnp.int32(h)):
            copy.start()

    barrier = pltpu.get_barrier_semaphore()

    def greet(device):
        pl.semaphore_signal(barrier, inc=1, device_id={"tm": device}, device_id_type=MESH)

    greet(other_core)
    greet(pal_device)
    greet(up_down_device)
    pl.when(is_cut_row)(lambda: greet(cut_device))
    pl.semaphore_wait(barrier, 3 + is_cut_row.astype(jnp.int32))

    def transfer(way, slot, h, target, device):
        return pltpu.make_async_remote_copy(
            src_ref=kv.at[slot, h],
            dst_ref=kv.at[target, h],
            send_sem=send_sem.at[way, slot, h],
            recv_sem=recv_sem.at[target, h],
            device_id={"tm": device},
            device_id_type=MESH,
        )

    def arrive(slot, h):
        transfer(0, slot, h, slot, pal_device).wait_recv()

    def to_pal(slot, h):
        return transfer(0, slot, h, slot, pal_device)

    def up_down(slot, h):
        return transfer(1, slot, h, slot, up_down_device)

    def cross(slot, h):
        return transfer(1, slot, h, tiles - 1 - slot, cut_device)

    def send_q(h):
        return pltpu.make_async_remote_copy(
            src_ref=q_s.at[h],
            dst_ref=guest_q.at[h],
            send_sem=q_send_sem.at[h],
            recv_sem=q_recv_sem.at[h],
            device_id={"tm": up_down_device},
            device_id_type=MESH,
        )

    def send_share(h):
        return tuple(
            pltpu.make_async_remote_copy(
                src_ref=source.at[h],
                dst_ref=target.at[h],
                send_sem=share_send_sem.at[which, h],
                recv_sem=share_recv_sem.at[which, h],
                device_id={"tm": up_down_device},
                device_id_type=MESH,
            )
            for which, (source, target) in enumerate(((share_out, share_in), (stat_out, stat_in)))
        )

    own_half = pl.ds(pl.multiple_of(group * half, 16), half)
    their_half = pl.ds(pl.multiple_of((1 - group) * half, 16), half)

    def send_att(h):
        return pltpu.make_async_remote_copy(
            src_ref=done_s.at[h, their_half],
            dst_ref=other_s.at[h],
            send_sem=att_send_sem.at[h],
            recv_sem=att_recv_sem.at[h],
            device_id={"tm": other_core},
            device_id_type=MESH,
        )

    def send_own(h):
        to_pal(role, h).start()
        pl.when(is_outer_row)(lambda: up_down(role, h).start())

    for h in (last, *range(last)):
        for copy in load(jnp.int32(h)):
            copy.wait()
        if h == last:
            pl.when(is_cut_row)(lambda: cross(role, jnp.int32(last)).start())
        else:
            send_own(jnp.int32(h))
    send_own(jnp.int32(last))
    for h in range(heads):
        pl.when(is_corner)(lambda: send_q(jnp.int32(h)).start())
    for h in range(heads):
        for which in range(2):
            load_w(h, which).start()

    exponent_scale = (HD ** (-0.5)) * LOG2E

    def attend(queries, slots, h, old_max=None):
        scores = [
            lax.dot_general(queries, kv[slot, h, 0], (((1,), (1,)), ((), ())), preferred_element_type=jnp.float32)
            for slot in slots
        ]
        row_max = functools.reduce(jnp.maximum, [jnp.max(s, axis=1, keepdims=True) for s in scores])
        if old_max is not None:
            row_max = jnp.maximum(row_max, old_max)
        weights = [jnp.exp2((s - row_max) * exponent_scale) for s in scores]
        total = sum(jnp.sum(w, axis=1, keepdims=True) for w in weights)
        result = sum(
            jnp.dot(w.astype(jnp.bfloat16), kv[slot, h, 1], preferred_element_type=jnp.float32)
            for w, slot in zip(weights, slots)
        )
        return row_max, total, result

    def attend_more(slots, h):
        old_max = m_s[h][:, :1]
        row_max, total, result = attend(q_s[h], slots, h, old_max)
        keep = jnp.exp2((old_max - row_max) * exponent_scale)
        return row_max, total + keep * l_s[h][:, :1], result + keep * acc_s[h]

    def hold(h, row_max, total, result):
        m_s[h] = jnp.broadcast_to(row_max, (rows, HD))
        l_s[h] = jnp.broadcast_to(total, (rows, HD))
        acc_s[h] = result

    def finish(h, row_max, total, result):
        done_s[h] = (result / total).astype(jnp.bfloat16)

    def share(h):
        row_max, total, result = attend(guest_q[h], (2, 6), h)
        share_out[h] = (result / total).astype(jnp.bfloat16)
        lane = lax.broadcasted_iota(jnp.int32, (rows, HD), 1)
        stats = jnp.where(lax.rem(lane, 8) < 4, row_max, total)
        stat_out[h] = jnp.transpose(stats)[:8]

    def merge(h):
        row_max, total, result = m_s[h], l_s[h], acc_s[h]
        their_max = jnp.transpose(jnp.broadcast_to(stat_in[h, 0:1, :], (HD, rows)))
        their_total = jnp.transpose(jnp.broadcast_to(stat_in[h, 4:5, :], (HD, rows)))
        top = jnp.maximum(row_max, their_max)
        keep = jnp.exp2((row_max - top) * exponent_scale)
        weight = their_total * jnp.exp2((their_max - top) * exponent_scale)
        finish(h, None, keep * total + weight, keep * result + weight * share_in[h].astype(jnp.float32))

    width = out_ref.shape[1]
    chunk = 512

    def mix(first, stop):
        lhs = jnp.concatenate(
            [part for h in range(first, stop) for part in (done_s[h, own_half, :], other_s[h])], axis=1
        )
        depth = slice(2 * first * HD, 2 * stop * HD)

        def product(n):
            columns = pl.ds(n * chunk, chunk)
            return columns, jnp.dot(lhs, w_s[depth, columns], preferred_element_type=jnp.float32)

        return (product(n) for n in range(width // chunk))

    early_heads = heads - 2

    def ready(h):
        return jnp.logical_and(h >= 0, h < heads)

    @pl.loop(0, 2 * heads + 2)
    def _(i):
        settled = i - heads - jnp.where(is_cut_row, 2, 3)
        pl.when(ready(settled))(lambda: send_att(settled).start())

        @pl.when(i == 2 * heads)
        def _():
            for h in range(heads):
                for which in range(2):
                    load_w(h, which).wait()
            for h in range(early_heads):
                send_att(h).wait_recv()
            for columns, value in mix(0, early_heads):
                mixed_s[:, columns] = value

        @pl.when(i < heads)
        def _():
            arrive(pal, i)
            pl.when(role == 0)(lambda: up_down(pal, i).start())
            pl.when(jnp.logical_and(is_cut_row, i < last))(lambda: cross(pal, i).start())

        @pl.when(is_cut_row)
        def _():
            @pl.when(i == 0)
            def _():
                arrive(side, i)
                cross(side, i).start()
                arrive(straight, jnp.int32(last))
                up_down(straight, jnp.int32(last)).start()
                pl.when(is_host)(lambda: to_pal(straight, jnp.int32(last)).start())

            relayed = i - 2

            @pl.when(jnp.logical_and(relayed >= 0, relayed < last))
            def _():
                arrive(swapped, relayed)
                up_down(swapped, relayed).start()

            crossed = jnp.where(i == 2, 0, i - heads)

            @pl.when(jnp.logical_or(i == 2, jnp.logical_and(crossed >= 1, crossed < heads)))
            def _():
                arrive(far, crossed)
                to_pal(far, crossed).start()

            def pass_on(h, first):
                @pl.when(jnp.logical_and(h >= first, h < heads))
                def _():
                    arrive(side, h)
                    cross(side, h).start()

            pass_on(jnp.where(i == heads - 2, 1, 2 * (i - heads) + 4), 1)
            pass_on(2 * (i - heads) + 5, 2)

        @pl.when(is_outer_row)
        def _():
            @pl.when(i == 1)
            def _():
                arrive(straight, jnp.int32(last))
                to_pal(straight, jnp.int32(last)).start()

            relayed = i - 3

            @pl.when(jnp.logical_and(relayed >= 0, relayed < last))
            def _():
                arrive(swapped, relayed)
                to_pal(swapped, relayed).start()

        @pl.when(i < heads)
        def _():
            hold(i, *attend(q_s[i], (row_base, row_base + 1), i))

        @pl.when(is_outer_row)
        def _():
            h = jnp.where(i == heads, last, i - heads - 1)

            @pl.when(jnp.logical_and(i >= heads, i < 2 * heads))
            def _():
                arrive(jnp.where(h == last, swapped, straight), h)
                hold(h, *attend_more((4, 5), h))

            ending = i - heads - 2

            @pl.when(jnp.logical_and(ready(ending), role == 0))
            def _():
                finish(ending, None, l_s[ending], acc_s[ending])

            @pl.when(jnp.logical_and(ready(ending), is_corner))
            def _():
                for copy in send_share(ending):
                    copy.wait_recv()
                merge(ending)

        ending = i - heads - 1

        @pl.when(jnp.logical_and(ready(ending), role == 2))
        def _():
            arrive(1, ending)
            pl.when(ending == last)(lambda: arrive(5, ending))
            arrive(pal_far, ending)
            finish(ending, *attend_more((1, 5, 6, 7), ending))

        @pl.when(jnp.logical_and(ready(ending), is_host))
        def _():
            send_q(ending).wait_recv()
            arrive(pal_far, ending)
            share(ending)
            for copy in send_share(ending):
                copy.start()
            finish(ending, *attend_more((6, 7), ending))

    pl.when(is_outer_row)(lambda: send_att(last).start())
    for h in range(early_heads, heads):
        send_att(h).wait_recv()
    for columns, value in mix(early_heads, heads):
        out_ref[:, columns] = (mixed_s[:, columns] + value).astype(out_ref.dtype)

    @pl.loop(0, heads)
    def _(h):
        send_att(h).wait_send()
        to_pal(role, h).wait_send()

        @pl.when(is_cut_row)
        def _():
            to_pal(far, h).wait_send()
            pl.when(jnp.logical_and(is_host, h == last))(lambda: to_pal(straight, h).wait_send())
            up_down(jnp.where(h == last, straight, swapped), h).wait_send()
            cross(jnp.where(h == last, role, pal), h).wait_send()
            cross(side, h).wait_send()

            @pl.when(is_host)
            def _():
                for copy in send_share(h):
                    copy.wait_send()

        @pl.when(is_outer_row)
        def _():
            to_pal(jnp.where(h == last, straight, swapped), h).wait_send()
            up_down(role, h).wait_send()
            pl.when(role == 0)(lambda: up_down(pal, h).wait_send())
            pl.when(is_corner)(lambda: send_q(h).wait_send())


def balanced_call(query_states, key_states, value_states, out_weight):
    rows, half_width = query_states.shape[1:]
    heads = half_width // HD
    depth, width = out_weight.shape
    tiles = lax.axis_size("tm") // 2
    dma = pltpu.SemaphoreType.DMA
    return pl.pallas_call(
        functools.partial(balanced_kernel, tiles),
        out_shape=jax.ShapeDtypeStruct((rows // 2, width), jnp.bfloat16),
        in_specs=[pl.BlockSpec(memory_space=pl.ANY)] * 4,
        out_specs=pl.BlockSpec(memory_space=pltpu.VMEM),
        scratch_shapes=[
            pltpu.VMEM((heads, rows, HD), jnp.bfloat16),
            pltpu.VMEM((heads, rows, HD), jnp.bfloat16),
            pltpu.VMEM((tiles, heads, 2, rows, HD), jnp.bfloat16),
            pltpu.VMEM((depth, width), jnp.bfloat16),
            pltpu.VMEM((heads, rows, HD), jnp.float32),
            pltpu.VMEM((heads, rows, HD), jnp.float32),
            pltpu.VMEM((heads, rows, HD), jnp.float32),
            pltpu.VMEM((rows // 2, width), jnp.float32),
            pltpu.VMEM((heads, rows, HD), jnp.bfloat16),
            pltpu.VMEM((heads, rows // 2, HD), jnp.bfloat16),
            pltpu.VMEM((heads, rows, HD), jnp.bfloat16),
            pltpu.VMEM((heads, rows, HD), jnp.bfloat16),
            pltpu.VMEM((heads, 8, rows), jnp.float32),
            pltpu.VMEM((heads, 8, rows), jnp.float32),
            dma((3, heads)),
            dma((heads, 2)),
            dma((2, tiles, heads)),
            dma((tiles, heads)),
            dma((heads,)),
            dma((heads,)),
            dma((2, heads)),
            dma((2, heads)),
            dma((heads,)),
            dma((heads,)),
        ],
        compiler_params=pltpu.CompilerParams(
            collective_id=0, has_side_effects=True, vmem_limit_bytes=40 * 1024 * 1024
        ),
    )(*(pltpu.with_memory_space_constraint(x, pltpu.HBM) for x in (query_states, key_states, value_states, out_weight)))


def general_call(query_states, key_states, value_states, out_weight):
    rows, half_width = query_states.shape[1:]
    heads = half_width // HD
    depth, width = out_weight.shape
    time_count = lax.axis_size("tm") // (2 * TCOLS)
    return pl.pallas_call(
        functools.partial(general_kernel, time_count, heads),
        out_shape=jax.ShapeDtypeStruct((rows // 2, width), jnp.bfloat16),
        in_specs=[pl.BlockSpec(memory_space=pl.ANY)] * 4,
        out_specs=pl.BlockSpec(memory_space=pltpu.VMEM),
        scratch_shapes=[
            pltpu.VMEM((heads, rows, HD), jnp.bfloat16),
            pltpu.VMEM((11, heads, 2, rows, HD), jnp.bfloat16),
            pltpu.VMEM((depth, width), jnp.bfloat16),
            pltpu.VMEM((heads, rows, HD), jnp.float32),
            pltpu.VMEM((heads, rows, HD), jnp.float32),
            pltpu.VMEM((heads, rows, HD), jnp.float32),
            pltpu.VMEM((heads, rows // 2, HD), jnp.bfloat16),
            pltpu.VMEM((2, heads, rows // 2, HD), jnp.bfloat16),
            pltpu.SemaphoreType.DMA((3, heads)),
            pltpu.SemaphoreType.DMA,
            pltpu.SemaphoreType.DMA((13, heads)),
            pltpu.SemaphoreType.DMA((11, heads)),
            pltpu.SemaphoreType.DMA((heads,)),
            pltpu.SemaphoreType.DMA((heads,)),
        ],
        compiler_params=pltpu.CompilerParams(
            collective_id=0, has_side_effects=True, vmem_limit_bytes=56 * 1024 * 1024
        ),
    )(query_states, key_states, value_states, out_weight)


def per_device(query_states, key_states, value_states, out_weight):
    call = balanced_call if lax.axis_size("tm") == 4 * TCOLS else general_call
    return call(query_states, key_states, value_states, out_weight)


def solution(mesh):
    in_specs = (
        P(("parts", "tm"), None, None),
        P(("parts", "tm"), None, None),
        P(("parts", "tm"), None, None),
        P(),
    )
    out_specs = P(("parts", "tm"), None)
    return jax.shard_map(
        per_device, mesh=mesh, in_specs=in_specs, out_specs=out_specs, check_vma=False
    )
```

```python
import functools

import jax
import jax.numpy as jnp
from jax import lax
from jax.experimental import pallas as pl
from jax.experimental.pallas import tpu as pltpu
from jax.sharding import PartitionSpec as P

TCOLS = 4
HD = 128
MESH = pl.DeviceIdType.MESH
LOG2E = 1.4426950408889634

DIRECT_OWN = 2
DIRECT_CORNER = 1
AHEAD = 2
LAG_TIME = 2
LAG_CORNER = 3
LAG_MIDDLE = 5

NEAR = 2
OUT_CHUNK = 512
FIRST_OWN, FIRST_CROSSED, LAST_CROSSED, LAST_FAR = range(4)


def slot_of(time_step, col_step):
    return (time_step + 1) * 3 + col_step + 1


def general_kernel(
    time_count,
    heads,
    q_hbm,
    k_hbm,
    v_hbm,
    w_hbm,
    out_ref,
    q_s,
    kv,
    w_s,
    m_s,
    l_s,
    acc_s,
    outgoing,
    attended,
    load_sem,
    w_sem,
    send_sem,
    recv_sem,
    att_send_sem,
    att_recv_sem,
):
    rows = q_s.shape[1]
    half = rows // 2
    me = lax.axis_index("tm")
    group = lax.rem(me, 2)
    tile = lax.div(me, 2)
    col = lax.rem(tile, TCOLS)
    time = lax.div(tile, TCOLS)
    has_time = {-1: time > 0, 1: time < time_count - 1}
    has_col = {-1: col > 0, 1: col < TCOLS - 1}
    outer = 1 - 2 * lax.rem(col, 2)
    is_edge = jnp.logical_or(col == 0, col == TCOLS - 1)
    is_middle = jnp.logical_not(is_edge)
    outer_device = me + 2 * outer
    middle_device = me - 2 * outer
    relay_device = me + 4 * outer
    other_core = me + 1 - 2 * group
    own_slot = slot_of(0, 0)
    stride = TCOLS
    has_hop = {-1: tile >= stride // 2, 1: tile + stride // 2 < time_count * TCOLS}
    is_hop = jnp.logical_and(has_hop[-1], has_hop[1])

    def hop_slot(step):
        return 9 if step < 0 else 10

    def load(h):
        columns = pl.ds(pl.multiple_of(h * HD, HD), HD)
        return (
            pltpu.make_async_copy(k_hbm.at[0, :, columns], kv.at[own_slot, h, 0], load_sem.at[0, h]),
            pltpu.make_async_copy(v_hbm.at[0, :, columns], kv.at[own_slot, h, 1], load_sem.at[1, h]),
            pltpu.make_async_copy(q_hbm.at[0, :, columns], q_s.at[h], load_sem.at[2, h]),
        )

    for h in range(heads):
        for copy in load(jnp.int32(h)):
            copy.start()
    w_copy = pltpu.make_async_copy(w_hbm, w_s, w_sem)
    w_copy.start()

    barrier = pltpu.get_barrier_semaphore()

    def greet(device):
        pl.semaphore_signal(barrier, inc=1, device_id={"tm": device}, device_id_type=MESH)

    greetings = jnp.int32(2)
    greet(other_core)
    greet(outer_device)
    for step in (-1, 1):
        pl.when(has_hop[step])(lambda step=step: greet(me + stride * step))
        greetings = greetings + has_hop[step].astype(jnp.int32)
    pl.when(is_middle)(lambda: greet(middle_device))
    greetings = greetings + is_middle.astype(jnp.int32)
    pl.semaphore_wait(barrier, greetings)

    def transfer(kind, h, source, target, device):
        return pltpu.make_async_remote_copy(
            src_ref=kv.at[source, h],
            dst_ref=kv.at[target, h],
            send_sem=send_sem.at[kind, h],
            recv_sem=recv_sem.at[target, h],
            device_id={"tm": device},
            device_id_type=MESH,
        )

    def arrive(slot, h):
        transfer(0, h, slot, slot, other_core).wait_recv()

    def send_time(step, h):
        return transfer(0 if step < 0 else 1, h, own_slot, hop_slot(step), me + stride * step)

    def send_hop(step, h):
        return transfer(11 if step < 0 else 12, h, hop_slot(step), slot_of(-step, 0), me + stride * step)

    def send_outer(step, h):
        return transfer(3 + step, h, slot_of(step, 0), slot_of(step, 0) - outer, outer_device)

    def send_middle(step, h):
        return transfer(6 + step, h, slot_of(step, 0), slot_of(step, 0) + outer, middle_device)

    def send_relay(step, h):
        return transfer(9 + step, h, slot_of(step, 0) + outer, slot_of(step, 0) - outer, relay_device)

    def straight(step, h):
        return h >= heads - (DIRECT_OWN if step == 0 else DIRECT_CORNER)

    def send_att(h):
        return pltpu.make_async_remote_copy(
            src_ref=outgoing.at[h],
            dst_ref=attended.at[group, h],
            send_sem=att_send_sem.at[h],
            recv_sem=att_recv_sem.at[h],
            device_id={"tm": other_core},
            device_id_type=MESH,
        )

    def recv_att(h):
        return pltpu.make_async_remote_copy(
            src_ref=outgoing.at[h],
            dst_ref=attended.at[1 - group, h],
            send_sem=att_send_sem.at[h],
            recv_sem=att_recv_sem.at[h],
            device_id={"tm": other_core},
            device_id_type=MESH,
        )

    def send_own(h):
        for copy in load(h):
            copy.wait()
        for step in (-1, 1):
            pl.when(has_time[step])(lambda step=step: send_time(step, h).start())
        send_outer(0, h).start()
        if DIRECT_OWN:
            pl.when(jnp.logical_and(is_middle, straight(0, h)))(lambda: send_middle(0, h).start())

    for h in range(AHEAD):
        send_own(jnp.int32(h))

    exponent_scale = (HD ** (-0.5)) * LOG2E

    def attend(slot, h, first=False):
        scores = lax.dot_general(
            q_s[h], kv[slot, h, 0], (((1,), (1,)), ((), ())), preferred_element_type=jnp.float32
        )
        row_max = jnp.max(scores, axis=1, keepdims=True)
        if not first:
            old_max = m_s[h][:, :1]
            row_max = jnp.maximum(row_max, old_max)
        weights = jnp.exp2((scores - row_max) * exponent_scale)
        total = jnp.sum(weights, axis=1, keepdims=True)
        result = jnp.dot(weights.astype(jnp.bfloat16), kv[slot, h, 1], preferred_element_type=jnp.float32)
        if not first:
            keep = jnp.exp2((old_max - row_max) * exponent_scale)
            total = total + keep * l_s[h][:, :1]
            result = result + keep * acc_s[h]
        m_s[h] = jnp.broadcast_to(row_max, (rows, HD))
        l_s[h] = jnp.broadcast_to(total, (rows, HD))
        acc_s[h] = result

    def finish(h):
        acc_s[h] = acc_s[h] / l_s[h]
        attended[group, h] = acc_s[h, pl.ds(pl.multiple_of(group * half, 16), half), :].astype(jnp.bfloat16)
        outgoing[h] = acc_s[h, pl.ds(pl.multiple_of((1 - group) * half, 16), half), :].astype(jnp.bfloat16)

    def ready(h):
        return jnp.logical_and(h >= 0, h < heads)

    @pl.loop(0, heads + LAG_MIDDLE)
    def _(i):
        pl.when(i + AHEAD < heads)(lambda: send_own(i + AHEAD))

        @pl.when(jnp.logical_and(i < heads, is_edge))
        def _():
            arrive(own_slot + outer, i)
            pl.when(jnp.logical_not(straight(0, i)))(lambda: send_relay(0, i).start())

        @pl.when(jnp.logical_and(i < heads, is_hop))
        def _():
            for step in (-1, 1):
                arrive(hop_slot(step), i)
                send_hop(step, i).start()

        crossed = i - LAG_TIME

        @pl.when(ready(crossed))
        def _():
            for step in (-1, 1):

                @pl.when(has_time[step])
                def _():
                    arrive(slot_of(step, 0), crossed)
                    send_outer(step, crossed).start()
                    if DIRECT_CORNER:
                        pl.when(jnp.logical_and(is_middle, straight(step, crossed)))(
                            lambda: send_middle(step, crossed).start()
                        )

        back = i - LAG_CORNER

        @pl.when(jnp.logical_and(ready(back), is_edge))
        def _():
            for step in (-1, 1):

                @pl.when(has_time[step])
                def _():
                    arrive(slot_of(step, 0) + outer, back)
                    pl.when(jnp.logical_not(straight(step, back)))(lambda: send_relay(step, back).start())

        pl.when(i < heads)(lambda: attend(own_slot, i, first=True))

        @pl.when(ready(crossed))
        def _():
            for step in (-1, 1):
                pl.when(has_time[step])(lambda: attend(slot_of(step, 0), crossed))

        @pl.when(ready(back))
        def _():
            pl.when(is_middle)(lambda: arrive(own_slot + outer, back))
            attend(own_slot + outer, back)
            for step in (-1, 1):

                @pl.when(has_time[step])
                def _():
                    pl.when(is_middle)(lambda: arrive(slot_of(step, 0) + outer, back))
                    attend(slot_of(step, 0) + outer, back)

        last = i - LAG_MIDDLE

        @pl.when(last >= 1)
        def _():
            send_att(last - 1).start()

        @pl.when(last >= 0)
        def _():
            @pl.when(is_middle)
            def _():
                arrive(own_slot - outer, last)
                attend(own_slot - outer, last)
                for step in (-1, 1):

                    @pl.when(has_time[step])
                    def _():
                        arrive(slot_of(step, 0) - outer, last)
                        attend(slot_of(step, 0) - outer, last)

            finish(last)

    send_att(heads - 1).start()
    w_copy.wait()

    for h in range(heads):
        recv_att(h).wait_recv()

    width = out_ref.shape[1]
    chunk = 512
    lhs = jnp.concatenate([attended[part, h] for part in range(2) for h in range(heads)], axis=1)

    @pl.loop(0, width // chunk, unroll=True)
    def _(n):
        columns = pl.ds(pl.multiple_of(n * chunk, chunk), chunk)
        out_ref[:, columns] = jnp.dot(lhs, w_s[:, columns], preferred_element_type=jnp.float32).astype(
            out_ref.dtype
        )

    @pl.loop(0, heads)
    def _(h):
        send_att(h).wait_send()
        send_outer(0, h).wait_send()

        @pl.when(is_hop)
        def _():
            for step in (-1, 1):
                send_hop(step, h).wait_send()

        if DIRECT_OWN:
            pl.when(jnp.logical_and(is_middle, straight(0, h)))(lambda: send_middle(0, h).wait_send())
        pl.when(jnp.logical_and(is_edge, jnp.logical_not(straight(0, h))))(
            lambda: send_relay(0, h).wait_send()
        )
        for step in (-1, 1):

            @pl.when(has_time[step])
            def _():
                send_time(step, h).wait_send()
                send_outer(step, h).wait_send()
                if DIRECT_CORNER:
                    pl.when(jnp.logical_and(is_middle, straight(step, h)))(
                        lambda: send_middle(step, h).wait_send()
                    )
                pl.when(jnp.logical_and(is_edge, jnp.logical_not(straight(step, h))))(
                    lambda: send_relay(step, h).wait_send()
                )


def balanced_kernel(
    tiles,
    q_hbm,
    k_hbm,
    v_hbm,
    w_hbm,
    out_ref,
    q_s,
    guest_q,
    kv,
    w_s,
    m_s,
    l_s,
    acc_s,
    mixed_s,
    done_s,
    other_s,
    share_out,
    share_in,
    stat_out,
    stat_in,
    load_sem,
    q_sem,
    w_sem,
    send_sem,
    recv_sem,
    q_send_sem,
    q_recv_sem,
    share_send_sem,
    share_recv_sem,
    att_send_sem,
    att_recv_sem,
):
    heads, rows = q_s.shape[:2]
    half = rows // 2
    last = heads - 1
    early_heads = heads - 2
    me = lax.axis_index("tm")
    group = lax.rem(me, 2)
    tile = lax.div(me, 2)
    lower = tile < tiles // 2
    role = jnp.where(lower, tile, tiles - 1 - tile)
    side = lax.rem(role, 2)
    is_cut_row = role >= 2
    is_outer_row = jnp.logical_not(is_cut_row)
    is_corner = role == 1
    is_near = role == 2
    is_host = role == 3
    pal = role + 1 - 2 * side
    row_base = role - side
    swapped = 5 - side
    straight = 4 + side
    far = 6 + side
    pal_far = 7 - side
    other_core = me + 1 - 2 * group

    def device_of(slot):
        return 2 * jnp.where(lower, slot, tiles - 1 - slot) + group

    pal_device = device_of(pal)
    up_down_device = device_of(jnp.where(is_cut_row, role - 2, role + 2))
    cut_device = device_of(role + 2)
    corner_device = device_of(1)

    def load(h):
        columns = pl.ds(pl.multiple_of(h * HD, HD), HD)
        return (
            pltpu.make_async_copy(k_hbm.at[0, :, columns], kv.at[role, h, 0], load_sem.at[h]),
            pltpu.make_async_copy(v_hbm.at[0, :, columns], kv.at[role, h, 1], load_sem.at[h]),
            pltpu.make_async_copy(q_hbm.at[0, :, columns], q_s.at[h], q_sem),
        )

    def load_w(h, which):
        owner = group if which == 0 else 1 - group
        source = pl.ds(pl.multiple_of((owner * heads + h) * HD, HD), HD)
        target = pl.ds(pl.multiple_of((2 * h + which) * HD, HD), HD)
        return pltpu.make_async_copy(w_hbm.at[source], w_s.at[target], w_sem)

    for h in (last, *range(last)):
        for copy in load(jnp.int32(h)):
            copy.start()

    barrier = pltpu.get_barrier_semaphore()

    def greet(device):
        pl.semaphore_signal(barrier, inc=1, device_id={"tm": device}, device_id_type=MESH)

    greet(other_core)
    greet(pal_device)
    greet(up_down_device)
    pl.when(is_cut_row)(lambda: greet(cut_device))
    pl.when(is_corner)(lambda: greet(device_of(2)))
    pl.semaphore_wait(barrier, 3 + is_cut_row.astype(jnp.int32) + is_near.astype(jnp.int32))

    def transfer(way, slot, h, target, device, part=None, kind=0, landing=0):
        return pltpu.make_async_remote_copy(
            src_ref=kv.at[slot, h] if part is None else kv.at[slot, h, part],
            dst_ref=kv.at[target, h] if part is None else kv.at[target, h, part],
            send_sem=send_sem.at[way],
            recv_sem=recv_sem.at[landing, kind] if part == 1 else recv_sem.at[target, h],
            device_id={"tm": device},
            device_id_type=MESH,
        )

    def arrive(slot, h, part=None, kind=0):
        transfer(0, slot, h, slot, pal_device, part, kind, role).wait_recv()

    def to_pal(slot, h, part=None, kind=0, way=0):
        return transfer(way, slot, h, slot, pal_device, part, kind, pal)

    def up_down(slot, h):
        return transfer(1, slot, h, slot, up_down_device)

    def cross(slot, h, part=None, kind=0):
        return transfer(2, slot, h, tiles - 1 - slot, cut_device, part, kind, pal)

    def split_or_whole(is_split, act):
        pl.when(jnp.logical_not(is_split))(lambda: act(None))

        @pl.when(is_split)
        def _():
            for part in range(2):
                act(part)

    def send_q(h, source=q_s, device=up_down_device):
        return pltpu.make_async_remote_copy(
            src_ref=source.at[h],
            dst_ref=guest_q.at[h],
            send_sem=q_send_sem,
            recv_sem=q_recv_sem.at[h],
            device_id={"tm": device},
            device_id_type=MESH,
        )

    def send_share(h):
        return tuple(
            pltpu.make_async_remote_copy(
                src_ref=source.at[h],
                dst_ref=target.at[h],
                send_sem=share_send_sem.at[which],
                recv_sem=share_recv_sem.at[which, h],
                device_id={"tm": corner_device},
                device_id_type=MESH,
            )
            for which, (source, target) in enumerate(((share_out, share_in), (stat_out, stat_in)))
        )

    own_half = pl.ds(pl.multiple_of(group * half, 16), half)
    their_half = pl.ds(pl.multiple_of((1 - group) * half, 16), half)

    def send_att(h):
        return pltpu.make_async_remote_copy(
            src_ref=done_s.at[h, their_half],
            dst_ref=other_s.at[h],
            send_sem=att_send_sem,
            recv_sem=att_recv_sem.at[jnp.where(h < early_heads, 0, 1)],
            device_id={"tm": other_core},
            device_id_type=MESH,
        )

    def recv_att(first, stop, which):
        rows_in = other_s.at[pl.ds(first, stop - first)]
        pltpu.make_async_copy(rows_in, rows_in, att_recv_sem.at[which]).wait()

    def send_own(h):
        if h == 0:
            split_or_whole(is_cut_row, lambda part: to_pal(role, 0, part, FIRST_OWN).start())
        else:
            to_pal(role, h).start()
        pl.when(is_outer_row)(lambda: up_down(role, h).start())

    for h in (last, *range(last)):
        pltpu.make_async_copy(kv.at[role, h], kv.at[role, h], load_sem.at[h]).wait()
        if h == last:
            pl.when(is_cut_row)(lambda: cross(role, last).start())
        else:
            send_own(h)
        if h == 1:
            pltpu.make_async_copy(q_s, q_s, q_sem).wait()

            @pl.when(is_corner)
            def _():
                for near in range(heads - NEAR, heads):
                    send_q(near, device=pal_device).start()
    send_own(last)

    @pl.when(is_corner)
    def _():
        for h in range(heads - NEAR):
            send_q(h).start()

    exponent_scale = (HD ** (-0.5)) * LOG2E

    def attend(queries, slots, h, old_max=None):
        scores = [
            lax.dot_general(queries, kv[slot, h, 0], (((1,), (1,)), ((), ())), preferred_element_type=jnp.float32)
            for slot in slots
        ]
        row_max = functools.reduce(jnp.maximum, [jnp.max(s, axis=1, keepdims=True) for s in scores])
        if old_max is not None:
            row_max = jnp.maximum(row_max, old_max)
        weights = [jnp.exp2((s - row_max) * exponent_scale) for s in scores]
        total = sum(jnp.sum(w, axis=1, keepdims=True) for w in weights)
        result = sum(
            jnp.dot(w.astype(jnp.bfloat16), kv[slot, h, 1], preferred_element_type=jnp.float32)
            for w, slot in zip(weights, slots)
        )
        return row_max, total, result

    def attend_more(slots, h):
        old_max = m_s[h][:, :1]
        row_max, total, result = attend(q_s[h], slots, h, old_max)
        keep = jnp.exp2((old_max - row_max) * exponent_scale)
        return row_max, total + keep * l_s[h][:, :1], result + keep * acc_s[h]

    def hold(h, row_max, total, result):
        m_s[h] = jnp.broadcast_to(row_max, (rows, HD))
        l_s[h] = jnp.broadcast_to(total, (rows, HD))
        acc_s[h] = result

    def finish(h, row_max, total, result):
        done_s[h] = (result / total).astype(jnp.bfloat16)

    def share(h):
        row_max, total, result = attend(guest_q[h], (2, 6), h)
        share_out[h] = (result / total).astype(jnp.bfloat16)
        lane = lax.broadcasted_iota(jnp.int32, (rows, HD), 1)
        stats = jnp.where(lax.rem(lane, 8) < 4, row_max, total)
        stat_out[h] = jnp.transpose(stats)[:8]

    def merge(h):
        row_max, total, result = m_s[h], l_s[h], acc_s[h]
        their_max = jnp.transpose(jnp.broadcast_to(stat_in[h, 0:1, :], (HD, rows)))
        their_total = jnp.transpose(jnp.broadcast_to(stat_in[h, 4:5, :], (HD, rows)))
        top = jnp.maximum(row_max, their_max)
        keep = jnp.exp2((row_max - top) * exponent_scale)
        weight = their_total * jnp.exp2((their_max - top) * exponent_scale)
        finish(h, None, keep * total + weight, keep * result + weight * share_in[h].astype(jnp.float32))

    width = out_ref.shape[1]
    chunk = OUT_CHUNK

    def mix(first, stop):
        lhs = jnp.concatenate(
            [part for h in range(first, stop) for part in (done_s[h, own_half, :], other_s[h])], axis=1
        )
        depth = slice(2 * first * HD, 2 * stop * HD)

        def product(n):
            columns = pl.ds(n * chunk, chunk)
            return columns, jnp.dot(lhs, w_s[depth, columns], preferred_element_type=jnp.float32)

        return (product(n) for n in range(width // chunk))

    def ready(h):
        return jnp.logical_and(h >= 0, h < heads)

    @pl.loop(0, 2 * heads + 2)
    def _(i):
        settled = i - heads - jnp.where(is_cut_row, 2, 3)
        pl.when(ready(settled))(lambda: send_att(settled).start())

        @pl.when(jnp.logical_and(i < heads, jnp.logical_or(is_outer_row, i > 0)))
        def _():
            arrive(pal, i)
            pl.when(role == 0)(lambda: up_down(pal, i).start())
            pl.when(jnp.logical_and(is_cut_row, i < last))(lambda: cross(pal, i).start())

        @pl.when(is_cut_row)
        def _():
            @pl.when(i == 0)
            def _():
                for part in range(2):
                    arrive(pal, 0, part, FIRST_OWN)
                    cross(pal, 0, part, FIRST_CROSSED).start()
                arrive(side, 0)
                cross(side, 0).start()
                arrive(straight, last)
                up_down(straight, last).start()
                pl.when(is_host)(lambda: to_pal(straight, last, way=3).start())

            @pl.when(i == 2)
            def _():
                for part in range(2):
                    arrive(swapped, 0, part, FIRST_CROSSED)
                up_down(swapped, 0).start()
                arrive(far, 0)
                to_pal(far, 0).start()

            relayed = i - 2

            @pl.when(jnp.logical_and(relayed >= 1, relayed < last))
            def _():
                arrive(swapped, relayed)
                up_down(swapped, relayed).start()

            crossed = i - heads

            def hand_on(part):
                arrive(far, crossed, part, LAST_CROSSED)
                to_pal(far, crossed, part, LAST_FAR).start()

            @pl.when(jnp.logical_and(crossed >= 1, crossed < heads))
            def _():
                split_or_whole(crossed == last, hand_on)

            def pass_on(h, first):
                @pl.when(jnp.logical_and(h >= first, h < heads))
                def _():
                    arrive(side, h)
                    split_or_whole(h == last, lambda part: cross(side, h, part, LAST_CROSSED).start())

            pass_on(jnp.where(i == heads - 2, 1, 2 * (i - heads) + 4), 1)
            pass_on(2 * (i - heads) + 5, 2)

        @pl.when(is_outer_row)
        def _():
            @pl.when(i == 1)
            def _():
                arrive(straight, last)
                to_pal(straight, last).start()

            relayed = i - 3

            @pl.when(jnp.logical_and(relayed >= 0, relayed < last))
            def _():
                arrive(swapped, relayed)
                to_pal(swapped, relayed).start()

        nearby = i - heads

        @pl.when(jnp.logical_and(is_near, jnp.logical_and(nearby >= heads - NEAR, nearby < heads)))
        def _():
            send_q(nearby).wait_recv()
            share(nearby)
            for copy in send_share(nearby):
                copy.start()

        @pl.when(i == 2 * heads - jnp.where(jnp.logical_and(is_cut_row, group == 0), 1, 0))
        def _():
            pltpu.make_async_copy(w_hbm, w_s, w_sem).wait()
            recv_att(0, early_heads, 0)
            for columns, value in mix(0, early_heads):
                mixed_s[:, columns] = value

        @pl.when(jnp.logical_and(i >= 1, i <= heads))
        def _():
            for which in range(2):
                load_w(i - 1, which).start()

        @pl.when(i < heads)
        def _():
            hold(i, *attend(q_s[i], (row_base, row_base + 1), i))

        @pl.when(jnp.logical_and(role == 0, i == 2))
        def _():
            for h in range(heads - NEAR, heads):
                send_q(h).wait_recv()
                send_q(h, source=guest_q).start()

        @pl.when(is_outer_row)
        def _():
            h = jnp.where(i == heads, last, i - heads - 1)

            @pl.when(jnp.logical_and(i >= heads, i < 2 * heads))
            def _():
                arrive(jnp.where(h == last, swapped, straight), h)
                hold(h, *attend_more((4, 5), h))

            ending = i - heads - 2

            @pl.when(jnp.logical_and(ready(ending), role == 0))
            def _():
                finish(ending, None, l_s[ending], acc_s[ending])

            @pl.when(jnp.logical_and(ready(ending), is_corner))
            def _():
                for copy in send_share(ending):
                    copy.wait_recv()
                merge(ending)

        ending = i - heads - 1

        @pl.when(jnp.logical_and(ready(ending), is_cut_row))
        def _():
            split_or_whole(ending == last, lambda part: arrive(pal_far, ending, part, LAST_FAR))

        @pl.when(jnp.logical_and(ready(ending), is_near))
        def _():
            arrive(1, ending)
            pl.when(ending == last)(lambda: arrive(5, ending))
            finish(ending, *attend_more((1, 5, 6, 7), ending))

        @pl.when(jnp.logical_and(ready(ending), is_host))
        def _():
            @pl.when(ending < heads - NEAR)
            def _():
                send_q(ending).wait_recv()
                share(ending)
                for copy in send_share(ending):
                    copy.start()

            finish(ending, *attend_more((6, 7), ending))

    pl.when(is_outer_row)(lambda: send_att(last).start())
    recv_att(early_heads, heads, 1)
    for columns, value in mix(early_heads, heads):
        out_ref[:, columns] = (mixed_s[:, columns] + value).astype(out_ref.dtype)

    def drain(way, count):
        tiles_sent = kv.at[pl.ds(0, count)]
        pltpu.make_async_remote_copy(
            src_ref=tiles_sent,
            dst_ref=tiles_sent,
            send_sem=send_sem.at[way],
            recv_sem=recv_sem.at[0, 0],
            device_id={"tm": pal_device},
            device_id_type=MESH,
        ).wait_send()

    def drain_rows(sent, sem):
        pltpu.make_async_remote_copy(
            src_ref=sent,
            dst_ref=sent,
            send_sem=sem,
            recv_sem=recv_sem.at[0, 0],
            device_id={"tm": pal_device},
            device_id_type=MESH,
        ).wait_send()

    drain(0, 2)
    drain(1, 1)
    drain_rows(other_s, att_send_sem)
    pl.when(role == 0)(lambda: drain(1, 1))
    pl.when(role == 0)(lambda: drain_rows(guest_q.at[pl.ds(0, NEAR)], q_send_sem))
    pl.when(is_corner)(lambda: drain_rows(q_s, q_send_sem))
    pl.when(is_cut_row)(lambda: drain(2, 2))
    pl.when(is_host)(lambda: drain_rows(kv.at[0, 0], send_sem.at[3]))
    for count, sender in ((heads - NEAR, is_host), (NEAR, is_near)):
        pl.when(sender)(lambda count=count: drain_rows(share_out.at[pl.ds(0, count)], share_send_sem.at[0]))
        pl.when(sender)(lambda count=count: drain_rows(stat_out.at[pl.ds(0, count)], share_send_sem.at[1]))


def balanced_call(query_states, key_states, value_states, out_weight):
    rows, half_width = query_states.shape[1:]
    heads = half_width // HD
    depth, width = out_weight.shape
    tiles = lax.axis_size("tm") // 2
    dma = pltpu.SemaphoreType.DMA
    return pl.pallas_call(
        functools.partial(balanced_kernel, tiles),
        out_shape=jax.ShapeDtypeStruct((rows // 2, width), jnp.bfloat16),
        in_specs=[pl.BlockSpec(memory_space=pl.ANY)] * 4,
        out_specs=pl.BlockSpec(memory_space=pltpu.VMEM),
        scratch_shapes=[
            pltpu.VMEM((heads, rows, HD), jnp.bfloat16),
            pltpu.VMEM((heads, rows, HD), jnp.bfloat16),
            pltpu.VMEM((tiles, heads, 2, rows, HD), jnp.bfloat16),
            pltpu.VMEM((depth, width), jnp.bfloat16),
            pltpu.VMEM((heads, rows, HD), jnp.float32),
            pltpu.VMEM((heads, rows, HD), jnp.float32),
            pltpu.VMEM((heads, rows, HD), jnp.float32),
            pltpu.VMEM((rows // 2, width), jnp.float32),
            pltpu.VMEM((heads, rows, HD), jnp.bfloat16),
            pltpu.VMEM((heads, rows // 2, HD), jnp.bfloat16),
            pltpu.VMEM((heads, rows, HD), jnp.bfloat16),
            pltpu.VMEM((heads, rows, HD), jnp.bfloat16),
            pltpu.VMEM((heads, 8, rows), jnp.float32),
            pltpu.VMEM((heads, 8, rows), jnp.float32),
            dma((heads,)),
            dma,
            dma,
            dma((4,)),
            dma((tiles, heads)),
            dma,
            dma((heads,)),
            dma((2,)),
            dma((2, heads)),
            dma,
            dma((2,)),
        ],
        compiler_params=pltpu.CompilerParams(
            collective_id=0, has_side_effects=True, vmem_limit_bytes=40 * 1024 * 1024
        ),
    )(*(pltpu.with_memory_space_constraint(x, pltpu.HBM) for x in (query_states, key_states, value_states, out_weight)))


def general_call(query_states, key_states, value_states, out_weight):
    rows, half_width = query_states.shape[1:]
    heads = half_width // HD
    depth, width = out_weight.shape
    time_count = lax.axis_size("tm") // (2 * TCOLS)
    return pl.pallas_call(
        functools.partial(general_kernel, time_count, heads),
        out_shape=jax.ShapeDtypeStruct((rows // 2, width), jnp.bfloat16),
        in_specs=[pl.BlockSpec(memory_space=pl.ANY)] * 4,
        out_specs=pl.BlockSpec(memory_space=pltpu.VMEM),
        scratch_shapes=[
            pltpu.VMEM((heads, rows, HD), jnp.bfloat16),
            pltpu.VMEM((11, heads, 2, rows, HD), jnp.bfloat16),
            pltpu.VMEM((depth, width), jnp.bfloat16),
            pltpu.VMEM((heads, rows, HD), jnp.float32),
            pltpu.VMEM((heads, rows, HD), jnp.float32),
            pltpu.VMEM((heads, rows, HD), jnp.float32),
            pltpu.VMEM((heads, rows // 2, HD), jnp.bfloat16),
            pltpu.VMEM((2, heads, rows // 2, HD), jnp.bfloat16),
            pltpu.SemaphoreType.DMA((3, heads)),
            pltpu.SemaphoreType.DMA,
            pltpu.SemaphoreType.DMA((13, heads)),
            pltpu.SemaphoreType.DMA((11, heads)),
            pltpu.SemaphoreType.DMA((heads,)),
            pltpu.SemaphoreType.DMA((heads,)),
        ],
        compiler_params=pltpu.CompilerParams(
            collective_id=0, has_side_effects=True, vmem_limit_bytes=56 * 1024 * 1024
        ),
    )(query_states, key_states, value_states, out_weight)


def per_device(query_states, key_states, value_states, out_weight):
    call = balanced_call if lax.axis_size("tm") == 4 * TCOLS else general_call
    return call(query_states, key_states, value_states, out_weight)


def solution(mesh):
    in_specs = (
        P(("parts", "tm"), None, None),
        P(("parts", "tm"), None, None),
        P(("parts", "tm"), None, None),
        P(),
    )
    out_specs = P(("parts", "tm"), None)
    return jax.shard_map(
        per_device, mesh=mesh, in_specs=in_specs, out_specs=out_specs, check_vma=False
    )
```

```python
import functools

import jax
import jax.numpy as jnp
from jax import lax
from jax.experimental import pallas as pl
from jax.experimental.pallas import tpu as pltpu
from jax.sharding import PartitionSpec as P

TCOLS = 4
HD = 128
MESH = pl.DeviceIdType.MESH
LOG2E = 1.4426950408889634

DIRECT_OWN = 2
DIRECT_CORNER = 1
AHEAD = 2
LAG_TIME = 2
LAG_CORNER = 3
LAG_MIDDLE = 5

NEAR = 2
OUT_CHUNK = 512
FIRST_OWN, FIRST_CROSSED = range(2)


def slot_of(time_step, col_step):
    return (time_step + 1) * 3 + col_step + 1


def general_kernel(
    time_count,
    heads,
    q_hbm,
    k_hbm,
    v_hbm,
    w_hbm,
    out_ref,
    q_s,
    kv,
    w_s,
    m_s,
    l_s,
    acc_s,
    outgoing,
    attended,
    load_sem,
    w_sem,
    send_sem,
    recv_sem,
    att_send_sem,
    att_recv_sem,
):
    rows = q_s.shape[1]
    half = rows // 2
    me = lax.axis_index("tm")
    group = lax.rem(me, 2)
    tile = lax.div(me, 2)
    col = lax.rem(tile, TCOLS)
    time = lax.div(tile, TCOLS)
    has_time = {-1: time > 0, 1: time < time_count - 1}
    has_col = {-1: col > 0, 1: col < TCOLS - 1}
    outer = 1 - 2 * lax.rem(col, 2)
    is_edge = jnp.logical_or(col == 0, col == TCOLS - 1)
    is_middle = jnp.logical_not(is_edge)
    outer_device = me + 2 * outer
    middle_device = me - 2 * outer
    relay_device = me + 4 * outer
    other_core = me + 1 - 2 * group
    own_slot = slot_of(0, 0)
    stride = TCOLS
    has_hop = {-1: tile >= stride // 2, 1: tile + stride // 2 < time_count * TCOLS}
    is_hop = jnp.logical_and(has_hop[-1], has_hop[1])

    def hop_slot(step):
        return 9 if step < 0 else 10

    def load(h):
        columns = pl.ds(pl.multiple_of(h * HD, HD), HD)
        return (
            pltpu.make_async_copy(k_hbm.at[0, :, columns], kv.at[own_slot, h, 0], load_sem.at[0, h]),
            pltpu.make_async_copy(v_hbm.at[0, :, columns], kv.at[own_slot, h, 1], load_sem.at[1, h]),
            pltpu.make_async_copy(q_hbm.at[0, :, columns], q_s.at[h], load_sem.at[2, h]),
        )

    for h in range(heads):
        for copy in load(jnp.int32(h)):
            copy.start()
    w_copy = pltpu.make_async_copy(w_hbm, w_s, w_sem)
    w_copy.start()

    barrier = pltpu.get_barrier_semaphore()

    def greet(device):
        pl.semaphore_signal(barrier, inc=1, device_id={"tm": device}, device_id_type=MESH)

    greetings = jnp.int32(2)
    greet(other_core)
    greet(outer_device)
    for step in (-1, 1):
        pl.when(has_hop[step])(lambda step=step: greet(me + stride * step))
        greetings = greetings + has_hop[step].astype(jnp.int32)
    pl.when(is_middle)(lambda: greet(middle_device))
    greetings = greetings + is_middle.astype(jnp.int32)
    pl.semaphore_wait(barrier, greetings)

    def transfer(kind, h, source, target, device):
        return pltpu.make_async_remote_copy(
            src_ref=kv.at[source, h],
            dst_ref=kv.at[target, h],
            send_sem=send_sem.at[kind, h],
            recv_sem=recv_sem.at[target, h],
            device_id={"tm": device},
            device_id_type=MESH,
        )

    def arrive(slot, h):
        transfer(0, h, slot, slot, other_core).wait_recv()

    def send_time(step, h):
        return transfer(0 if step < 0 else 1, h, own_slot, hop_slot(step), me + stride * step)

    def send_hop(step, h):
        return transfer(11 if step < 0 else 12, h, hop_slot(step), slot_of(-step, 0), me + stride * step)

    def send_outer(step, h):
        return transfer(3 + step, h, slot_of(step, 0), slot_of(step, 0) - outer, outer_device)

    def send_middle(step, h):
        return transfer(6 + step, h, slot_of(step, 0), slot_of(step, 0) + outer, middle_device)

    def send_relay(step, h):
        return transfer(9 + step, h, slot_of(step, 0) + outer, slot_of(step, 0) - outer, relay_device)

    def straight(step, h):
        return h >= heads - (DIRECT_OWN if step == 0 else DIRECT_CORNER)

    def send_att(h):
        return pltpu.make_async_remote_copy(
            src_ref=outgoing.at[h],
            dst_ref=attended.at[group, h],
            send_sem=att_send_sem.at[h],
            recv_sem=att_recv_sem.at[h],
            device_id={"tm": other_core},
            device_id_type=MESH,
        )

    def recv_att(h):
        return pltpu.make_async_remote_copy(
            src_ref=outgoing.at[h],
            dst_ref=attended.at[1 - group, h],
            send_sem=att_send_sem.at[h],
            recv_sem=att_recv_sem.at[h],
            device_id={"tm": other_core},
            device_id_type=MESH,
        )

    def send_own(h):
        for copy in load(h):
            copy.wait()
        for step in (-1, 1):
            pl.when(has_time[step])(lambda step=step: send_time(step, h).start())
        send_outer(0, h).start()
        if DIRECT_OWN:
            pl.when(jnp.logical_and(is_middle, straight(0, h)))(lambda: send_middle(0, h).start())

    for h in range(AHEAD):
        send_own(jnp.int32(h))

    exponent_scale = (HD ** (-0.5)) * LOG2E

    def attend(slot, h, first=False):
        scores = lax.dot_general(
            q_s[h], kv[slot, h, 0], (((1,), (1,)), ((), ())), preferred_element_type=jnp.float32
        )
        row_max = jnp.max(scores, axis=1, keepdims=True)
        if not first:
            old_max = m_s[h][:, :1]
            row_max = jnp.maximum(row_max, old_max)
        weights = jnp.exp2((scores - row_max) * exponent_scale)
        total = jnp.sum(weights, axis=1, keepdims=True)
        result = jnp.dot(weights.astype(jnp.bfloat16), kv[slot, h, 1], preferred_element_type=jnp.float32)
        if not first:
            keep = jnp.exp2((old_max - row_max) * exponent_scale)
            total = total + keep * l_s[h][:, :1]
            result = result + keep * acc_s[h]
        m_s[h] = jnp.broadcast_to(row_max, (rows, HD))
        l_s[h] = jnp.broadcast_to(total, (rows, HD))
        acc_s[h] = result

    def finish(h):
        acc_s[h] = acc_s[h] / l_s[h]
        attended[group, h] = acc_s[h, pl.ds(pl.multiple_of(group * half, 16), half), :].astype(jnp.bfloat16)
        outgoing[h] = acc_s[h, pl.ds(pl.multiple_of((1 - group) * half, 16), half), :].astype(jnp.bfloat16)

    def ready(h):
        return jnp.logical_and(h >= 0, h < heads)

    @pl.loop(0, heads + LAG_MIDDLE)
    def _(i):
        pl.when(i + AHEAD < heads)(lambda: send_own(i + AHEAD))

        @pl.when(jnp.logical_and(i < heads, is_edge))
        def _():
            arrive(own_slot + outer, i)
            pl.when(jnp.logical_not(straight(0, i)))(lambda: send_relay(0, i).start())

        @pl.when(jnp.logical_and(i < heads, is_hop))
        def _():
            for step in (-1, 1):
                arrive(hop_slot(step), i)
                send_hop(step, i).start()

        crossed = i - LAG_TIME

        @pl.when(ready(crossed))
        def _():
            for step in (-1, 1):

                @pl.when(has_time[step])
                def _():
                    arrive(slot_of(step, 0), crossed)
                    send_outer(step, crossed).start()
                    if DIRECT_CORNER:
                        pl.when(jnp.logical_and(is_middle, straight(step, crossed)))(
                            lambda: send_middle(step, crossed).start()
                        )

        back = i - LAG_CORNER

        @pl.when(jnp.logical_and(ready(back), is_edge))
        def _():
            for step in (-1, 1):

                @pl.when(has_time[step])
                def _():
                    arrive(slot_of(step, 0) + outer, back)
                    pl.when(jnp.logical_not(straight(step, back)))(lambda: send_relay(step, back).start())

        pl.when(i < heads)(lambda: attend(own_slot, i, first=True))

        @pl.when(ready(crossed))
        def _():
            for step in (-1, 1):
                pl.when(has_time[step])(lambda: attend(slot_of(step, 0), crossed))

        @pl.when(ready(back))
        def _():
            pl.when(is_middle)(lambda: arrive(own_slot + outer, back))
            attend(own_slot + outer, back)
            for step in (-1, 1):

                @pl.when(has_time[step])
                def _():
                    pl.when(is_middle)(lambda: arrive(slot_of(step, 0) + outer, back))
                    attend(slot_of(step, 0) + outer, back)

        last = i - LAG_MIDDLE

        @pl.when(last >= 1)
        def _():
            send_att(last - 1).start()

        @pl.when(last >= 0)
        def _():
            @pl.when(is_middle)
            def _():
                arrive(own_slot - outer, last)
                attend(own_slot - outer, last)
                for step in (-1, 1):

                    @pl.when(has_time[step])
                    def _():
                        arrive(slot_of(step, 0) - outer, last)
                        attend(slot_of(step, 0) - outer, last)

            finish(last)

    send_att(heads - 1).start()
    w_copy.wait()

    for h in range(heads):
        recv_att(h).wait_recv()

    width = out_ref.shape[1]
    chunk = 512
    lhs = jnp.concatenate([attended[part, h] for part in range(2) for h in range(heads)], axis=1)

    @pl.loop(0, width // chunk, unroll=True)
    def _(n):
        columns = pl.ds(pl.multiple_of(n * chunk, chunk), chunk)
        out_ref[:, columns] = jnp.dot(lhs, w_s[:, columns], preferred_element_type=jnp.float32).astype(
            out_ref.dtype
        )

    @pl.loop(0, heads)
    def _(h):
        send_att(h).wait_send()
        send_outer(0, h).wait_send()

        @pl.when(is_hop)
        def _():
            for step in (-1, 1):
                send_hop(step, h).wait_send()

        if DIRECT_OWN:
            pl.when(jnp.logical_and(is_middle, straight(0, h)))(lambda: send_middle(0, h).wait_send())
        pl.when(jnp.logical_and(is_edge, jnp.logical_not(straight(0, h))))(
            lambda: send_relay(0, h).wait_send()
        )
        for step in (-1, 1):

            @pl.when(has_time[step])
            def _():
                send_time(step, h).wait_send()
                send_outer(step, h).wait_send()
                if DIRECT_CORNER:
                    pl.when(jnp.logical_and(is_middle, straight(step, h)))(
                        lambda: send_middle(step, h).wait_send()
                    )
                pl.when(jnp.logical_and(is_edge, jnp.logical_not(straight(step, h))))(
                    lambda: send_relay(step, h).wait_send()
                )


def crossing_order(heads):
    order = [(from_pal, h) for h in range(heads - 4) for from_pal in (True, False)]
    order += [(True, heads - 4), (True, heads - 3), (False, heads - 4), (True, heads - 2)]
    return order + [(False, h) for h in range(heads - 3, heads)]


def balanced_kernel(
    tiles,
    q_hbm,
    k_hbm,
    v_hbm,
    w_hbm,
    out_ref,
    q_s,
    guest_q,
    kv,
    w_s,
    m_s,
    l_s,
    acc_s,
    mixed_s,
    done_s,
    other_s,
    share_out,
    share_in,
    stat_out,
    stat_in,
    pal_q,
    pal_share_out,
    pal_share_in,
    pal_stat_out,
    pal_stat_in,
    load_sem,
    q_sem,
    w_sem,
    send_sem,
    recv_sem,
    q_send_sem,
    q_recv_sem,
    share_send_sem,
    share_recv_sem,
    pal_send_sem,
    pal_recv_sem,
    att_send_sem,
    att_recv_sem,
):
    heads, rows = q_s.shape[:2]
    half = rows // 2
    last = heads - 1
    early_heads = heads - 3
    tail = heads - NEAR
    me = lax.axis_index("tm")
    group = lax.rem(me, 2)
    tile = lax.div(me, 2)
    lower = tile < tiles // 2
    role = jnp.where(lower, tile, tiles - 1 - tile)
    side = lax.rem(role, 2)
    is_cut_row = role >= 2
    is_outer_row = jnp.logical_not(is_cut_row)
    is_corner = role == 1
    is_near = role == 2
    is_host = role == 3
    pal = role + 1 - 2 * side
    row_base = role - side
    swapped = 5 - side
    straight = 4 + side
    far = 6 + side
    pal_far = 7 - side
    other_core = me + 1 - 2 * group

    def device_of(slot):
        return 2 * jnp.where(lower, slot, tiles - 1 - slot) + group

    pal_device = device_of(pal)
    up_down_device = device_of(jnp.where(is_cut_row, role - 2, role + 2))
    cut_device = device_of(role + 2)
    corner_device = device_of(1)

    def load(h):
        columns = pl.ds(pl.multiple_of(h * HD, HD), HD)
        return (
            pltpu.make_async_copy(k_hbm.at[0, :, columns], kv.at[role, h, 0], load_sem.at[h]),
            pltpu.make_async_copy(v_hbm.at[0, :, columns], kv.at[role, h, 1], load_sem.at[h]),
            pltpu.make_async_copy(q_hbm.at[0, :, columns], q_s.at[h], q_sem),
        )

    def load_w(h, which):
        owner = group if which == 0 else 1 - group
        source = pl.ds(pl.multiple_of((owner * heads + h) * HD, HD), HD)
        target = pl.ds(pl.multiple_of((2 * h + which) * HD, HD), HD)
        return pltpu.make_async_copy(w_hbm.at[source], w_s.at[target], w_sem)

    for h in (last, *range(last)):
        for copy in load(jnp.int32(h)):
            copy.start()

    barrier = pltpu.get_barrier_semaphore()

    def greet(device):
        pl.semaphore_signal(barrier, inc=1, device_id={"tm": device}, device_id_type=MESH)

    greet(other_core)
    greet(pal_device)
    greet(up_down_device)
    pl.when(is_cut_row)(lambda: greet(cut_device))
    pl.when(is_corner)(lambda: greet(device_of(2)))
    pl.semaphore_wait(barrier, 3 + is_cut_row.astype(jnp.int32) + is_near.astype(jnp.int32))

    def transfer(way, slot, h, target, device, part=None, kind=0, landing=0):
        return pltpu.make_async_remote_copy(
            src_ref=kv.at[slot, h] if part is None else kv.at[slot, h, part],
            dst_ref=kv.at[target, h] if part is None else kv.at[target, h, part],
            send_sem=send_sem.at[way],
            recv_sem=recv_sem.at[landing, kind] if part == 1 else recv_sem.at[target, h],
            device_id={"tm": device},
            device_id_type=MESH,
        )

    def arrive(slot, h, part=None, kind=0):
        transfer(0, slot, h, slot, pal_device, part, kind, role).wait_recv()

    def to_pal(slot, h, part=None, kind=0):
        return transfer(0, slot, h, slot, pal_device, part, kind, pal)

    def up_down(slot, h, way=1):
        return transfer(way, slot, h, slot, up_down_device)

    def cross(slot, h, part=None, kind=0):
        return transfer(2, slot, h, tiles - 1 - slot, cut_device, part, kind, pal)

    def split_or_whole(is_split, act):
        pl.when(jnp.logical_not(is_split))(lambda: act(None))

        @pl.when(is_split)
        def _():
            for part in range(2):
                act(part)

    def send_q(h, source=q_s, device=up_down_device):
        return pltpu.make_async_remote_copy(
            src_ref=source.at[h],
            dst_ref=guest_q.at[h],
            send_sem=q_send_sem,
            recv_sem=q_recv_sem.at[h],
            device_id={"tm": device},
            device_id_type=MESH,
        )

    def lend_q(h):
        return pltpu.make_async_remote_copy(
            src_ref=q_s.at[h],
            dst_ref=share_in.at[h],
            send_sem=q_send_sem,
            recv_sem=share_recv_sem.at[0, h],
            device_id={"tm": up_down_device},
            device_id_type=MESH,
        )

    def send_share(h, device=corner_device):
        return tuple(
            pltpu.make_async_remote_copy(
                src_ref=source.at[h],
                dst_ref=target.at[h],
                send_sem=share_send_sem.at[which],
                recv_sem=share_recv_sem.at[which, h],
                device_id={"tm": device},
                device_id_type=MESH,
            )
            for which, (source, target) in enumerate(((share_out, share_in), (stat_out, stat_in)))
        )

    def send_pal(source, target, which, index):
        return pltpu.make_async_remote_copy(
            src_ref=source,
            dst_ref=target,
            send_sem=pal_send_sem.at[which],
            recv_sem=pal_recv_sem.at[which, index],
            device_id={"tm": pal_device},
            device_id_type=MESH,
        )

    def send_pal_share(index):
        return (
            send_pal(pal_share_out.at[index], pal_share_in.at[index], 1, index),
            send_pal(pal_stat_out.at[index], pal_stat_in.at[index], 2, index),
        )

    own_half = pl.ds(pl.multiple_of(group * half, 16), half)
    their_half = pl.ds(pl.multiple_of((1 - group) * half, 16), half)

    def send_att(h):
        return pltpu.make_async_remote_copy(
            src_ref=done_s.at[h, their_half],
            dst_ref=other_s.at[h],
            send_sem=att_send_sem,
            recv_sem=att_recv_sem.at[jnp.where(h < early_heads, 0, 1)],
            device_id={"tm": other_core},
            device_id_type=MESH,
        )

    def recv_att(first, stop, which):
        rows_in = other_s.at[pl.ds(first, stop - first)]
        pltpu.make_async_copy(rows_in, rows_in, att_recv_sem.at[which]).wait()

    def send_own(h):
        if h == 0:
            split_or_whole(is_cut_row, lambda part: to_pal(role, 0, part, FIRST_OWN).start())
        else:
            to_pal(role, h).start()
        pl.when(is_outer_row)(lambda: up_down(role, h).start())

    for h in (last, *range(last)):
        pltpu.make_async_copy(kv.at[role, h], kv.at[role, h], load_sem.at[h]).wait()
        if h == last:
            pl.when(is_cut_row)(lambda: cross(role, last).start())
        else:
            send_own(h)
        if h == 1:
            pltpu.make_async_copy(q_s, q_s, q_sem).wait()

            @pl.when(is_corner)
            def _():
                for near in range(heads - NEAR, heads):
                    send_q(near, device=pal_device).start()
    send_own(last)

    @pl.when(is_corner)
    def _():
        for h in range(heads - NEAR):
            send_q(h).start()

    @pl.when(is_near)
    def _():
        for h in range(heads):
            lend_q(h).start()

    @pl.when(is_cut_row)
    def _():
        for h in range(tail, heads):
            send_pal(q_s.at[h], pal_q.at[h - tail], 0, h - tail).start()

    exponent_scale = (HD ** (-0.5)) * LOG2E

    def attend(queries, slots, h, old_max=None):
        scores = [
            lax.dot_general(queries, kv[slot, h, 0], (((1,), (1,)), ((), ())), preferred_element_type=jnp.float32)
            for slot in slots
        ]
        row_max = functools.reduce(jnp.maximum, [jnp.max(s, axis=1, keepdims=True) for s in scores])
        if old_max is not None:
            row_max = jnp.maximum(row_max, old_max)
        weights = [jnp.exp2((s - row_max) * exponent_scale) for s in scores]
        total = sum(jnp.sum(w, axis=1, keepdims=True) for w in weights)
        result = sum(
            jnp.dot(w.astype(jnp.bfloat16), kv[slot, h, 1], preferred_element_type=jnp.float32)
            for w, slot in zip(weights, slots)
        )
        return row_max, total, result

    def attend_more(slots, h):
        old_max = m_s[h][:, :1]
        row_max, total, result = attend(q_s[h], slots, h, old_max)
        keep = jnp.exp2((old_max - row_max) * exponent_scale)
        return row_max, total + keep * l_s[h][:, :1], result + keep * acc_s[h]

    def hold(h, row_max, total, result):
        m_s[h] = jnp.broadcast_to(row_max, (rows, HD))
        l_s[h] = jnp.broadcast_to(total, (rows, HD))
        acc_s[h] = result

    def finish(h, row_max, total, result):
        done_s[h] = (result / total).astype(jnp.bfloat16)

    def share(h, queries, slots, share_to, stat_to):
        row_max, total, result = attend(queries, slots, h)
        share_to[...] = (result / total).astype(jnp.bfloat16)
        lane = lax.broadcasted_iota(jnp.int32, (rows, HD), 1)
        stats = jnp.where(lax.rem(lane, 8) < 4, row_max, total)
        stat_to[...] = jnp.transpose(stats)[:8]

    def merge(h, shared, stats):
        row_max, total, result = m_s[h], l_s[h], acc_s[h]
        their_max = jnp.transpose(jnp.broadcast_to(stats[0:1, :], (HD, rows)))
        their_total = jnp.transpose(jnp.broadcast_to(stats[4:5, :], (HD, rows)))
        top = jnp.maximum(row_max, their_max)
        keep = jnp.exp2((row_max - top) * exponent_scale)
        weight = their_total * jnp.exp2((their_max - top) * exponent_scale)
        return top, keep * total + weight, keep * result + weight * shared[...].astype(jnp.float32)

    width = out_ref.shape[1]
    chunk = OUT_CHUNK

    def mix(first, stop):
        lhs = jnp.concatenate(
            [part for h in range(first, stop) for part in (done_s[h, own_half, :], other_s[h])], axis=1
        )
        depth = slice(2 * first * HD, 2 * stop * HD)

        def product(n):
            columns = pl.ds(n * chunk, chunk)
            return columns, jnp.dot(lhs, w_s[depth, columns], preferred_element_type=jnp.float32)

        return (product(n) for n in range(width // chunk))

    def ready(h):
        return jnp.logical_and(h >= 0, h < heads)

    @pl.loop(0, 2 * heads + 2)
    def _(i):
        settled = jnp.where(
            jnp.logical_and(role == 0, i == heads + 1), last, i - heads - jnp.where(is_corner, 3, 2)
        )
        settles = jnp.logical_and(ready(settled), jnp.logical_or(role != 0, i <= 2 * heads))
        pl.when(settles)(lambda: send_att(settled).start())

        @pl.when(jnp.logical_and(i < heads, jnp.logical_or(is_outer_row, i > 0)))
        def _():
            arrive(pal, i)
            pl.when(jnp.logical_and(is_cut_row, i < last))(lambda: cross(pal, i).start())

        @pl.when(is_cut_row)
        def _():
            @pl.when(i == 0)
            def _():
                for part in range(2):
                    arrive(pal, 0, part, FIRST_OWN)
                    cross(pal, 0, part, FIRST_CROSSED).start()
                arrive(side, 0)
                cross(side, 0).start()
                arrive(straight, last)
                up_down(straight, last).start()

            def pass_on(h):
                arrive(side, h)
                cross(side, h).start()

            def take(from_pal, h):
                if from_pal:
                    for part in range(2) if h == 0 else (None,):
                        arrive(swapped, h, part, FIRST_CROSSED)
                    up_down(swapped, h).start()
                else:
                    arrive(far, h)
                    if h < tail:
                        to_pal(far, h).start()

            at = 0
            for place, (from_pal, h) in enumerate(crossing_order(heads)):
                at = max(at, h)
                if not from_pal and h > 0:
                    pl.when(i == at)(lambda h=h: pass_on(h))
            for place, (from_pal, h) in enumerate(crossing_order(heads)):
                pl.when(i == place + 1)(lambda from_pal=from_pal, h=h: take(from_pal, h))

        @pl.when(is_outer_row)
        def _():
            @pl.when(i == 1)
            def _():
                arrive(straight, last)
                to_pal(straight, last).start()

            def relay(j):
                arrive(swapped, j)
                to_pal(swapped, j).start()

            for place, (from_pal, h) in enumerate(crossing_order(heads)):
                if from_pal:
                    at = place + (3 if h < heads - 3 else 2)
                    pl.when(i == at)(lambda h=h: relay(h))

        nearby = i - heads

        @pl.when(jnp.logical_and(is_near, jnp.logical_and(nearby >= heads - NEAR, nearby < heads)))
        def _():
            send_q(nearby).wait_recv()
            share(nearby, guest_q[nearby], (2, 6), share_out.at[nearby], stat_out.at[nearby])
            for copy in send_share(nearby):
                copy.start()

        @pl.when(jnp.logical_and(is_cut_row, jnp.logical_and(nearby >= tail, nearby < heads)))
        def _():
            index = nearby - tail
            send_pal(q_s.at[nearby], pal_q.at[index], 0, index).wait_recv()
            share(nearby, pal_q[index], (far,), pal_share_out.at[index], pal_stat_out.at[index])
            for copy in send_pal_share(index):
                copy.start()

        @pl.when(i == 2 * heads - jnp.where(jnp.logical_and(is_cut_row, group == 1), 0, 1))
        def _():
            pltpu.make_async_copy(w_hbm, w_s, w_sem).wait()
            recv_att(0, early_heads, 0)
            for columns, value in mix(0, early_heads):
                mixed_s[:, columns] = value

        @pl.when(jnp.logical_and(i >= 1, i <= heads))
        def _():
            for which in range(2):
                load_w(i - 1, which).start()

        @pl.when(i < heads)
        def _():
            hold(i, *attend(q_s[i], (row_base, row_base + 1), i))

        @pl.when(jnp.logical_and(i < heads, role == 0))
        def _():
            lend_q(i).wait_recv()
            share(i, share_in[i], (1,), share_out.at[i], stat_out.at[i])
            for copy in send_share(i, up_down_device):
                copy.start()

        @pl.when(jnp.logical_and(ready(i - last), is_near))
        def _():
            h = i - last
            for copy in send_share(h):
                copy.wait_recv()
            hold(h, *merge(h, share_in.at[h], stat_in.at[h]))

        @pl.when(jnp.logical_and(role == 0, i == 2))
        def _():
            for h in range(heads - NEAR, heads):
                send_q(h).wait_recv()
                send_q(h, source=guest_q).start()

        @pl.when(is_outer_row)
        def _():
            h = jnp.where(i == heads, last, i - heads - 1)

            @pl.when(jnp.logical_and(i >= heads, i < 2 * heads))
            def _():
                arrive(jnp.where(h == last, swapped, straight), h)
                pl.when(jnp.logical_and(role == 0, h == last))(lambda: up_down(swapped, h, way=3).start())
                state = attend_more((4, 5), h)
                pl.when(role == 0)(lambda: finish(h, *state))
                pl.when(is_corner)(lambda: hold(h, *state))

            ending = i - heads - 2

            @pl.when(jnp.logical_and(ready(ending), is_corner))
            def _():
                for copy in send_share(ending):
                    copy.wait_recv()
                finish(ending, *merge(ending, share_in.at[ending], stat_in.at[ending]))

        ending = i - heads - 1

        @pl.when(jnp.logical_and(ready(ending), is_near))
        def _():
            pl.when(ending == last)(lambda: arrive(5, ending))
            hold(ending, *attend_more((5, 6), ending))

        @pl.when(jnp.logical_and(ready(ending), is_host))
        def _():
            @pl.when(ending < tail)
            def _():
                send_q(ending).wait_recv()
                arrive(6, ending)
                share(ending, guest_q[ending], (2, 6), share_out.at[ending], stat_out.at[ending])
                for copy in send_share(ending):
                    copy.start()

            hold(ending, *attend_more((7,), ending))

        @pl.when(jnp.logical_and(is_cut_row, jnp.logical_and(ending >= 0, ending < tail)))
        def _():
            pl.when(is_near)(lambda: arrive(7, ending))
            finish(ending, *attend_more((pal_far,), ending))

        @pl.when(jnp.logical_and(is_cut_row, jnp.logical_and(ending >= tail, ending < heads)))
        def _():
            index = ending - tail
            for copy in send_pal_share(index):
                copy.wait_recv()
            finish(ending, *merge(ending, pal_share_in.at[index], pal_stat_in.at[index]))

    pl.when(is_corner)(lambda: send_att(last).start())
    recv_att(early_heads, heads, 1)
    for columns, value in mix(early_heads, heads):
        out_ref[:, columns] = (mixed_s[:, columns] + value).astype(out_ref.dtype)

    def drain(way, count):
        tiles_sent = kv.at[pl.ds(0, count)]
        pltpu.make_async_remote_copy(
            src_ref=tiles_sent,
            dst_ref=tiles_sent,
            send_sem=send_sem.at[way],
            recv_sem=recv_sem.at[0, 0],
            device_id={"tm": pal_device},
            device_id_type=MESH,
        ).wait_send()

    def drain_rows(sent, sem):
        pltpu.make_async_remote_copy(
            src_ref=sent,
            dst_ref=sent,
            send_sem=sem,
            recv_sem=recv_sem.at[0, 0],
            device_id={"tm": pal_device},
            device_id_type=MESH,
        ).wait_send()

    pl.when(is_outer_row)(lambda: drain(0, 2))

    @pl.when(is_cut_row)
    def _():
        drain_rows(kv.at[pl.ds(0, 2), pl.ds(0, heads - NEAR // 2)], send_sem.at[0])
        drain_rows(pal_q, pal_send_sem.at[0])
        drain_rows(pal_share_out, pal_send_sem.at[1])
        drain_rows(pal_stat_out, pal_send_sem.at[2])

    drain(1, 1)
    drain_rows(other_s, att_send_sem)
    pl.when(role == 0)(lambda: drain_rows(kv.at[0, 0], send_sem.at[3]))
    pl.when(role == 0)(lambda: drain_rows(guest_q.at[pl.ds(0, NEAR)], q_send_sem))
    pl.when(jnp.logical_or(is_corner, is_near))(lambda: drain_rows(q_s, q_send_sem))
    pl.when(is_cut_row)(lambda: drain(2, 2))
    for count, sender in ((heads, role == 0), (heads - NEAR, is_host), (NEAR, is_near)):
        pl.when(sender)(lambda count=count: drain_rows(share_out.at[pl.ds(0, count)], share_send_sem.at[0]))
        pl.when(sender)(lambda count=count: drain_rows(stat_out.at[pl.ds(0, count)], share_send_sem.at[1]))


def balanced_call(query_states, key_states, value_states, out_weight):
    rows, half_width = query_states.shape[1:]
    heads = half_width // HD
    depth, width = out_weight.shape
    tiles = lax.axis_size("tm") // 2
    dma = pltpu.SemaphoreType.DMA
    return pl.pallas_call(
        functools.partial(balanced_kernel, tiles),
        out_shape=jax.ShapeDtypeStruct((rows // 2, width), jnp.bfloat16),
        in_specs=[pl.BlockSpec(memory_space=pl.ANY)] * 4,
        out_specs=pl.BlockSpec(memory_space=pltpu.VMEM),
        scratch_shapes=[
            pltpu.VMEM((heads, rows, HD), jnp.bfloat16),
            pltpu.VMEM((heads, rows, HD), jnp.bfloat16),
            pltpu.VMEM((tiles, heads, 2, rows, HD), jnp.bfloat16),
            pltpu.VMEM((depth, width), jnp.bfloat16),
            pltpu.VMEM((heads, rows, HD), jnp.float32),
            pltpu.VMEM((heads, rows, HD), jnp.float32),
            pltpu.VMEM((heads, rows, HD), jnp.float32),
            pltpu.VMEM((rows // 2, width), jnp.float32),
            pltpu.VMEM((heads, rows, HD), jnp.bfloat16),
            pltpu.VMEM((heads, rows // 2, HD), jnp.bfloat16),
            pltpu.VMEM((heads, rows, HD), jnp.bfloat16),
            pltpu.VMEM((heads, rows, HD), jnp.bfloat16),
            pltpu.VMEM((heads, 8, rows), jnp.float32),
            pltpu.VMEM((heads, 8, rows), jnp.float32),
            pltpu.VMEM((NEAR, rows, HD), jnp.bfloat16),
            pltpu.VMEM((NEAR, rows, HD), jnp.bfloat16),
            pltpu.VMEM((NEAR, rows, HD), jnp.bfloat16),
            pltpu.VMEM((NEAR, 8, rows), jnp.float32),
            pltpu.VMEM((NEAR, 8, rows), jnp.float32),
            dma((heads,)),
            dma,
            dma,
            dma((4,)),
            dma((tiles, heads)),
            dma,
            dma((heads,)),
            dma((2,)),
            dma((2, heads)),
            dma((3,)),
            dma((3, NEAR)),
            dma,
            dma((2,)),
        ],
        compiler_params=pltpu.CompilerParams(
            collective_id=0, has_side_effects=True, vmem_limit_bytes=40 * 1024 * 1024
        ),
    )(*(pltpu.with_memory_space_constraint(x, pltpu.HBM) for x in (query_states, key_states, value_states, out_weight)))


def general_call(query_states, key_states, value_states, out_weight):
    rows, half_width = query_states.shape[1:]
    heads = half_width // HD
    depth, width = out_weight.shape
    time_count = lax.axis_size("tm") // (2 * TCOLS)
    return pl.pallas_call(
        functools.partial(general_kernel, time_count, heads),
        out_shape=jax.ShapeDtypeStruct((rows // 2, width), jnp.bfloat16),
        in_specs=[pl.BlockSpec(memory_space=pl.ANY)] * 4,
        out_specs=pl.BlockSpec(memory_space=pltpu.VMEM),
        scratch_shapes=[
            pltpu.VMEM((heads, rows, HD), jnp.bfloat16),
            pltpu.VMEM((11, heads, 2, rows, HD), jnp.bfloat16),
            pltpu.VMEM((depth, width), jnp.bfloat16),
            pltpu.VMEM((heads, rows, HD), jnp.float32),
            pltpu.VMEM((heads, rows, HD), jnp.float32),
            pltpu.VMEM((heads, rows, HD), jnp.float32),
            pltpu.VMEM((heads, rows // 2, HD), jnp.bfloat16),
            pltpu.VMEM((2, heads, rows // 2, HD), jnp.bfloat16),
            pltpu.SemaphoreType.DMA((3, heads)),
            pltpu.SemaphoreType.DMA,
            pltpu.SemaphoreType.DMA((13, heads)),
            pltpu.SemaphoreType.DMA((11, heads)),
            pltpu.SemaphoreType.DMA((heads,)),
            pltpu.SemaphoreType.DMA((heads,)),
        ],
        compiler_params=pltpu.CompilerParams(
            collective_id=0, has_side_effects=True, vmem_limit_bytes=56 * 1024 * 1024
        ),
    )(query_states, key_states, value_states, out_weight)


def per_device(query_states, key_states, value_states, out_weight):
    two_times = lax.axis_size("tm") == 4 * TCOLS and query_states.shape[2] >= 4 * HD
    call = balanced_call if two_times else general_call
    return call(query_states, key_states, value_states, out_weight)


def solution(mesh):
    in_specs = (
        P(("parts", "tm"), None, None),
        P(("parts", "tm"), None, None),
        P(("parts", "tm"), None, None),
        P(),
    )
    out_specs = P(("parts", "tm"), None)
    return jax.shard_map(
        per_device, mesh=mesh, in_specs=in_specs, out_specs=out_specs, check_vma=False
    )
```

```python
import functools

import jax
import jax.numpy as jnp
from jax import lax
from jax.experimental import pallas as pl
from jax.experimental.pallas import tpu as pltpu
from jax.sharding import PartitionSpec as P

TCOLS = 4
HD = 128
MESH = pl.DeviceIdType.MESH
LOG2E = 1.4426950408889634

DIRECT_OWN = 2
DIRECT_CORNER = 1
AHEAD = 2
LAG_TIME = 2
LAG_CORNER = 3
LAG_MIDDLE = 5

NEAR = 2
OUT_CHUNK = 512
FIRST_OWN, FIRST_CROSSED = range(2)


def slot_of(time_step, col_step):
    return (time_step + 1) * 3 + col_step + 1


def general_kernel(
    time_count,
    heads,
    q_hbm,
    k_hbm,
    v_hbm,
    w_hbm,
    out_ref,
    q_s,
    kv,
    w_s,
    m_s,
    l_s,
    acc_s,
    outgoing,
    attended,
    load_sem,
    w_sem,
    send_sem,
    recv_sem,
    att_send_sem,
    att_recv_sem,
):
    rows = q_s.shape[1]
    half = rows // 2
    me = lax.axis_index("tm")
    group = lax.rem(me, 2)
    tile = lax.div(me, 2)
    col = lax.rem(tile, TCOLS)
    time = lax.div(tile, TCOLS)
    has_time = {-1: time > 0, 1: time < time_count - 1}
    has_col = {-1: col > 0, 1: col < TCOLS - 1}
    outer = 1 - 2 * lax.rem(col, 2)
    is_edge = jnp.logical_or(col == 0, col == TCOLS - 1)
    is_middle = jnp.logical_not(is_edge)
    outer_device = me + 2 * outer
    middle_device = me - 2 * outer
    relay_device = me + 4 * outer
    other_core = me + 1 - 2 * group
    own_slot = slot_of(0, 0)
    stride = TCOLS
    has_hop = {-1: tile >= stride // 2, 1: tile + stride // 2 < time_count * TCOLS}
    is_hop = jnp.logical_and(has_hop[-1], has_hop[1])

    def hop_slot(step):
        return 9 if step < 0 else 10

    def load(h):
        columns = pl.ds(pl.multiple_of(h * HD, HD), HD)
        return (
            pltpu.make_async_copy(k_hbm.at[0, :, columns], kv.at[own_slot, h, 0], load_sem.at[0, h]),
            pltpu.make_async_copy(v_hbm.at[0, :, columns], kv.at[own_slot, h, 1], load_sem.at[1, h]),
            pltpu.make_async_copy(q_hbm.at[0, :, columns], q_s.at[h], load_sem.at[2, h]),
        )

    for h in range(heads):
        for copy in load(jnp.int32(h)):
            copy.start()
    w_copy = pltpu.make_async_copy(w_hbm, w_s, w_sem)
    w_copy.start()

    barrier = pltpu.get_barrier_semaphore()

    def greet(device):
        pl.semaphore_signal(barrier, inc=1, device_id={"tm": device}, device_id_type=MESH)

    greetings = jnp.int32(2)
    greet(other_core)
    greet(outer_device)
    for step in (-1, 1):
        pl.when(has_hop[step])(lambda step=step: greet(me + stride * step))
        greetings = greetings + has_hop[step].astype(jnp.int32)
    pl.when(is_middle)(lambda: greet(middle_device))
    greetings = greetings + is_middle.astype(jnp.int32)
    pl.semaphore_wait(barrier, greetings)

    def transfer(kind, h, source, target, device):
        return pltpu.make_async_remote_copy(
            src_ref=kv.at[source, h],
            dst_ref=kv.at[target, h],
            send_sem=send_sem.at[kind, h],
            recv_sem=recv_sem.at[target, h],
            device_id={"tm": device},
            device_id_type=MESH,
        )

    def arrive(slot, h):
        transfer(0, h, slot, slot, other_core).wait_recv()

    def send_time(step, h):
        return transfer(0 if step < 0 else 1, h, own_slot, hop_slot(step), me + stride * step)

    def send_hop(step, h):
        return transfer(11 if step < 0 else 12, h, hop_slot(step), slot_of(-step, 0), me + stride * step)

    def send_outer(step, h):
        return transfer(3 + step, h, slot_of(step, 0), slot_of(step, 0) - outer, outer_device)

    def send_middle(step, h):
        return transfer(6 + step, h, slot_of(step, 0), slot_of(step, 0) + outer, middle_device)

    def send_relay(step, h):
        return transfer(9 + step, h, slot_of(step, 0) + outer, slot_of(step, 0) - outer, relay_device)

    def straight(step, h):
        return h >= heads - (DIRECT_OWN if step == 0 else DIRECT_CORNER)

    def send_att(h):
        return pltpu.make_async_remote_copy(
            src_ref=outgoing.at[h],
            dst_ref=attended.at[group, h],
            send_sem=att_send_sem.at[h],
            recv_sem=att_recv_sem.at[h],
            device_id={"tm": other_core},
            device_id_type=MESH,
        )

    def recv_att(h):
        return pltpu.make_async_remote_copy(
            src_ref=outgoing.at[h],
            dst_ref=attended.at[1 - group, h],
            send_sem=att_send_sem.at[h],
            recv_sem=att_recv_sem.at[h],
            device_id={"tm": other_core},
            device_id_type=MESH,
        )

    def send_own(h):
        for copy in load(h):
            copy.wait()
        for step in (-1, 1):
            pl.when(has_time[step])(lambda step=step: send_time(step, h).start())
        send_outer(0, h).start()
        if DIRECT_OWN:
            pl.when(jnp.logical_and(is_middle, straight(0, h)))(lambda: send_middle(0, h).start())

    for h in range(AHEAD):
        send_own(jnp.int32(h))

    exponent_scale = (HD ** (-0.5)) * LOG2E

    def attend(slot, h, first=False):
        scores = lax.dot_general(
            q_s[h], kv[slot, h, 0], (((1,), (1,)), ((), ())), preferred_element_type=jnp.float32
        )
        row_max = jnp.max(scores, axis=1, keepdims=True)
        if not first:
            old_max = m_s[h][:, :1]
            row_max = jnp.maximum(row_max, old_max)
        weights = jnp.exp2((scores - row_max) * exponent_scale)
        total = jnp.sum(weights, axis=1, keepdims=True)
        result = jnp.dot(weights.astype(jnp.bfloat16), kv[slot, h, 1], preferred_element_type=jnp.float32)
        if not first:
            keep = jnp.exp2((old_max - row_max) * exponent_scale)
            total = total + keep * l_s[h][:, :1]
            result = result + keep * acc_s[h]
        m_s[h] = jnp.broadcast_to(row_max, (rows, HD))
        l_s[h] = jnp.broadcast_to(total, (rows, HD))
        acc_s[h] = result

    def finish(h):
        acc_s[h] = acc_s[h] / l_s[h]
        attended[group, h] = acc_s[h, pl.ds(pl.multiple_of(group * half, 16), half), :].astype(jnp.bfloat16)
        outgoing[h] = acc_s[h, pl.ds(pl.multiple_of((1 - group) * half, 16), half), :].astype(jnp.bfloat16)

    def ready(h):
        return jnp.logical_and(h >= 0, h < heads)

    @pl.loop(0, heads + LAG_MIDDLE)
    def _(i):
        pl.when(i + AHEAD < heads)(lambda: send_own(i + AHEAD))

        @pl.when(jnp.logical_and(i < heads, is_edge))
        def _():
            arrive(own_slot + outer, i)
            pl.when(jnp.logical_not(straight(0, i)))(lambda: send_relay(0, i).start())

        @pl.when(jnp.logical_and(i < heads, is_hop))
        def _():
            for step in (-1, 1):
                arrive(hop_slot(step), i)
                send_hop(step, i).start()

        crossed = i - LAG_TIME

        @pl.when(ready(crossed))
        def _():
            for step in (-1, 1):

                @pl.when(has_time[step])
                def _():
                    arrive(slot_of(step, 0), crossed)
                    send_outer(step, crossed).start()
                    if DIRECT_CORNER:
                        pl.when(jnp.logical_and(is_middle, straight(step, crossed)))(
                            lambda: send_middle(step, crossed).start()
                        )

        back = i - LAG_CORNER

        @pl.when(jnp.logical_and(ready(back), is_edge))
        def _():
            for step in (-1, 1):

                @pl.when(has_time[step])
                def _():
                    arrive(slot_of(step, 0) + outer, back)
                    pl.when(jnp.logical_not(straight(step, back)))(lambda: send_relay(step, back).start())

        pl.when(i < heads)(lambda: attend(own_slot, i, first=True))

        @pl.when(ready(crossed))
        def _():
            for step in (-1, 1):
                pl.when(has_time[step])(lambda: attend(slot_of(step, 0), crossed))

        @pl.when(ready(back))
        def _():
            pl.when(is_middle)(lambda: arrive(own_slot + outer, back))
            attend(own_slot + outer, back)
            for step in (-1, 1):

                @pl.when(has_time[step])
                def _():
                    pl.when(is_middle)(lambda: arrive(slot_of(step, 0) + outer, back))
                    attend(slot_of(step, 0) + outer, back)

        last = i - LAG_MIDDLE

        @pl.when(last >= 1)
        def _():
            send_att(last - 1).start()

        @pl.when(last >= 0)
        def _():
            @pl.when(is_middle)
            def _():
                arrive(own_slot - outer, last)
                attend(own_slot - outer, last)
                for step in (-1, 1):

                    @pl.when(has_time[step])
                    def _():
                        arrive(slot_of(step, 0) - outer, last)
                        attend(slot_of(step, 0) - outer, last)

            finish(last)

    send_att(heads - 1).start()
    w_copy.wait()

    for h in range(heads):
        recv_att(h).wait_recv()

    width = out_ref.shape[1]
    chunk = 512
    lhs = jnp.concatenate([attended[part, h] for part in range(2) for h in range(heads)], axis=1)

    @pl.loop(0, width // chunk, unroll=True)
    def _(n):
        columns = pl.ds(pl.multiple_of(n * chunk, chunk), chunk)
        out_ref[:, columns] = jnp.dot(lhs, w_s[:, columns], preferred_element_type=jnp.float32).astype(
            out_ref.dtype
        )

    @pl.loop(0, heads)
    def _(h):
        send_att(h).wait_send()
        send_outer(0, h).wait_send()

        @pl.when(is_hop)
        def _():
            for step in (-1, 1):
                send_hop(step, h).wait_send()

        if DIRECT_OWN:
            pl.when(jnp.logical_and(is_middle, straight(0, h)))(lambda: send_middle(0, h).wait_send())
        pl.when(jnp.logical_and(is_edge, jnp.logical_not(straight(0, h))))(
            lambda: send_relay(0, h).wait_send()
        )
        for step in (-1, 1):

            @pl.when(has_time[step])
            def _():
                send_time(step, h).wait_send()
                send_outer(step, h).wait_send()
                if DIRECT_CORNER:
                    pl.when(jnp.logical_and(is_middle, straight(step, h)))(
                        lambda: send_middle(step, h).wait_send()
                    )
                pl.when(jnp.logical_and(is_edge, jnp.logical_not(straight(step, h))))(
                    lambda: send_relay(step, h).wait_send()
                )


def crossing_order(heads):
    order = [(from_pal, h) for h in range(heads - 4) for from_pal in (True, False)]
    order += [(True, heads - 4), (True, heads - 3), (False, heads - 4), (True, heads - 2)]
    return order + [(False, h) for h in range(heads - 3, heads)]


def balanced_kernel(
    tiles,
    q_hbm,
    k_hbm,
    v_hbm,
    w_hbm,
    out_ref,
    q_s,
    guest_q,
    kv,
    w_s,
    m_s,
    l_s,
    acc_s,
    mixed_s,
    done_s,
    other_s,
    share_out,
    share_in,
    stat_out,
    stat_in,
    pal_q,
    pal_share_out,
    pal_share_in,
    pal_stat_out,
    pal_stat_in,
    load_sem,
    q_sem,
    w_sem,
    send_sem,
    recv_sem,
    q_send_sem,
    q_recv_sem,
    share_send_sem,
    share_recv_sem,
    pal_send_sem,
    pal_recv_sem,
    att_send_sem,
    att_recv_sem,
):
    heads, rows = q_s.shape[:2]
    half = rows // 2
    last = heads - 1
    early_heads = heads - 3
    first_heads = heads - 4
    tail = heads - NEAR
    me = lax.axis_index("tm")
    group = lax.rem(me, 2)
    tile = lax.div(me, 2)
    lower = tile < tiles // 2
    role = jnp.where(lower, tile, tiles - 1 - tile)
    side = lax.rem(role, 2)
    is_cut_row = role >= 2
    is_outer_row = jnp.logical_not(is_cut_row)
    is_corner = role == 1
    is_near = role == 2
    is_host = role == 3
    pal = role + 1 - 2 * side
    row_base = role - side
    swapped = 5 - side
    straight = 4 + side
    far = 6 + side
    pal_far = 7 - side
    other_core = me + 1 - 2 * group

    def device_of(slot):
        return 2 * jnp.where(lower, slot, tiles - 1 - slot) + group

    pal_device = device_of(pal)
    up_down_device = device_of(jnp.where(is_cut_row, role - 2, role + 2))
    cut_device = device_of(role + 2)
    corner_device = device_of(1)

    def load(h):
        columns = pl.ds(pl.multiple_of(h * HD, HD), HD)
        return (
            pltpu.make_async_copy(k_hbm.at[0, :, columns], kv.at[role, h, 0], load_sem.at[h]),
            pltpu.make_async_copy(v_hbm.at[0, :, columns], kv.at[role, h, 1], load_sem.at[h]),
            pltpu.make_async_copy(q_hbm.at[0, :, columns], q_s.at[h], q_sem),
        )

    def load_w(h, which):
        owner = group if which == 0 else 1 - group
        source = pl.ds(pl.multiple_of((owner * heads + h) * HD, HD), HD)
        target = pl.ds(pl.multiple_of((2 * h + which) * HD, HD), HD)
        return pltpu.make_async_copy(w_hbm.at[source], w_s.at[target], w_sem)

    for h in (last, *range(last)):
        for copy in load(jnp.int32(h)):
            copy.start()

    barrier = pltpu.get_barrier_semaphore()

    def greet(device):
        pl.semaphore_signal(barrier, inc=1, device_id={"tm": device}, device_id_type=MESH)

    greet(other_core)
    greet(pal_device)
    greet(up_down_device)
    pl.when(is_cut_row)(lambda: greet(cut_device))
    pl.when(is_corner)(lambda: greet(device_of(2)))
    pl.semaphore_wait(barrier, 3 + is_cut_row.astype(jnp.int32) + is_near.astype(jnp.int32))

    def transfer(way, slot, h, target, device, part=None, kind=0, landing=0):
        return pltpu.make_async_remote_copy(
            src_ref=kv.at[slot, h] if part is None else kv.at[slot, h, part],
            dst_ref=kv.at[target, h] if part is None else kv.at[target, h, part],
            send_sem=send_sem.at[way],
            recv_sem=recv_sem.at[landing, kind] if part == 1 else recv_sem.at[target, h],
            device_id={"tm": device},
            device_id_type=MESH,
        )

    def arrive(slot, h, part=None, kind=0):
        transfer(0, slot, h, slot, pal_device, part, kind, role).wait_recv()

    def to_pal(slot, h, part=None, kind=0):
        return transfer(0, slot, h, slot, pal_device, part, kind, pal)

    def up_down(slot, h, way=1):
        return transfer(way, slot, h, slot, up_down_device)

    def cross(slot, h, part=None, kind=0):
        return transfer(2, slot, h, tiles - 1 - slot, cut_device, part, kind, pal)

    def split_or_whole(is_split, act):
        pl.when(jnp.logical_not(is_split))(lambda: act(None))

        @pl.when(is_split)
        def _():
            for part in range(2):
                act(part)

    def send_q(h, source=q_s, device=up_down_device):
        return pltpu.make_async_remote_copy(
            src_ref=source.at[h],
            dst_ref=guest_q.at[h],
            send_sem=q_send_sem,
            recv_sem=q_recv_sem.at[h],
            device_id={"tm": device},
            device_id_type=MESH,
        )

    def lend_q(h):
        return pltpu.make_async_remote_copy(
            src_ref=q_s.at[h],
            dst_ref=share_in.at[h],
            send_sem=q_send_sem,
            recv_sem=share_recv_sem.at[0, h],
            device_id={"tm": up_down_device},
            device_id_type=MESH,
        )

    def send_share(h, device=corner_device):
        return tuple(
            pltpu.make_async_remote_copy(
                src_ref=source.at[h],
                dst_ref=target.at[h],
                send_sem=share_send_sem.at[which],
                recv_sem=share_recv_sem.at[which, h],
                device_id={"tm": device},
                device_id_type=MESH,
            )
            for which, (source, target) in enumerate(((share_out, share_in), (stat_out, stat_in)))
        )

    def send_pal(source, target, which, index):
        return pltpu.make_async_remote_copy(
            src_ref=source,
            dst_ref=target,
            send_sem=pal_send_sem.at[which],
            recv_sem=pal_recv_sem.at[which, index],
            device_id={"tm": pal_device},
            device_id_type=MESH,
        )

    def send_pal_share(index):
        return (
            send_pal(pal_share_out.at[index], pal_share_in.at[index], 1, index),
            send_pal(pal_stat_out.at[index], pal_stat_in.at[index], 2, index),
        )

    own_half = pl.ds(pl.multiple_of(group * half, 16), half)
    their_half = pl.ds(pl.multiple_of((1 - group) * half, 16), half)

    def send_att(h):
        return pltpu.make_async_remote_copy(
            src_ref=done_s.at[h, their_half],
            dst_ref=other_s.at[h],
            send_sem=att_send_sem,
            recv_sem=att_recv_sem.at[jnp.where(h < first_heads, 0, jnp.where(h < early_heads, 1, 2))],
            device_id={"tm": other_core},
            device_id_type=MESH,
        )

    def recv_att(first, stop, which):
        rows_in = other_s.at[pl.ds(first, stop - first)]
        pltpu.make_async_copy(rows_in, rows_in, att_recv_sem.at[which]).wait()

    def send_own(h):
        if h == 0:
            split_or_whole(is_cut_row, lambda part: to_pal(role, 0, part, FIRST_OWN).start())
        else:
            to_pal(role, h).start()
        pl.when(is_outer_row)(lambda: up_down(role, h).start())

    for h in (last, *range(last)):
        pltpu.make_async_copy(kv.at[role, h], kv.at[role, h], load_sem.at[h]).wait()
        if h == last:
            pl.when(is_cut_row)(lambda: cross(role, last).start())
        else:
            send_own(h)
        if h == 1:
            pltpu.make_async_copy(q_s, q_s, q_sem).wait()

            @pl.when(is_corner)
            def _():
                for near in range(heads - NEAR, heads):
                    send_q(near, device=pal_device).start()
    send_own(last)

    @pl.when(is_corner)
    def _():
        for h in range(heads - NEAR):
            send_q(h).start()

    @pl.when(is_near)
    def _():
        for h in range(heads):
            lend_q(h).start()

    @pl.when(is_cut_row)
    def _():
        for h in range(tail, heads):
            send_pal(q_s.at[h], pal_q.at[h - tail], 0, h - tail).start()

    exponent_scale = (HD ** (-0.5)) * LOG2E

    def attend(queries, slots, h, old_max=None):
        scores = [
            lax.dot_general(queries, kv[slot, h, 0], (((1,), (1,)), ((), ())), preferred_element_type=jnp.float32)
            for slot in slots
        ]
        row_max = functools.reduce(jnp.maximum, [jnp.max(s, axis=1, keepdims=True) for s in scores])
        if old_max is not None:
            row_max = jnp.maximum(row_max, old_max)
        weights = [jnp.exp2((s - row_max) * exponent_scale) for s in scores]
        total = sum(jnp.sum(w, axis=1, keepdims=True) for w in weights)
        result = sum(
            jnp.dot(w.astype(jnp.bfloat16), kv[slot, h, 1], preferred_element_type=jnp.float32)
            for w, slot in zip(weights, slots)
        )
        return row_max, total, result

    def attend_more(slots, h):
        old_max = m_s[h][:, :1]
        row_max, total, result = attend(q_s[h], slots, h, old_max)
        keep = jnp.exp2((old_max - row_max) * exponent_scale)
        return row_max, total + keep * l_s[h][:, :1], result + keep * acc_s[h]

    def hold(h, row_max, total, result):
        m_s[h] = jnp.broadcast_to(row_max, (rows, HD))
        l_s[h] = jnp.broadcast_to(total, (rows, HD))
        acc_s[h] = result

    def finish(h, row_max, total, result):
        done_s[h] = (result / total).astype(jnp.bfloat16)

    def share(h, queries, slots, share_to, stat_to):
        row_max, total, result = attend(queries, slots, h)
        share_to[...] = (result / total).astype(jnp.bfloat16)
        lane = lax.broadcasted_iota(jnp.int32, (rows, HD), 1)
        stats = jnp.where(lax.rem(lane, 8) < 4, row_max, total)
        stat_to[...] = jnp.transpose(stats)[:8]

    def merge(h, shared, stats):
        row_max, total, result = m_s[h], l_s[h], acc_s[h]
        their_max = jnp.transpose(jnp.broadcast_to(stats[0:1, :], (HD, rows)))
        their_total = jnp.transpose(jnp.broadcast_to(stats[4:5, :], (HD, rows)))
        top = jnp.maximum(row_max, their_max)
        keep = jnp.exp2((row_max - top) * exponent_scale)
        weight = their_total * jnp.exp2((their_max - top) * exponent_scale)
        return top, keep * total + weight, keep * result + weight * shared[...].astype(jnp.float32)

    width = out_ref.shape[1]
    chunk = OUT_CHUNK

    def mix(first, stop):
        lhs = jnp.concatenate(
            [part for h in range(first, stop) for part in (done_s[h, own_half, :], other_s[h])], axis=1
        )
        depth = slice(2 * first * HD, 2 * stop * HD)

        def product(n):
            columns = pl.ds(n * chunk, chunk)
            return columns, jnp.dot(lhs, w_s[depth, columns], preferred_element_type=jnp.float32)

        return (product(n) for n in range(width // chunk))

    def ready(h):
        return jnp.logical_and(h >= 0, h < heads)

    is_slow = jnp.logical_and(is_cut_row, group == 0)
    mix_at = 2 * heads - jnp.where(is_slow, 3, jnp.where(is_cut_row, 0, 1))
    mix_gap = is_slow.astype(jnp.int32)

    @pl.loop(0, 2 * heads + 2)
    def _(i):
        settled = jnp.where(
            jnp.logical_and(role == 0, i == heads + 1), last, i - heads - jnp.where(is_corner, 3, 2)
        )
        settles = jnp.logical_and(ready(settled), jnp.logical_or(role != 0, i <= 2 * heads))
        pl.when(settles)(lambda: send_att(settled).start())

        @pl.when(i == mix_at)
        def _():
            pltpu.make_async_copy(w_hbm, w_s, w_sem).wait()
            recv_att(0, first_heads, 0)
            for columns, value in mix(0, first_heads):
                mixed_s[:, columns] = value

        @pl.when(i == mix_at + mix_gap)
        def _():
            recv_att(first_heads, early_heads, 1)
            for columns, value in mix(first_heads, early_heads):
                mixed_s[:, columns] += value

        @pl.when(jnp.logical_and(i < heads, jnp.logical_or(is_outer_row, i > 0)))
        def _():
            arrive(pal, i)
            pl.when(jnp.logical_and(is_cut_row, i < last))(lambda: cross(pal, i).start())

        @pl.when(is_cut_row)
        def _():
            @pl.when(i == 0)
            def _():
                for part in range(2):
                    arrive(pal, 0, part, FIRST_OWN)
                    cross(pal, 0, part, FIRST_CROSSED).start()
                arrive(side, 0)
                cross(side, 0).start()
                arrive(straight, last)
                up_down(straight, last).start()

            def pass_on(h):
                arrive(side, h)
                cross(side, h).start()

            def take(from_pal, h):
                if from_pal:
                    for part in range(2) if h == 0 else (None,):
                        arrive(swapped, h, part, FIRST_CROSSED)
                    up_down(swapped, h).start()
                else:
                    arrive(far, h)
                    if h < tail:
                        to_pal(far, h).start()

            at = 0
            for place, (from_pal, h) in enumerate(crossing_order(heads)):
                at = max(at, h)
                if not from_pal and h > 0:
                    pl.when(i == at)(lambda h=h: pass_on(h))
            for place, (from_pal, h) in enumerate(crossing_order(heads)):
                pl.when(i == place + 1)(lambda from_pal=from_pal, h=h: take(from_pal, h))

        @pl.when(is_outer_row)
        def _():
            @pl.when(i == 1)
            def _():
                arrive(straight, last)
                to_pal(straight, last).start()

            def relay(j):
                arrive(swapped, j)
                to_pal(swapped, j).start()

            for place, (from_pal, h) in enumerate(crossing_order(heads)):
                if from_pal:
                    at = place + (3 if h < heads - 3 else 2)
                    pl.when(i == at)(lambda h=h: relay(h))

        nearby = i - heads

        @pl.when(jnp.logical_and(is_near, jnp.logical_and(nearby >= heads - NEAR, nearby < heads)))
        def _():
            send_q(nearby).wait_recv()
            share(nearby, guest_q[nearby], (2, 6), share_out.at[nearby], stat_out.at[nearby])
            for copy in send_share(nearby):
                copy.start()

        @pl.when(jnp.logical_and(is_cut_row, jnp.logical_and(nearby >= tail, nearby < heads)))
        def _():
            index = nearby - tail
            send_pal(q_s.at[nearby], pal_q.at[index], 0, index).wait_recv()
            share(nearby, pal_q[index], (far,), pal_share_out.at[index], pal_stat_out.at[index])
            for copy in send_pal_share(index):
                copy.start()

        @pl.when(jnp.logical_and(i >= 1, i <= heads))
        def _():
            for which in range(2):
                load_w(i - 1, which).start()

        @pl.when(i < heads)
        def _():
            hold(i, *attend(q_s[i], (row_base, row_base + 1), i))

        @pl.when(jnp.logical_and(i < heads, role == 0))
        def _():
            lend_q(i).wait_recv()
            share(i, share_in[i], (1,), share_out.at[i], stat_out.at[i])
            for copy in send_share(i, up_down_device):
                copy.start()

        @pl.when(jnp.logical_and(ready(i - last), is_near))
        def _():
            h = i - last
            for copy in send_share(h):
                copy.wait_recv()
            hold(h, *merge(h, share_in.at[h], stat_in.at[h]))

        @pl.when(jnp.logical_and(role == 0, i == 2))
        def _():
            for h in range(heads - NEAR, heads):
                send_q(h).wait_recv()
                send_q(h, source=guest_q).start()

        @pl.when(is_outer_row)
        def _():
            h = jnp.where(i == heads, last, i - heads - 1)

            @pl.when(jnp.logical_and(i >= heads, i < 2 * heads))
            def _():
                arrive(jnp.where(h == last, swapped, straight), h)
                pl.when(jnp.logical_and(role == 0, h == last))(lambda: up_down(swapped, h, way=3).start())
                state = attend_more((4, 5), h)
                pl.when(role == 0)(lambda: finish(h, *state))
                pl.when(is_corner)(lambda: hold(h, *state))

            ending = i - heads - 2

            @pl.when(jnp.logical_and(ready(ending), is_corner))
            def _():
                for copy in send_share(ending):
                    copy.wait_recv()
                finish(ending, *merge(ending, share_in.at[ending], stat_in.at[ending]))

        ending = i - heads - 1

        is_whole = jnp.logical_and(ending >= 0, ending < tail)
        is_tail = jnp.logical_and(ending >= tail, ending < heads)

        @pl.when(jnp.logical_and(is_whole, is_near))
        def _():
            arrive(7, ending)
            finish(ending, *attend_more((5, 6, 7), ending))

        @pl.when(jnp.logical_and(is_whole, is_host))
        def _():
            send_q(ending).wait_recv()
            arrive(6, ending)
            share(ending, guest_q[ending], (2, 6), share_out.at[ending], stat_out.at[ending])
            for copy in send_share(ending):
                copy.start()
            finish(ending, *attend_more((6, 7), ending))

        @pl.when(jnp.logical_and(is_tail, is_near))
        def _():
            pl.when(ending == last)(lambda: arrive(5, ending))
            hold(ending, *attend_more((5, 6), ending))

        @pl.when(jnp.logical_and(is_tail, is_host))
        def _():
            hold(ending, *attend_more((7,), ending))

        @pl.when(jnp.logical_and(is_cut_row, is_tail))
        def _():
            index = ending - tail
            for copy in send_pal_share(index):
                copy.wait_recv()
            finish(ending, *merge(ending, pal_share_in.at[index], pal_stat_in.at[index]))

    pl.when(is_corner)(lambda: send_att(last).start())
    recv_att(early_heads, heads, 2)
    for columns, value in mix(early_heads, heads):
        out_ref[:, columns] = (mixed_s[:, columns] + value).astype(out_ref.dtype)

    def drain(way, count):
        tiles_sent = kv.at[pl.ds(0, count)]
        pltpu.make_async_remote_copy(
            src_ref=tiles_sent,
            dst_ref=tiles_sent,
            send_sem=send_sem.at[way],
            recv_sem=recv_sem.at[0, 0],
            device_id={"tm": pal_device},
            device_id_type=MESH,
        ).wait_send()

    def drain_rows(sent, sem):
        pltpu.make_async_remote_copy(
            src_ref=sent,
            dst_ref=sent,
            send_sem=sem,
            recv_sem=recv_sem.at[0, 0],
            device_id={"tm": pal_device},
            device_id_type=MESH,
        ).wait_send()

    pl.when(is_outer_row)(lambda: drain(0, 2))

    @pl.when(is_cut_row)
    def _():
        drain_rows(kv.at[pl.ds(0, 2), pl.ds(0, heads - NEAR // 2)], send_sem.at[0])
        drain_rows(pal_q, pal_send_sem.at[0])
        drain_rows(pal_share_out, pal_send_sem.at[1])
        drain_rows(pal_stat_out, pal_send_sem.at[2])

    drain(1, 1)
    drain_rows(other_s, att_send_sem)
    pl.when(role == 0)(lambda: drain_rows(kv.at[0, 0], send_sem.at[3]))
    pl.when(role == 0)(lambda: drain_rows(guest_q.at[pl.ds(0, NEAR)], q_send_sem))
    pl.when(jnp.logical_or(is_corner, is_near))(lambda: drain_rows(q_s, q_send_sem))
    pl.when(is_cut_row)(lambda: drain(2, 2))
    for count, sender in ((heads, role == 0), (heads - NEAR, is_host), (NEAR, is_near)):
        pl.when(sender)(lambda count=count: drain_rows(share_out.at[pl.ds(0, count)], share_send_sem.at[0]))
        pl.when(sender)(lambda count=count: drain_rows(stat_out.at[pl.ds(0, count)], share_send_sem.at[1]))


def balanced_call(query_states, key_states, value_states, out_weight):
    rows, half_width = query_states.shape[1:]
    heads = half_width // HD
    depth, width = out_weight.shape
    tiles = lax.axis_size("tm") // 2
    dma = pltpu.SemaphoreType.DMA
    return pl.pallas_call(
        functools.partial(balanced_kernel, tiles),
        out_shape=jax.ShapeDtypeStruct((rows // 2, width), jnp.bfloat16),
        in_specs=[pl.BlockSpec(memory_space=pl.ANY)] * 4,
        out_specs=pl.BlockSpec(memory_space=pltpu.VMEM),
        scratch_shapes=[
            pltpu.VMEM((heads, rows, HD), jnp.bfloat16),
            pltpu.VMEM((heads, rows, HD), jnp.bfloat16),
            pltpu.VMEM((tiles, heads, 2, rows, HD), jnp.bfloat16),
            pltpu.VMEM((depth, width), jnp.bfloat16),
            pltpu.VMEM((heads, rows, HD), jnp.float32),
            pltpu.VMEM((heads, rows, HD), jnp.float32),
            pltpu.VMEM((heads, rows, HD), jnp.float32),
            pltpu.VMEM((rows // 2, width), jnp.float32),
            pltpu.VMEM((heads, rows, HD), jnp.bfloat16),
            pltpu.VMEM((heads, rows // 2, HD), jnp.bfloat16),
            pltpu.VMEM((heads, rows, HD), jnp.bfloat16),
            pltpu.VMEM((heads, rows, HD), jnp.bfloat16),
            pltpu.VMEM((heads, 8, rows), jnp.float32),
            pltpu.VMEM((heads, 8, rows), jnp.float32),
            pltpu.VMEM((NEAR, rows, HD), jnp.bfloat16),
            pltpu.VMEM((NEAR, rows, HD), jnp.bfloat16),
            pltpu.VMEM((NEAR, rows, HD), jnp.bfloat16),
            pltpu.VMEM((NEAR, 8, rows), jnp.float32),
            pltpu.VMEM((NEAR, 8, rows), jnp.float32),
            dma((heads,)),
            dma,
            dma,
            dma((4,)),
            dma((tiles, heads)),
            dma,
            dma((heads,)),
            dma((2,)),
            dma((2, heads)),
            dma((3,)),
            dma((3, NEAR)),
            dma,
            dma((3,)),
        ],
        compiler_params=pltpu.CompilerParams(
            collective_id=0, has_side_effects=True, vmem_limit_bytes=40 * 1024 * 1024
        ),
    )(*(pltpu.with_memory_space_constraint(x, pltpu.HBM) for x in (query_states, key_states, value_states, out_weight)))


def general_call(query_states, key_states, value_states, out_weight):
    rows, half_width = query_states.shape[1:]
    heads = half_width // HD
    depth, width = out_weight.shape
    time_count = lax.axis_size("tm") // (2 * TCOLS)
    return pl.pallas_call(
        functools.partial(general_kernel, time_count, heads),
        out_shape=jax.ShapeDtypeStruct((rows // 2, width), jnp.bfloat16),
        in_specs=[pl.BlockSpec(memory_space=pl.ANY)] * 4,
        out_specs=pl.BlockSpec(memory_space=pltpu.VMEM),
        scratch_shapes=[
            pltpu.VMEM((heads, rows, HD), jnp.bfloat16),
            pltpu.VMEM((11, heads, 2, rows, HD), jnp.bfloat16),
            pltpu.VMEM((depth, width), jnp.bfloat16),
            pltpu.VMEM((heads, rows, HD), jnp.float32),
            pltpu.VMEM((heads, rows, HD), jnp.float32),
            pltpu.VMEM((heads, rows, HD), jnp.float32),
            pltpu.VMEM((heads, rows // 2, HD), jnp.bfloat16),
            pltpu.VMEM((2, heads, rows // 2, HD), jnp.bfloat16),
            pltpu.SemaphoreType.DMA((3, heads)),
            pltpu.SemaphoreType.DMA,
            pltpu.SemaphoreType.DMA((13, heads)),
            pltpu.SemaphoreType.DMA((11, heads)),
            pltpu.SemaphoreType.DMA((heads,)),
            pltpu.SemaphoreType.DMA((heads,)),
        ],
        compiler_params=pltpu.CompilerParams(
            collective_id=0, has_side_effects=True, vmem_limit_bytes=56 * 1024 * 1024
        ),
    )(query_states, key_states, value_states, out_weight)


def per_device(query_states, key_states, value_states, out_weight):
    two_times = lax.axis_size("tm") == 4 * TCOLS and query_states.shape[2] >= 5 * HD
    call = balanced_call if two_times else general_call
    return call(query_states, key_states, value_states, out_weight)


def solution(mesh):
    in_specs = (
        P(("parts", "tm"), None, None),
        P(("parts", "tm"), None, None),
        P(("parts", "tm"), None, None),
        P(),
    )
    out_specs = P(("parts", "tm"), None)
    return jax.shard_map(
        per_device, mesh=mesh, in_specs=in_specs, out_specs=out_specs, check_vma=False
    )
```

```python
import functools

import jax
import jax.numpy as jnp
from jax import lax
from jax.experimental import pallas as pl
from jax.experimental.pallas import tpu as pltpu
from jax.sharding import PartitionSpec as P

TCOLS = 4
HD = 128
MESH = pl.DeviceIdType.MESH
LOG2E = 1.4426950408889634

DIRECT_OWN = 2
DIRECT_CORNER = 1
AHEAD = 2
LAG_TIME = 2
LAG_CORNER = 3
LAG_MIDDLE = 5

NEAR = 2
OUT_CHUNK = 512
FIRST_OWN, FIRST_CROSSED = range(2)


def slot_of(time_step, col_step):
    return (time_step + 1) * 3 + col_step + 1


def general_kernel(
    time_count,
    heads,
    q_hbm,
    k_hbm,
    v_hbm,
    w_hbm,
    out_ref,
    q_s,
    kv,
    w_s,
    m_s,
    l_s,
    acc_s,
    outgoing,
    attended,
    load_sem,
    w_sem,
    send_sem,
    recv_sem,
    att_send_sem,
    att_recv_sem,
):
    rows = q_s.shape[1]
    half = rows // 2
    me = lax.axis_index("tm")
    group = lax.rem(me, 2)
    tile = lax.div(me, 2)
    col = lax.rem(tile, TCOLS)
    time = lax.div(tile, TCOLS)
    has_time = {-1: time > 0, 1: time < time_count - 1}
    has_col = {-1: col > 0, 1: col < TCOLS - 1}
    outer = 1 - 2 * lax.rem(col, 2)
    is_edge = jnp.logical_or(col == 0, col == TCOLS - 1)
    is_middle = jnp.logical_not(is_edge)
    outer_device = me + 2 * outer
    middle_device = me - 2 * outer
    relay_device = me + 4 * outer
    other_core = me + 1 - 2 * group
    own_slot = slot_of(0, 0)
    stride = TCOLS
    has_hop = {-1: tile >= stride // 2, 1: tile + stride // 2 < time_count * TCOLS}
    is_hop = jnp.logical_and(has_hop[-1], has_hop[1])

    def hop_slot(step):
        return 9 if step < 0 else 10

    def load(h):
        columns = pl.ds(pl.multiple_of(h * HD, HD), HD)
        return (
            pltpu.make_async_copy(k_hbm.at[0, :, columns], kv.at[own_slot, h, 0], load_sem.at[0, h]),
            pltpu.make_async_copy(v_hbm.at[0, :, columns], kv.at[own_slot, h, 1], load_sem.at[1, h]),
            pltpu.make_async_copy(q_hbm.at[0, :, columns], q_s.at[h], load_sem.at[2, h]),
        )

    for h in range(heads):
        for copy in load(jnp.int32(h)):
            copy.start()
    w_copy = pltpu.make_async_copy(w_hbm, w_s, w_sem)
    w_copy.start()

    barrier = pltpu.get_barrier_semaphore()

    def greet(device):
        pl.semaphore_signal(barrier, inc=1, device_id={"tm": device}, device_id_type=MESH)

    greetings = jnp.int32(2)
    greet(other_core)
    greet(outer_device)
    for step in (-1, 1):
        pl.when(has_hop[step])(lambda step=step: greet(me + stride * step))
        greetings = greetings + has_hop[step].astype(jnp.int32)
    pl.when(is_middle)(lambda: greet(middle_device))
    greetings = greetings + is_middle.astype(jnp.int32)
    pl.semaphore_wait(barrier, greetings)

    def transfer(kind, h, source, target, device):
        return pltpu.make_async_remote_copy(
            src_ref=kv.at[source, h],
            dst_ref=kv.at[target, h],
            send_sem=send_sem.at[kind, h],
            recv_sem=recv_sem.at[target, h],
            device_id={"tm": device},
            device_id_type=MESH,
        )

    def arrive(slot, h):
        transfer(0, h, slot, slot, other_core).wait_recv()

    def send_time(step, h):
        return transfer(0 if step < 0 else 1, h, own_slot, hop_slot(step), me + stride * step)

    def send_hop(step, h):
        return transfer(11 if step < 0 else 12, h, hop_slot(step), slot_of(-step, 0), me + stride * step)

    def send_outer(step, h):
        return transfer(3 + step, h, slot_of(step, 0), slot_of(step, 0) - outer, outer_device)

    def send_middle(step, h):
        return transfer(6 + step, h, slot_of(step, 0), slot_of(step, 0) + outer, middle_device)

    def send_relay(step, h):
        return transfer(9 + step, h, slot_of(step, 0) + outer, slot_of(step, 0) - outer, relay_device)

    def straight(step, h):
        return h >= heads - (DIRECT_OWN if step == 0 else DIRECT_CORNER)

    def send_att(h):
        return pltpu.make_async_remote_copy(
            src_ref=outgoing.at[h],
            dst_ref=attended.at[group, h],
            send_sem=att_send_sem.at[h],
            recv_sem=att_recv_sem.at[h],
            device_id={"tm": other_core},
            device_id_type=MESH,
        )

    def recv_att(h):
        return pltpu.make_async_remote_copy(
            src_ref=outgoing.at[h],
            dst_ref=attended.at[1 - group, h],
            send_sem=att_send_sem.at[h],
            recv_sem=att_recv_sem.at[h],
            device_id={"tm": other_core},
            device_id_type=MESH,
        )

    def send_own(h):
        for copy in load(h):
            copy.wait()
        for step in (-1, 1):
            pl.when(has_time[step])(lambda step=step: send_time(step, h).start())
        send_outer(0, h).start()
        if DIRECT_OWN:
            pl.when(jnp.logical_and(is_middle, straight(0, h)))(lambda: send_middle(0, h).start())

    for h in range(AHEAD):
        send_own(jnp.int32(h))

    exponent_scale = (HD ** (-0.5)) * LOG2E

    def attend(slot, h, first=False):
        scores = lax.dot_general(
            q_s[h], kv[slot, h, 0], (((1,), (1,)), ((), ())), preferred_element_type=jnp.float32
        )
        row_max = jnp.max(scores, axis=1, keepdims=True)
        if not first:
            old_max = m_s[h][:, :1]
            row_max = jnp.maximum(row_max, old_max)
        weights = jnp.exp2((scores - row_max) * exponent_scale)
        total = jnp.sum(weights, axis=1, keepdims=True)
        result = jnp.dot(weights.astype(jnp.bfloat16), kv[slot, h, 1], preferred_element_type=jnp.float32)
        if not first:
            keep = jnp.exp2((old_max - row_max) * exponent_scale)
            total = total + keep * l_s[h][:, :1]
            result = result + keep * acc_s[h]
        m_s[h] = jnp.broadcast_to(row_max, (rows, HD))
        l_s[h] = jnp.broadcast_to(total, (rows, HD))
        acc_s[h] = result

    def finish(h):
        acc_s[h] = acc_s[h] / l_s[h]
        attended[group, h] = acc_s[h, pl.ds(pl.multiple_of(group * half, 16), half), :].astype(jnp.bfloat16)
        outgoing[h] = acc_s[h, pl.ds(pl.multiple_of((1 - group) * half, 16), half), :].astype(jnp.bfloat16)

    def ready(h):
        return jnp.logical_and(h >= 0, h < heads)

    @pl.loop(0, heads + LAG_MIDDLE)
    def _(i):
        pl.when(i + AHEAD < heads)(lambda: send_own(i + AHEAD))

        @pl.when(jnp.logical_and(i < heads, is_edge))
        def _():
            arrive(own_slot + outer, i)
            pl.when(jnp.logical_not(straight(0, i)))(lambda: send_relay(0, i).start())

        @pl.when(jnp.logical_and(i < heads, is_hop))
        def _():
            for step in (-1, 1):
                arrive(hop_slot(step), i)
                send_hop(step, i).start()

        crossed = i - LAG_TIME

        @pl.when(ready(crossed))
        def _():
            for step in (-1, 1):

                @pl.when(has_time[step])
                def _():
                    arrive(slot_of(step, 0), crossed)
                    send_outer(step, crossed).start()
                    if DIRECT_CORNER:
                        pl.when(jnp.logical_and(is_middle, straight(step, crossed)))(
                            lambda: send_middle(step, crossed).start()
                        )

        back = i - LAG_CORNER

        @pl.when(jnp.logical_and(ready(back), is_edge))
        def _():
            for step in (-1, 1):

                @pl.when(has_time[step])
                def _():
                    arrive(slot_of(step, 0) + outer, back)
                    pl.when(jnp.logical_not(straight(step, back)))(lambda: send_relay(step, back).start())

        pl.when(i < heads)(lambda: attend(own_slot, i, first=True))

        @pl.when(ready(crossed))
        def _():
            for step in (-1, 1):
                pl.when(has_time[step])(lambda: attend(slot_of(step, 0), crossed))

        @pl.when(ready(back))
        def _():
            pl.when(is_middle)(lambda: arrive(own_slot + outer, back))
            attend(own_slot + outer, back)
            for step in (-1, 1):

                @pl.when(has_time[step])
                def _():
                    pl.when(is_middle)(lambda: arrive(slot_of(step, 0) + outer, back))
                    attend(slot_of(step, 0) + outer, back)

        last = i - LAG_MIDDLE

        @pl.when(last >= 1)
        def _():
            send_att(last - 1).start()

        @pl.when(last >= 0)
        def _():
            @pl.when(is_middle)
            def _():
                arrive(own_slot - outer, last)
                attend(own_slot - outer, last)
                for step in (-1, 1):

                    @pl.when(has_time[step])
                    def _():
                        arrive(slot_of(step, 0) - outer, last)
                        attend(slot_of(step, 0) - outer, last)

            finish(last)

    send_att(heads - 1).start()
    w_copy.wait()

    for h in range(heads):
        recv_att(h).wait_recv()

    width = out_ref.shape[1]
    chunk = 512
    lhs = jnp.concatenate([attended[part, h] for part in range(2) for h in range(heads)], axis=1)

    @pl.loop(0, width // chunk, unroll=True)
    def _(n):
        columns = pl.ds(pl.multiple_of(n * chunk, chunk), chunk)
        out_ref[:, columns] = jnp.dot(lhs, w_s[:, columns], preferred_element_type=jnp.float32).astype(
            out_ref.dtype
        )

    @pl.loop(0, heads)
    def _(h):
        send_att(h).wait_send()
        send_outer(0, h).wait_send()

        @pl.when(is_hop)
        def _():
            for step in (-1, 1):
                send_hop(step, h).wait_send()

        if DIRECT_OWN:
            pl.when(jnp.logical_and(is_middle, straight(0, h)))(lambda: send_middle(0, h).wait_send())
        pl.when(jnp.logical_and(is_edge, jnp.logical_not(straight(0, h))))(
            lambda: send_relay(0, h).wait_send()
        )
        for step in (-1, 1):

            @pl.when(has_time[step])
            def _():
                send_time(step, h).wait_send()
                send_outer(step, h).wait_send()
                if DIRECT_CORNER:
                    pl.when(jnp.logical_and(is_middle, straight(step, h)))(
                        lambda: send_middle(step, h).wait_send()
                    )
                pl.when(jnp.logical_and(is_edge, jnp.logical_not(straight(step, h))))(
                    lambda: send_relay(step, h).wait_send()
                )


def crossing_order(heads):
    order = [(from_pal, h) for h in range(heads - 4) for from_pal in (True, False)]
    order += [(True, heads - 4), (True, heads - 3), (False, heads - 4), (True, heads - 2)]
    return order + [(False, h) for h in range(heads - 3, heads)]


def balanced_kernel(
    tiles,
    q_hbm,
    k_hbm,
    v_hbm,
    w_hbm,
    out_ref,
    q_s,
    guest_q,
    kv,
    w_s,
    m_s,
    l_s,
    acc_s,
    mixed_s,
    done_s,
    other_s,
    share_out,
    share_in,
    stat_out,
    stat_in,
    pal_q,
    pal_share_out,
    pal_share_in,
    pal_stat_out,
    pal_stat_in,
    load_sem,
    q_sem,
    w_sem,
    send_sem,
    recv_sem,
    q_send_sem,
    q_recv_sem,
    share_send_sem,
    share_recv_sem,
    pal_send_sem,
    pal_recv_sem,
    att_send_sem,
    att_recv_sem,
):
    heads, rows = q_s.shape[:2]
    half = rows // 2
    last = heads - 1
    early_heads = heads - 3
    first_heads = heads - 4
    tail = heads - NEAR
    me = lax.axis_index("tm")
    group = lax.rem(me, 2)
    tile = lax.div(me, 2)
    lower = tile < tiles // 2
    role = jnp.where(lower, tile, tiles - 1 - tile)
    side = lax.rem(role, 2)
    is_cut_row = role >= 2
    is_outer_row = jnp.logical_not(is_cut_row)
    is_corner = role == 1
    is_near = role == 2
    is_host = role == 3
    pal = role + 1 - 2 * side
    row_base = role - side
    swapped = 5 - side
    straight = 4 + side
    far = 6 + side
    pal_far = 7 - side
    other_core = me + 1 - 2 * group

    def device_of(slot):
        return 2 * jnp.where(lower, slot, tiles - 1 - slot) + group

    pal_device = device_of(pal)
    up_down_device = device_of(jnp.where(is_cut_row, role - 2, role + 2))
    cut_device = device_of(role + 2)
    corner_device = device_of(1)

    def load(h):
        columns = pl.ds(pl.multiple_of(h * HD, HD), HD)
        return (
            pltpu.make_async_copy(k_hbm.at[0, :, columns], kv.at[role, h, 0], load_sem.at[h]),
            pltpu.make_async_copy(v_hbm.at[0, :, columns], kv.at[role, h, 1], load_sem.at[h]),
            pltpu.make_async_copy(q_hbm.at[0, :, columns], q_s.at[h], q_sem),
        )

    def load_w(h, which):
        owner = group if which == 0 else 1 - group
        source = pl.ds(pl.multiple_of((owner * heads + h) * HD, HD), HD)
        target = pl.ds(pl.multiple_of((which * heads + h) * HD, HD), HD)
        return pltpu.make_async_copy(w_hbm.at[source], w_s.at[target], w_sem)

    barrier = pltpu.get_barrier_semaphore()

    def greet(device):
        pl.semaphore_signal(barrier, inc=1, device_id={"tm": device}, device_id_type=MESH)

    greet(other_core)
    greet(pal_device)
    greet(up_down_device)
    pl.when(is_cut_row)(lambda: greet(cut_device))
    pl.when(is_corner)(lambda: greet(device_of(2)))
    for h in (last, *range(last)):
        for copy in load(jnp.int32(h)):
            copy.start()
    pl.semaphore_wait(barrier, 3 + is_cut_row.astype(jnp.int32) + is_near.astype(jnp.int32))

    def transfer(way, slot, h, target, device, part=None, kind=0, landing=0):
        return pltpu.make_async_remote_copy(
            src_ref=kv.at[slot, h] if part is None else kv.at[slot, h, part],
            dst_ref=kv.at[target, h] if part is None else kv.at[target, h, part],
            send_sem=send_sem.at[way],
            recv_sem=recv_sem.at[landing, kind] if part == 1 else recv_sem.at[target, h],
            device_id={"tm": device},
            device_id_type=MESH,
        )

    def arrive(slot, h, part=None, kind=0):
        transfer(0, slot, h, slot, pal_device, part, kind, role).wait_recv()

    def to_pal(slot, h, part=None, kind=0, way=0):
        return transfer(way, slot, h, slot, pal_device, part, kind, pal)

    def up_down(slot, h, way=1):
        return transfer(way, slot, h, slot, up_down_device)

    def cross(slot, h, part=None, kind=0):
        return transfer(2, slot, h, tiles - 1 - slot, cut_device, part, kind, pal)

    def split_or_whole(is_split, act):
        pl.when(jnp.logical_not(is_split))(lambda: act(None))

        @pl.when(is_split)
        def _():
            for part in range(2):
                act(part)

    def send_q(h, source=q_s, device=up_down_device):
        return pltpu.make_async_remote_copy(
            src_ref=source.at[h],
            dst_ref=guest_q.at[h],
            send_sem=q_send_sem,
            recv_sem=q_recv_sem.at[h],
            device_id={"tm": device},
            device_id_type=MESH,
        )

    def lend_q(h):
        return pltpu.make_async_remote_copy(
            src_ref=q_s.at[h],
            dst_ref=share_in.at[h],
            send_sem=q_send_sem,
            recv_sem=share_recv_sem.at[0, h],
            device_id={"tm": up_down_device},
            device_id_type=MESH,
        )

    def send_share(h, device=corner_device):
        return tuple(
            pltpu.make_async_remote_copy(
                src_ref=source.at[h],
                dst_ref=target.at[h],
                send_sem=share_send_sem.at[which],
                recv_sem=share_recv_sem.at[which, h],
                device_id={"tm": device},
                device_id_type=MESH,
            )
            for which, (source, target) in enumerate(((share_out, share_in), (stat_out, stat_in)))
        )

    def send_pal(source, target, which, index):
        return pltpu.make_async_remote_copy(
            src_ref=source,
            dst_ref=target,
            send_sem=pal_send_sem.at[which],
            recv_sem=pal_recv_sem.at[which, index],
            device_id={"tm": pal_device},
            device_id_type=MESH,
        )

    def send_pal_share(index):
        return (
            send_pal(pal_share_out.at[index], pal_share_in.at[index], 1, index),
            send_pal(pal_stat_out.at[index], pal_stat_in.at[index], 2, index),
        )

    own_half = pl.ds(pl.multiple_of(group * half, 16), half)
    their_half = pl.ds(pl.multiple_of((1 - group) * half, 16), half)

    def send_att(h):
        return pltpu.make_async_remote_copy(
            src_ref=done_s.at[h, their_half],
            dst_ref=other_s.at[h],
            send_sem=att_send_sem,
            recv_sem=att_recv_sem.at[jnp.where(h < first_heads, 0, jnp.where(h < early_heads, 1, 2))],
            device_id={"tm": other_core},
            device_id_type=MESH,
        )

    def recv_att(first, stop, which):
        rows_in = other_s.at[pl.ds(first, stop - first)]
        pltpu.make_async_copy(rows_in, rows_in, att_recv_sem.at[which]).wait()

    def send_own(h):
        if h == 0:
            split_or_whole(is_cut_row, lambda part: to_pal(role, 0, part, FIRST_OWN).start())
        else:
            to_pal(role, h).start()
        pl.when(is_outer_row)(lambda: up_down(role, h).start())

    for h in (last, *range(last)):
        pltpu.make_async_copy(kv.at[role, h], kv.at[role, h], load_sem.at[h]).wait()
        if h == last:
            pl.when(is_cut_row)(lambda: cross(role, last).start())
        else:
            send_own(h)
        if h == 1:
            pltpu.make_async_copy(q_s, q_s, q_sem).wait()

            @pl.when(is_corner)
            def _():
                send_q(last, device=pal_device).start()
    send_own(last)

    @pl.when(is_corner)
    def _():
        for h in (*range(tail, last), *range(tail)):
            send_q(h).start()

    @pl.when(is_near)
    def _():
        for h in range(heads):
            lend_q(h).start()

    @pl.when(is_cut_row)
    def _():
        for h in range(tail, heads):
            send_pal(q_s.at[h], pal_q.at[h - tail], 0, h - tail).start()

    exponent_scale = (HD ** (-0.5)) * LOG2E

    def attend(queries, slots, h, old_max=None):
        scores = [
            lax.dot_general(queries, kv[slot, h, 0], (((1,), (1,)), ((), ())), preferred_element_type=jnp.float32)
            for slot in slots
        ]
        row_max = functools.reduce(jnp.maximum, [jnp.max(s, axis=1, keepdims=True) for s in scores])
        if old_max is not None:
            row_max = jnp.maximum(row_max, old_max)
        weights = [jnp.exp2((s - row_max) * exponent_scale) for s in scores]
        total = sum(jnp.sum(w, axis=1, keepdims=True) for w in weights)
        result = sum(
            jnp.dot(w.astype(jnp.bfloat16), kv[slot, h, 1], preferred_element_type=jnp.float32)
            for w, slot in zip(weights, slots)
        )
        return row_max, total, result

    def attend_more(slots, h):
        old_max = m_s[h][:, :1]
        row_max, total, result = attend(q_s[h], slots, h, old_max)
        keep = jnp.exp2((old_max - row_max) * exponent_scale)
        return row_max, total + keep * l_s[h][:, :1], result + keep * acc_s[h]

    def hold(h, row_max, total, result):
        m_s[h] = jnp.broadcast_to(row_max, (rows, HD))
        l_s[h] = jnp.broadcast_to(total, (rows, HD))
        acc_s[h] = result

    def finish(h, row_max, total, result):
        done_s[h] = (result / total).astype(jnp.bfloat16)

    def share(h, queries, slots, share_to, stat_to):
        row_max, total, result = attend(queries, slots, h)
        share_to[...] = (result / total).astype(jnp.bfloat16)
        lane = lax.broadcasted_iota(jnp.int32, (rows, HD), 1)
        stats = jnp.where(lax.rem(lane, 8) < 4, row_max, total)
        stat_to[...] = jnp.transpose(stats)[:8]

    def merge(h, shared, stats):
        row_max, total, result = m_s[h], l_s[h], acc_s[h]
        their_max = jnp.transpose(jnp.broadcast_to(stats[0:1, :], (HD, rows)))
        their_total = jnp.transpose(jnp.broadcast_to(stats[4:5, :], (HD, rows)))
        top = jnp.maximum(row_max, their_max)
        keep = jnp.exp2((row_max - top) * exponent_scale)
        weight = their_total * jnp.exp2((their_max - top) * exponent_scale)
        return top, keep * total + weight, keep * result + weight * shared[...].astype(jnp.float32)

    width = out_ref.shape[1]
    chunk = OUT_CHUNK

    def half_mix(which, first, stop):
        lhs = jnp.concatenate(
            [other_s[h] if which else done_s[h, own_half, :] for h in range(first, stop)], axis=1
        )
        depth = slice((which * heads + first) * HD, (which * heads + stop) * HD)

        def product(n):
            columns = pl.ds(n * chunk, chunk)
            return columns, jnp.dot(lhs, w_s[depth, columns], preferred_element_type=jnp.float32)

        return (product(n) for n in range(width // chunk))

    def mix(first, stop):
        for (columns, own), (_, other) in zip(half_mix(0, first, stop), half_mix(1, first, stop)):
            yield columns, own + other

    def ready(h):
        return jnp.logical_and(h >= 0, h < heads)

    is_slow = jnp.logical_and(is_cut_row, group == 0)
    mix_at = 2 * heads - jnp.where(is_slow, 3, jnp.where(is_cut_row, 0, 1))
    mix_gap = is_slow.astype(jnp.int32)

    @pl.loop(0, 2 * heads + 2)
    def _(i):
        settled = jnp.where(
            jnp.logical_and(role == 0, i == heads + 1), last, i - heads - jnp.where(is_corner, 3, 2)
        )
        settles = jnp.logical_and(ready(settled), jnp.logical_or(role != 0, i <= 2 * heads))
        held = jnp.logical_and(is_near, settled == tail - 1)
        pl.when(jnp.logical_and(settles, jnp.logical_not(held)))(lambda: send_att(settled).start())
        pl.when(jnp.logical_and(is_near, i == 2 * heads))(lambda: send_att(tail - 1).start())

        @pl.when(i == mix_at)
        def _():
            pltpu.make_async_copy(w_hbm, w_s, w_sem).wait()
            recv_att(0, first_heads, 0)
            for columns, value in mix(0, first_heads):
                mixed_s[:, columns] = value

        @pl.when(i == mix_at + mix_gap)
        def _():
            recv_att(first_heads, early_heads, 1)
            for columns, value in mix(first_heads, early_heads):
                mixed_s[:, columns] += value

        @pl.when(jnp.logical_and(i < heads, jnp.logical_or(is_outer_row, i > 0)))
        def _():
            arrive(pal, i)
            pl.when(jnp.logical_and(is_cut_row, i < last))(lambda: cross(pal, i).start())

        @pl.when(is_cut_row)
        def _():
            @pl.when(i == 0)
            def _():
                for part in range(2):
                    arrive(pal, 0, part, FIRST_OWN)
                    cross(pal, 0, part, FIRST_CROSSED).start()
                arrive(side, 0)
                cross(side, 0).start()
                arrive(straight, last)
                up_down(straight, last).start()

            def pass_on(h):
                arrive(side, h)
                cross(side, h).start()

            def take(from_pal, h):
                if from_pal:
                    for part in range(2) if h == 0 else (None,):
                        arrive(swapped, h, part, FIRST_CROSSED)
                    up_down(swapped, h).start()
                else:
                    arrive(far, h)
                    if h < tail:
                        to_pal(far, h, way=3).start()

            at = 0
            for place, (from_pal, h) in enumerate(crossing_order(heads)):
                at = max(at, h)
                if not from_pal and h > 0:
                    pl.when(i == at)(lambda h=h: pass_on(h))
            for place, (from_pal, h) in enumerate(crossing_order(heads)):
                pl.when(i == place + 1)(lambda from_pal=from_pal, h=h: take(from_pal, h))

        @pl.when(is_outer_row)
        def _():
            @pl.when(i == 1)
            def _():
                arrive(straight, last)
                to_pal(straight, last).start()

            def relay(j):
                arrive(swapped, j)
                to_pal(swapped, j).start()

            for place, (from_pal, h) in enumerate(crossing_order(heads)):
                if from_pal:
                    at = place + (3 if h < heads - 3 else 2)
                    pl.when(i == at)(lambda h=h: relay(h))

        nearby = i - heads

        @pl.when(jnp.logical_and(is_near, jnp.logical_and(nearby >= heads - NEAR, nearby < heads)))
        def _():
            send_q(nearby).wait_recv()
            share(nearby, guest_q[nearby], (2, 6), share_out.at[nearby], stat_out.at[nearby])
            for copy in send_share(nearby):
                copy.start()

        @pl.when(jnp.logical_and(is_cut_row, jnp.logical_and(nearby >= tail, nearby < heads)))
        def _():
            index = nearby - tail
            send_pal(q_s.at[nearby], pal_q.at[index], 0, index).wait_recv()
            share(nearby, pal_q[index], (far,), pal_share_out.at[index], pal_stat_out.at[index])
            for copy in send_pal_share(index):
                copy.start()

        @pl.when(jnp.logical_and(i >= 1, i <= heads))
        def _():
            for which in range(2):
                load_w(i - 1, which).start()

        @pl.when(i < heads)
        def _():
            hold(i, *attend(q_s[i], (row_base, row_base + 1), i))

        @pl.when(jnp.logical_and(i < heads, role == 0))
        def _():
            lend_q(i).wait_recv()
            share(i, share_in[i], (1,), share_out.at[i], stat_out.at[i])
            for copy in send_share(i, up_down_device):
                copy.start()

        @pl.when(jnp.logical_and(ready(i - last), is_near))
        def _():
            h = i - last
            for copy in send_share(h):
                copy.wait_recv()
            hold(h, *merge(h, share_in.at[h], stat_in.at[h]))

        @pl.when(jnp.logical_and(role == 0, i == 2))
        def _():
            send_q(last).wait_recv()
            send_q(last, source=guest_q).start()

        @pl.when(jnp.logical_and(is_host, i == heads))
        def _():
            for h in range(tail, last):
                send_q(h).wait_recv()
                send_q(h, source=guest_q, device=pal_device).start()

        @pl.when(is_outer_row)
        def _():
            ending = i - heads - 2

            @pl.when(jnp.logical_and(ready(ending), is_corner))
            def _():
                for copy in send_share(ending):
                    copy.wait_recv()
                finish(ending, *merge(ending, share_in.at[ending], stat_in.at[ending]))

            h = jnp.where(i == heads, last, i - heads - 1)

            @pl.when(jnp.logical_and(i >= heads, i < 2 * heads))
            def _():
                arrive(jnp.where(h == last, swapped, straight), h)
                pl.when(jnp.logical_and(role == 0, h == last))(lambda: up_down(swapped, h, way=3).start())
                state = attend_more((4, 5), h)
                pl.when(role == 0)(lambda: finish(h, *state))
                pl.when(is_corner)(lambda: hold(h, *state))

        ending = i - heads - 1

        is_whole = jnp.logical_and(ending >= 0, ending < tail)
        is_tail = jnp.logical_and(ending >= tail, ending < heads)

        waiting = jnp.where(i == 2 * heads - 1, tail - 1, ending)

        @pl.when(jnp.logical_and(jnp.logical_and(waiting >= 0, waiting < tail), jnp.logical_and(is_near, i != heads + tail)))
        def _():
            arrive(7, waiting)
            finish(waiting, *attend_more((5, 6, 7), waiting))

        @pl.when(jnp.logical_and(is_whole, is_host))
        def _():
            send_q(ending).wait_recv()
            arrive(6, ending)
            share(ending, guest_q[ending], (2, 6), share_out.at[ending], stat_out.at[ending])
            for copy in send_share(ending):
                copy.start()
            finish(ending, *attend_more((6, 7), ending))

        @pl.when(jnp.logical_and(is_tail, is_near))
        def _():
            pl.when(ending == last)(lambda: arrive(5, ending))
            hold(ending, *attend_more((5, 6), ending))

        @pl.when(jnp.logical_and(is_tail, is_host))
        def _():
            hold(ending, *attend_more((7,), ending))

        @pl.when(jnp.logical_and(is_cut_row, is_tail))
        def _():
            index = ending - tail
            for copy in send_pal_share(index):
                copy.wait_recv()
            finish(ending, *merge(ending, pal_share_in.at[index], pal_stat_in.at[index]))

    pl.when(is_corner)(lambda: send_att(last).start())
    for columns, value in half_mix(0, early_heads, heads):
        mixed_s[:, columns] += value
    recv_att(early_heads, heads, 2)
    for columns, value in half_mix(1, early_heads, heads):
        out_ref[:, columns] = (mixed_s[:, columns] + value).astype(out_ref.dtype)

    def drain(way, count):
        tiles_sent = kv.at[pl.ds(0, count)]
        pltpu.make_async_remote_copy(
            src_ref=tiles_sent,
            dst_ref=tiles_sent,
            send_sem=send_sem.at[way],
            recv_sem=recv_sem.at[0, 0],
            device_id={"tm": pal_device},
            device_id_type=MESH,
        ).wait_send()

    def drain_rows(sent, sem):
        pltpu.make_async_remote_copy(
            src_ref=sent,
            dst_ref=sent,
            send_sem=sem,
            recv_sem=recv_sem.at[0, 0],
            device_id={"tm": pal_device},
            device_id_type=MESH,
        ).wait_send()

    pl.when(is_outer_row)(lambda: drain(0, 2))

    @pl.when(is_cut_row)
    def _():
        drain(0, 1)
        drain_rows(kv.at[0, pl.ds(0, tail)], send_sem.at[3])
        drain_rows(pal_q, pal_send_sem.at[0])
        drain_rows(pal_share_out, pal_send_sem.at[1])
        drain_rows(pal_stat_out, pal_send_sem.at[2])

    drain(1, 1)
    drain_rows(other_s, att_send_sem)
    pl.when(role == 0)(lambda: drain_rows(kv.at[0, 0], send_sem.at[3]))
    pl.when(role == 0)(lambda: drain_rows(guest_q.at[0], q_send_sem))
    pl.when(is_host)(lambda: drain_rows(guest_q.at[pl.ds(0, NEAR - 1)], q_send_sem))
    pl.when(jnp.logical_or(is_corner, is_near))(lambda: drain_rows(q_s, q_send_sem))
    pl.when(is_cut_row)(lambda: drain(2, 2))
    for count, sender in ((heads, role == 0), (heads - NEAR, is_host), (NEAR, is_near)):
        pl.when(sender)(lambda count=count: drain_rows(share_out.at[pl.ds(0, count)], share_send_sem.at[0]))
        pl.when(sender)(lambda count=count: drain_rows(stat_out.at[pl.ds(0, count)], share_send_sem.at[1]))


def balanced_call(query_states, key_states, value_states, out_weight):
    rows, half_width = query_states.shape[1:]
    heads = half_width // HD
    depth, width = out_weight.shape
    tiles = lax.axis_size("tm") // 2
    dma = pltpu.SemaphoreType.DMA
    return pl.pallas_call(
        functools.partial(balanced_kernel, tiles),
        out_shape=jax.ShapeDtypeStruct((rows // 2, width), jnp.bfloat16),
        in_specs=[pl.BlockSpec(memory_space=pl.ANY)] * 4,
        out_specs=pl.BlockSpec(memory_space=pltpu.VMEM),
        scratch_shapes=[
            pltpu.VMEM((heads, rows, HD), jnp.bfloat16),
            pltpu.VMEM((heads, rows, HD), jnp.bfloat16),
            pltpu.VMEM((tiles, heads, 2, rows, HD), jnp.bfloat16),
            pltpu.VMEM((depth, width), jnp.bfloat16),
            pltpu.VMEM((heads, rows, HD), jnp.float32),
            pltpu.VMEM((heads, rows, HD), jnp.float32),
            pltpu.VMEM((heads, rows, HD), jnp.float32),
            pltpu.VMEM((rows // 2, width), jnp.float32),
            pltpu.VMEM((heads, rows, HD), jnp.bfloat16),
            pltpu.VMEM((heads, rows // 2, HD), jnp.bfloat16),
            pltpu.VMEM((heads, rows, HD), jnp.bfloat16),
            pltpu.VMEM((heads, rows, HD), jnp.bfloat16),
            pltpu.VMEM((heads, 8, rows), jnp.float32),
            pltpu.VMEM((heads, 8, rows), jnp.float32),
            pltpu.VMEM((NEAR, rows, HD), jnp.bfloat16),
            pltpu.VMEM((NEAR, rows, HD), jnp.bfloat16),
            pltpu.VMEM((NEAR, rows, HD), jnp.bfloat16),
            pltpu.VMEM((NEAR, 8, rows), jnp.float32),
            pltpu.VMEM((NEAR, 8, rows), jnp.float32),
            dma((heads,)),
            dma,
            dma,
            dma((4,)),
            dma((tiles, heads)),
            dma,
            dma((heads,)),
            dma((2,)),
            dma((2, heads)),
            dma((3,)),
            dma((3, NEAR)),
            dma,
            dma((3,)),
        ],
        compiler_params=pltpu.CompilerParams(
            collective_id=0, has_side_effects=True, vmem_limit_bytes=40 * 1024 * 1024
        ),
    )(*(pltpu.with_memory_space_constraint(x, pltpu.HBM) for x in (query_states, key_states, value_states, out_weight)))


def general_call(query_states, key_states, value_states, out_weight):
    rows, half_width = query_states.shape[1:]
    heads = half_width // HD
    depth, width = out_weight.shape
    time_count = lax.axis_size("tm") // (2 * TCOLS)
    return pl.pallas_call(
        functools.partial(general_kernel, time_count, heads),
        out_shape=jax.ShapeDtypeStruct((rows // 2, width), jnp.bfloat16),
        in_specs=[pl.BlockSpec(memory_space=pl.ANY)] * 4,
        out_specs=pl.BlockSpec(memory_space=pltpu.VMEM),
        scratch_shapes=[
            pltpu.VMEM((heads, rows, HD), jnp.bfloat16),
            pltpu.VMEM((11, heads, 2, rows, HD), jnp.bfloat16),
            pltpu.VMEM((depth, width), jnp.bfloat16),
            pltpu.VMEM((heads, rows, HD), jnp.float32),
            pltpu.VMEM((heads, rows, HD), jnp.float32),
            pltpu.VMEM((heads, rows, HD), jnp.float32),
            pltpu.VMEM((heads, rows // 2, HD), jnp.bfloat16),
            pltpu.VMEM((2, heads, rows // 2, HD), jnp.bfloat16),
            pltpu.SemaphoreType.DMA((3, heads)),
            pltpu.SemaphoreType.DMA,
            pltpu.SemaphoreType.DMA((13, heads)),
            pltpu.SemaphoreType.DMA((11, heads)),
            pltpu.SemaphoreType.DMA((heads,)),
            pltpu.SemaphoreType.DMA((heads,)),
        ],
        compiler_params=pltpu.CompilerParams(
            collective_id=0, has_side_effects=True, vmem_limit_bytes=56 * 1024 * 1024
        ),
    )(query_states, key_states, value_states, out_weight)


def per_device(query_states, key_states, value_states, out_weight):
    two_times = lax.axis_size("tm") == 4 * TCOLS and query_states.shape[2] >= 5 * HD
    call = balanced_call if two_times else general_call
    return call(query_states, key_states, value_states, out_weight)


def solution(mesh):
    in_specs = (
        P(("parts", "tm"), None, None),
        P(("parts", "tm"), None, None),
        P(("parts", "tm"), None, None),
        P(),
    )
    out_specs = P(("parts", "tm"), None)
    return jax.shard_map(
        per_device, mesh=mesh, in_specs=in_specs, out_specs=out_specs, check_vma=False
    )
```

```python
import functools

import jax
import jax.numpy as jnp
from jax import lax
from jax.experimental import pallas as pl
from jax.experimental.pallas import tpu as pltpu
from jax.sharding import PartitionSpec as P

TCOLS = 4
HD = 128
MESH = pl.DeviceIdType.MESH
LOG2E = 1.4426950408889634

DIRECT_OWN = 2
DIRECT_CORNER = 1
AHEAD = 2
LAG_TIME = 2
LAG_CORNER = 3
LAG_MIDDLE = 5

NEAR = 2
OUT_CHUNK = 512
FIRST_OWN, FIRST_CROSSED = range(2)


def slot_of(time_step, col_step):
    return (time_step + 1) * 3 + col_step + 1


def general_kernel(
    time_count,
    heads,
    q_hbm,
    k_hbm,
    v_hbm,
    w_hbm,
    out_ref,
    q_s,
    kv,
    w_s,
    m_s,
    l_s,
    acc_s,
    outgoing,
    attended,
    load_sem,
    w_sem,
    send_sem,
    recv_sem,
    att_send_sem,
    att_recv_sem,
):
    rows = q_s.shape[1]
    half = rows // 2
    me = lax.axis_index("tm")
    group = lax.rem(me, 2)
    tile = lax.div(me, 2)
    col = lax.rem(tile, TCOLS)
    time = lax.div(tile, TCOLS)
    has_time = {-1: time > 0, 1: time < time_count - 1}
    has_col = {-1: col > 0, 1: col < TCOLS - 1}
    outer = 1 - 2 * lax.rem(col, 2)
    is_edge = jnp.logical_or(col == 0, col == TCOLS - 1)
    is_middle = jnp.logical_not(is_edge)
    outer_device = me + 2 * outer
    middle_device = me - 2 * outer
    relay_device = me + 4 * outer
    other_core = me + 1 - 2 * group
    own_slot = slot_of(0, 0)
    stride = TCOLS
    has_hop = {-1: tile >= stride // 2, 1: tile + stride // 2 < time_count * TCOLS}
    is_hop = jnp.logical_and(has_hop[-1], has_hop[1])

    def hop_slot(step):
        return 9 if step < 0 else 10

    def load(h):
        columns = pl.ds(pl.multiple_of(h * HD, HD), HD)
        return (
            pltpu.make_async_copy(k_hbm.at[0, :, columns], kv.at[own_slot, h, 0], load_sem.at[0, h]),
            pltpu.make_async_copy(v_hbm.at[0, :, columns], kv.at[own_slot, h, 1], load_sem.at[1, h]),
            pltpu.make_async_copy(q_hbm.at[0, :, columns], q_s.at[h], load_sem.at[2, h]),
        )

    for h in range(heads):
        for copy in load(jnp.int32(h)):
            copy.start()
    w_copy = pltpu.make_async_copy(w_hbm, w_s, w_sem)
    w_copy.start()

    barrier = pltpu.get_barrier_semaphore()

    def greet(device):
        pl.semaphore_signal(barrier, inc=1, device_id={"tm": device}, device_id_type=MESH)

    greetings = jnp.int32(2)
    greet(other_core)
    greet(outer_device)
    for step in (-1, 1):
        pl.when(has_hop[step])(lambda step=step: greet(me + stride * step))
        greetings = greetings + has_hop[step].astype(jnp.int32)
    pl.when(is_middle)(lambda: greet(middle_device))
    greetings = greetings + is_middle.astype(jnp.int32)
    pl.semaphore_wait(barrier, greetings)

    def transfer(kind, h, source, target, device):
        return pltpu.make_async_remote_copy(
            src_ref=kv.at[source, h],
            dst_ref=kv.at[target, h],
            send_sem=send_sem.at[kind, h],
            recv_sem=recv_sem.at[target, h],
            device_id={"tm": device},
            device_id_type=MESH,
        )

    def arrive(slot, h):
        transfer(0, h, slot, slot, other_core).wait_recv()

    def send_time(step, h):
        return transfer(0 if step < 0 else 1, h, own_slot, hop_slot(step), me + stride * step)

    def send_hop(step, h):
        return transfer(11 if step < 0 else 12, h, hop_slot(step), slot_of(-step, 0), me + stride * step)

    def send_outer(step, h):
        return transfer(3 + step, h, slot_of(step, 0), slot_of(step, 0) - outer, outer_device)

    def send_middle(step, h):
        return transfer(6 + step, h, slot_of(step, 0), slot_of(step, 0) + outer, middle_device)

    def send_relay(step, h):
        return transfer(9 + step, h, slot_of(step, 0) + outer, slot_of(step, 0) - outer, relay_device)

    def straight(step, h):
        return h >= heads - (DIRECT_OWN if step == 0 else DIRECT_CORNER)

    def send_att(h):
        return pltpu.make_async_remote_copy(
            src_ref=outgoing.at[h],
            dst_ref=attended.at[group, h],
            send_sem=att_send_sem.at[h],
            recv_sem=att_recv_sem.at[h],
            device_id={"tm": other_core},
            device_id_type=MESH,
        )

    def recv_att(h):
        return pltpu.make_async_remote_copy(
            src_ref=outgoing.at[h],
            dst_ref=attended.at[1 - group, h],
            send_sem=att_send_sem.at[h],
            recv_sem=att_recv_sem.at[h],
            device_id={"tm": other_core},
            device_id_type=MESH,
        )

    def send_own(h):
        for copy in load(h):
            copy.wait()
        for step in (-1, 1):
            pl.when(has_time[step])(lambda step=step: send_time(step, h).start())
        send_outer(0, h).start()
        if DIRECT_OWN:
            pl.when(jnp.logical_and(is_middle, straight(0, h)))(lambda: send_middle(0, h).start())

    for h in range(AHEAD):
        send_own(jnp.int32(h))

    exponent_scale = (HD ** (-0.5)) * LOG2E

    def attend(slot, h, first=False):
        scores = lax.dot_general(
            q_s[h], kv[slot, h, 0], (((1,), (1,)), ((), ())), preferred_element_type=jnp.float32
        )
        row_max = jnp.max(scores, axis=1, keepdims=True)
        if not first:
            old_max = m_s[h][:, :1]
            row_max = jnp.maximum(row_max, old_max)
        weights = jnp.exp2((scores - row_max) * exponent_scale)
        total = jnp.sum(weights, axis=1, keepdims=True)
        result = jnp.dot(weights.astype(jnp.bfloat16), kv[slot, h, 1], preferred_element_type=jnp.float32)
        if not first:
            keep = jnp.exp2((old_max - row_max) * exponent_scale)
            total = total + keep * l_s[h][:, :1]
            result = result + keep * acc_s[h]
        m_s[h] = jnp.broadcast_to(row_max, (rows, HD))
        l_s[h] = jnp.broadcast_to(total, (rows, HD))
        acc_s[h] = result

    def finish(h):
        acc_s[h] = acc_s[h] / l_s[h]
        attended[group, h] = acc_s[h, pl.ds(pl.multiple_of(group * half, 16), half), :].astype(jnp.bfloat16)
        outgoing[h] = acc_s[h, pl.ds(pl.multiple_of((1 - group) * half, 16), half), :].astype(jnp.bfloat16)

    def ready(h):
        return jnp.logical_and(h >= 0, h < heads)

    @pl.loop(0, heads + LAG_MIDDLE)
    def _(i):
        pl.when(i + AHEAD < heads)(lambda: send_own(i + AHEAD))

        @pl.when(jnp.logical_and(i < heads, is_edge))
        def _():
            arrive(own_slot + outer, i)
            pl.when(jnp.logical_not(straight(0, i)))(lambda: send_relay(0, i).start())

        @pl.when(jnp.logical_and(i < heads, is_hop))
        def _():
            for step in (-1, 1):
                arrive(hop_slot(step), i)
                send_hop(step, i).start()

        crossed = i - LAG_TIME

        @pl.when(ready(crossed))
        def _():
            for step in (-1, 1):

                @pl.when(has_time[step])
                def _():
                    arrive(slot_of(step, 0), crossed)
                    send_outer(step, crossed).start()
                    if DIRECT_CORNER:
                        pl.when(jnp.logical_and(is_middle, straight(step, crossed)))(
                            lambda: send_middle(step, crossed).start()
                        )

        back = i - LAG_CORNER

        @pl.when(jnp.logical_and(ready(back), is_edge))
        def _():
            for step in (-1, 1):

                @pl.when(has_time[step])
                def _():
                    arrive(slot_of(step, 0) + outer, back)
                    pl.when(jnp.logical_not(straight(step, back)))(lambda: send_relay(step, back).start())

        pl.when(i < heads)(lambda: attend(own_slot, i, first=True))

        @pl.when(ready(crossed))
        def _():
            for step in (-1, 1):
                pl.when(has_time[step])(lambda: attend(slot_of(step, 0), crossed))

        @pl.when(ready(back))
        def _():
            pl.when(is_middle)(lambda: arrive(own_slot + outer, back))
            attend(own_slot + outer, back)
            for step in (-1, 1):

                @pl.when(has_time[step])
                def _():
                    pl.when(is_middle)(lambda: arrive(slot_of(step, 0) + outer, back))
                    attend(slot_of(step, 0) + outer, back)

        last = i - LAG_MIDDLE

        @pl.when(last >= 1)
        def _():
            send_att(last - 1).start()

        @pl.when(last >= 0)
        def _():
            @pl.when(is_middle)
            def _():
                arrive(own_slot - outer, last)
                attend(own_slot - outer, last)
                for step in (-1, 1):

                    @pl.when(has_time[step])
                    def _():
                        arrive(slot_of(step, 0) - outer, last)
                        attend(slot_of(step, 0) - outer, last)

            finish(last)

    send_att(heads - 1).start()
    w_copy.wait()

    for h in range(heads):
        recv_att(h).wait_recv()

    width = out_ref.shape[1]
    chunk = 512
    lhs = jnp.concatenate([attended[part, h] for part in range(2) for h in range(heads)], axis=1)

    @pl.loop(0, width // chunk, unroll=True)
    def _(n):
        columns = pl.ds(pl.multiple_of(n * chunk, chunk), chunk)
        out_ref[:, columns] = jnp.dot(lhs, w_s[:, columns], preferred_element_type=jnp.float32).astype(
            out_ref.dtype
        )

    @pl.loop(0, heads)
    def _(h):
        send_att(h).wait_send()
        send_outer(0, h).wait_send()

        @pl.when(is_hop)
        def _():
            for step in (-1, 1):
                send_hop(step, h).wait_send()

        if DIRECT_OWN:
            pl.when(jnp.logical_and(is_middle, straight(0, h)))(lambda: send_middle(0, h).wait_send())
        pl.when(jnp.logical_and(is_edge, jnp.logical_not(straight(0, h))))(
            lambda: send_relay(0, h).wait_send()
        )
        for step in (-1, 1):

            @pl.when(has_time[step])
            def _():
                send_time(step, h).wait_send()
                send_outer(step, h).wait_send()
                if DIRECT_CORNER:
                    pl.when(jnp.logical_and(is_middle, straight(step, h)))(
                        lambda: send_middle(step, h).wait_send()
                    )
                pl.when(jnp.logical_and(is_edge, jnp.logical_not(straight(step, h))))(
                    lambda: send_relay(step, h).wait_send()
                )


def crossing_order(heads):
    order = [(from_pal, h) for h in range(heads - 4) for from_pal in (True, False)]
    order += [(True, heads - 4), (True, heads - 3), (False, heads - 4), (True, heads - 2)]
    return order + [(False, h) for h in range(heads - 3, heads)]


def balanced_kernel(
    tiles,
    q_hbm,
    k_hbm,
    v_hbm,
    w_hbm,
    out_ref,
    q_s,
    guest_q,
    kv,
    w_s,
    m_s,
    l_s,
    acc_s,
    mixed_s,
    done_s,
    other_s,
    share_out,
    share_in,
    stat_out,
    stat_in,
    pal_q,
    pal_share_out,
    pal_share_in,
    pal_stat_out,
    pal_stat_in,
    load_sem,
    q_sem,
    w_sem,
    send_sem,
    recv_sem,
    q_send_sem,
    q_recv_sem,
    share_send_sem,
    share_recv_sem,
    pal_send_sem,
    pal_recv_sem,
    att_send_sem,
    att_recv_sem,
):
    heads, rows = q_s.shape[:2]
    half = rows // 2
    last = heads - 1
    early_heads = heads - 3
    first_heads = heads - 4
    tail = heads - NEAR
    me = lax.axis_index("tm")
    group = lax.rem(me, 2)
    tile = lax.div(me, 2)
    lower = tile < tiles // 2
    role = jnp.where(lower, tile, tiles - 1 - tile)
    side = lax.rem(role, 2)
    is_cut_row = role >= 2
    is_outer_row = jnp.logical_not(is_cut_row)
    is_corner = role == 1
    is_near = role == 2
    is_host = role == 3
    pal = role + 1 - 2 * side
    row_base = role - side
    swapped = 5 - side
    straight = 4 + side
    far = 6 + side
    pal_far = 7 - side
    other_core = me + 1 - 2 * group

    def device_of(slot):
        return 2 * jnp.where(lower, slot, tiles - 1 - slot) + group

    pal_device = device_of(pal)
    up_down_device = device_of(jnp.where(is_cut_row, role - 2, role + 2))
    cut_device = device_of(role + 2)
    corner_device = device_of(1)

    def load(h):
        columns = pl.ds(pl.multiple_of(h * HD, HD), HD)
        return (
            pltpu.make_async_copy(k_hbm.at[0, :, columns], kv.at[role, h, 0], load_sem.at[h]),
            pltpu.make_async_copy(v_hbm.at[0, :, columns], kv.at[role, h, 1], load_sem.at[h]),
            pltpu.make_async_copy(q_hbm.at[0, :, columns], q_s.at[h], q_sem),
        )

    def load_w(h, which):
        owner = group if which == 0 else 1 - group
        source = pl.ds(pl.multiple_of((owner * heads + h) * HD, HD), HD)
        target = pl.ds(pl.multiple_of((which * heads + h) * HD, HD), HD)
        return pltpu.make_async_copy(w_hbm.at[source], w_s.at[target], w_sem)

    barrier = pltpu.get_barrier_semaphore()

    def greet(device):
        pl.semaphore_signal(barrier, inc=1, device_id={"tm": device}, device_id_type=MESH)

    greet(other_core)
    greet(pal_device)
    greet(up_down_device)
    pl.when(is_cut_row)(lambda: greet(cut_device))
    pl.when(is_corner)(lambda: greet(device_of(2)))
    for h in (last, *range(last)):
        for copy in load(jnp.int32(h)):
            copy.start()
    pl.semaphore_wait(barrier, 3 + is_cut_row.astype(jnp.int32) + is_near.astype(jnp.int32))

    def transfer(way, slot, h, target, device, part=None, kind=0, landing=0):
        return pltpu.make_async_remote_copy(
            src_ref=kv.at[slot, h] if part is None else kv.at[slot, h, part],
            dst_ref=kv.at[target, h] if part is None else kv.at[target, h, part],
            send_sem=send_sem.at[way],
            recv_sem=recv_sem.at[landing, kind] if part == 1 else recv_sem.at[target, h],
            device_id={"tm": device},
            device_id_type=MESH,
        )

    def arrive(slot, h, part=None, kind=0):
        transfer(0, slot, h, slot, pal_device, part, kind, role).wait_recv()

    def to_pal(slot, h, part=None, kind=0, way=0):
        return transfer(way, slot, h, slot, pal_device, part, kind, pal)

    def up_down(slot, h, way=1):
        return transfer(way, slot, h, slot, up_down_device)

    def cross(slot, h, part=None, kind=0):
        return transfer(2, slot, h, tiles - 1 - slot, cut_device, part, kind, pal)

    def split_or_whole(is_split, act):
        pl.when(jnp.logical_not(is_split))(lambda: act(None))

        @pl.when(is_split)
        def _():
            for part in range(2):
                act(part)

    def send_q(h, source=q_s, device=up_down_device):
        return pltpu.make_async_remote_copy(
            src_ref=source.at[h],
            dst_ref=guest_q.at[h],
            send_sem=q_send_sem,
            recv_sem=q_recv_sem.at[h],
            device_id={"tm": device},
            device_id_type=MESH,
        )

    def lend_q(h):
        return pltpu.make_async_remote_copy(
            src_ref=q_s.at[h],
            dst_ref=share_in.at[h],
            send_sem=q_send_sem,
            recv_sem=share_recv_sem.at[0, h],
            device_id={"tm": up_down_device},
            device_id_type=MESH,
        )

    def send_share(h, device=corner_device):
        return tuple(
            pltpu.make_async_remote_copy(
                src_ref=source.at[h],
                dst_ref=target.at[h],
                send_sem=share_send_sem.at[which],
                recv_sem=share_recv_sem.at[which, h],
                device_id={"tm": device},
                device_id_type=MESH,
            )
            for which, (source, target) in enumerate(((share_out, share_in), (stat_out, stat_in)))
        )

    def send_pal(source, target, which, index):
        return pltpu.make_async_remote_copy(
            src_ref=source,
            dst_ref=target,
            send_sem=pal_send_sem.at[which],
            recv_sem=pal_recv_sem.at[which, index],
            device_id={"tm": pal_device},
            device_id_type=MESH,
        )

    def send_pal_share(index):
        return (
            send_pal(pal_share_out.at[index], pal_share_in.at[index], 1, index),
            send_pal(pal_stat_out.at[index], pal_stat_in.at[index], 2, index),
        )

    own_half = pl.ds(pl.multiple_of(group * half, 16), half)
    their_half = pl.ds(pl.multiple_of((1 - group) * half, 16), half)

    def send_att(h):
        return pltpu.make_async_remote_copy(
            src_ref=done_s.at[h, their_half],
            dst_ref=other_s.at[h],
            send_sem=att_send_sem,
            recv_sem=att_recv_sem.at[jnp.where(h < first_heads, 0, jnp.where(h < early_heads, 1, 2))],
            device_id={"tm": other_core},
            device_id_type=MESH,
        )

    def recv_att(first, stop, which):
        rows_in = other_s.at[pl.ds(first, stop - first)]
        pltpu.make_async_copy(rows_in, rows_in, att_recv_sem.at[which]).wait()

    def send_own(h):
        if h == 0:
            split_or_whole(is_cut_row, lambda part: to_pal(role, 0, part, FIRST_OWN).start())
        else:
            to_pal(role, h).start()
        pl.when(is_outer_row)(lambda: up_down(role, h).start())

    for h in (last, *range(last)):
        pltpu.make_async_copy(kv.at[role, h], kv.at[role, h], load_sem.at[h]).wait()
        if h == last:
            pl.when(is_cut_row)(lambda: cross(role, last).start())
        else:
            send_own(h)
        if h == 1:
            pltpu.make_async_copy(q_s, q_s, q_sem).wait()

            @pl.when(is_corner)
            def _():
                send_q(last, device=pal_device).start()
    send_own(last)

    @pl.when(is_corner)
    def _():
        for h in (*range(tail, last), *range(tail)):
            send_q(h).start()

    @pl.when(is_near)
    def _():
        for h in range(heads):
            lend_q(h).start()

    @pl.when(is_cut_row)
    def _():
        for h in range(tail, heads):
            send_pal(q_s.at[h], pal_q.at[h - tail], 0, h - tail).start()

    exponent_scale = (HD ** (-0.5)) * LOG2E

    def attend(queries, slots, h, old_max=None):
        scores = [
            lax.dot_general(queries, kv[slot, h, 0], (((1,), (1,)), ((), ())), preferred_element_type=jnp.float32)
            for slot in slots
        ]
        row_max = functools.reduce(jnp.maximum, [jnp.max(s, axis=1, keepdims=True) for s in scores])
        if old_max is not None:
            row_max = jnp.maximum(row_max, old_max)
        weights = [jnp.exp2((s - row_max) * exponent_scale) for s in scores]
        total = sum(jnp.sum(w, axis=1, keepdims=True) for w in weights)
        result = sum(
            jnp.dot(w.astype(jnp.bfloat16), kv[slot, h, 1], preferred_element_type=jnp.float32)
            for w, slot in zip(weights, slots)
        )
        return row_max, total, result

    def attend_more(slots, h):
        old_max = m_s[h][:, :1]
        row_max, total, result = attend(q_s[h], slots, h, old_max)
        keep = jnp.exp2((old_max - row_max) * exponent_scale)
        return row_max, total + keep * l_s[h][:, :1], result + keep * acc_s[h]

    def hold(h, row_max, total, result):
        m_s[h] = jnp.broadcast_to(row_max, (rows, HD))
        l_s[h] = jnp.broadcast_to(total, (rows, HD))
        acc_s[h] = result

    def finish(h, row_max, total, result):
        done_s[h] = (result / total).astype(jnp.bfloat16)

    def share(h, queries, slots, share_to, stat_to):
        row_max, total, result = attend(queries, slots, h)
        share_to[...] = (result / total).astype(jnp.bfloat16)
        lane = lax.broadcasted_iota(jnp.int32, (rows, HD), 1)
        stats = jnp.where(lax.rem(lane, 8) < 4, row_max, total)
        stat_to[...] = jnp.transpose(stats)[:8]

    def merge(h, shared, stats):
        row_max, total, result = m_s[h], l_s[h], acc_s[h]
        their_max = jnp.transpose(jnp.broadcast_to(stats[0:1, :], (HD, rows)))
        their_total = jnp.transpose(jnp.broadcast_to(stats[4:5, :], (HD, rows)))
        top = jnp.maximum(row_max, their_max)
        keep = jnp.exp2((row_max - top) * exponent_scale)
        weight = their_total * jnp.exp2((their_max - top) * exponent_scale)
        return top, keep * total + weight, keep * result + weight * shared[...].astype(jnp.float32)

    width = out_ref.shape[1]
    chunk = OUT_CHUNK

    def half_mix(which, first, stop):
        lhs = jnp.concatenate(
            [other_s[h] if which else done_s[h, own_half, :] for h in range(first, stop)], axis=1
        )
        depth = slice((which * heads + first) * HD, (which * heads + stop) * HD)

        def product(n):
            columns = pl.ds(n * chunk, chunk)
            return columns, jnp.dot(lhs, w_s[depth, columns], preferred_element_type=jnp.float32)

        return (product(n) for n in range(width // chunk))

    def mix(first, stop):
        for (columns, own), (_, other) in zip(half_mix(0, first, stop), half_mix(1, first, stop)):
            yield columns, own + other

    def ready(h):
        return jnp.logical_and(h >= 0, h < heads)

    is_slow = jnp.logical_and(is_cut_row, group == 0)
    mix_at = 2 * heads - jnp.where(is_slow, 3, 1)
    mix_gap = is_cut_row.astype(jnp.int32)

    @pl.loop(0, 2 * heads + 2)
    def _(i):
        settled = jnp.where(
            jnp.logical_and(role == 0, i == heads + 1), last, i - heads - jnp.where(is_corner, 3, 2)
        )
        settles = jnp.logical_and(ready(settled), jnp.logical_or(role != 0, i <= 2 * heads))
        held = jnp.logical_and(is_near, settled == tail - 1)
        pl.when(jnp.logical_and(settles, jnp.logical_not(held)))(lambda: send_att(settled).start())
        pl.when(jnp.logical_and(is_near, i == 2 * heads))(lambda: send_att(tail - 1).start())

        @pl.when(i == mix_at)
        def _():
            pltpu.make_async_copy(w_hbm, w_s, w_sem).wait()
            recv_att(0, first_heads, 0)
            for columns, value in mix(0, first_heads):
                mixed_s[:, columns] = value

        @pl.when(i == mix_at + mix_gap)
        def _():
            recv_att(first_heads, early_heads, 1)
            for columns, value in mix(first_heads, early_heads):
                mixed_s[:, columns] += value

        @pl.when(jnp.logical_and(i < heads, jnp.logical_or(is_outer_row, i > 0)))
        def _():
            arrive(pal, i)
            pl.when(jnp.logical_and(is_cut_row, i < last))(lambda: cross(pal, i).start())

        @pl.when(is_cut_row)
        def _():
            @pl.when(i == 0)
            def _():
                for part in range(2):
                    arrive(pal, 0, part, FIRST_OWN)
                    cross(pal, 0, part, FIRST_CROSSED).start()
                arrive(side, 0)
                cross(side, 0).start()
                arrive(straight, last)
                up_down(straight, last).start()

            def pass_on(h):
                arrive(side, h)
                cross(side, h).start()

            def take(from_pal, h):
                if from_pal:
                    for part in range(2) if h == 0 else (None,):
                        arrive(swapped, h, part, FIRST_CROSSED)
                    up_down(swapped, h).start()
                else:
                    arrive(far, h)
                    if h < tail:
                        to_pal(far, h, way=3).start()

            at = 0
            for place, (from_pal, h) in enumerate(crossing_order(heads)):
                at = max(at, h)
                if not from_pal and h > 0:
                    pl.when(i == at)(lambda h=h: pass_on(h))
            for place, (from_pal, h) in enumerate(crossing_order(heads)):
                pl.when(i == place + 1)(lambda from_pal=from_pal, h=h: take(from_pal, h))

        @pl.when(is_outer_row)
        def _():
            @pl.when(i == 1)
            def _():
                arrive(straight, last)
                to_pal(straight, last).start()

            def relay(j):
                arrive(swapped, j)
                to_pal(swapped, j).start()

            for place, (from_pal, h) in enumerate(crossing_order(heads)):
                if from_pal:
                    at = place + (3 if h < heads - 3 else 2)
                    pl.when(i == at)(lambda h=h: relay(h))

        nearby = i - heads

        @pl.when(jnp.logical_and(is_near, jnp.logical_and(nearby >= heads - NEAR, nearby < heads)))
        def _():
            send_q(nearby).wait_recv()
            share(nearby, guest_q[nearby], (2, 6), share_out.at[nearby], stat_out.at[nearby])
            for copy in send_share(nearby):
                copy.start()

        @pl.when(jnp.logical_and(is_cut_row, jnp.logical_and(nearby >= tail, nearby < heads)))
        def _():
            index = nearby - tail
            send_pal(q_s.at[nearby], pal_q.at[index], 0, index).wait_recv()
            share(nearby, pal_q[index], (far,), pal_share_out.at[index], pal_stat_out.at[index])
            for copy in send_pal_share(index):
                copy.start()

        @pl.when(jnp.logical_and(i >= 1, i <= heads))
        def _():
            for which in range(2):
                load_w(i - 1, which).start()

        @pl.when(i < heads)
        def _():
            hold(i, *attend(q_s[i], (row_base, row_base + 1), i))

        @pl.when(jnp.logical_and(i < heads, role == 0))
        def _():
            lend_q(i).wait_recv()
            share(i, share_in[i], (1,), share_out.at[i], stat_out.at[i])
            for copy in send_share(i, up_down_device):
                copy.start()

        @pl.when(jnp.logical_and(ready(i - last), is_near))
        def _():
            h = i - last
            for copy in send_share(h):
                copy.wait_recv()
            hold(h, *merge(h, share_in.at[h], stat_in.at[h]))

        @pl.when(jnp.logical_and(role == 0, i == 2))
        def _():
            send_q(last).wait_recv()
            send_q(last, source=guest_q).start()

        @pl.when(jnp.logical_and(is_host, i == heads))
        def _():
            for h in range(tail, last):
                send_q(h).wait_recv()
                send_q(h, source=guest_q, device=pal_device).start()

        @pl.when(is_outer_row)
        def _():
            ending = i - heads - 2

            @pl.when(jnp.logical_and(ready(ending), is_corner))
            def _():
                for copy in send_share(ending):
                    copy.wait_recv()
                finish(ending, *merge(ending, share_in.at[ending], stat_in.at[ending]))

            h = jnp.where(i == heads, last, i - heads - 1)

            @pl.when(jnp.logical_and(i >= heads, i < 2 * heads))
            def _():
                arrive(jnp.where(h == last, swapped, straight), h)
                pl.when(jnp.logical_and(role == 0, h == last))(lambda: up_down(swapped, h, way=3).start())
                state = attend_more((4, 5), h)
                pl.when(role == 0)(lambda: finish(h, *state))
                pl.when(is_corner)(lambda: hold(h, *state))

        ending = i - heads - 1

        is_whole = jnp.logical_and(ending >= 0, ending < tail)
        is_tail = jnp.logical_and(ending >= tail, ending < heads)

        waiting = jnp.where(i == 2 * heads - 1, tail - 1, ending)

        @pl.when(jnp.logical_and(jnp.logical_and(waiting >= 0, waiting < tail), jnp.logical_and(is_near, i != heads + tail)))
        def _():
            arrive(7, waiting)
            finish(waiting, *attend_more((5, 6, 7), waiting))

        @pl.when(jnp.logical_and(is_whole, is_host))
        def _():
            send_q(ending).wait_recv()
            arrive(6, ending)
            share(ending, guest_q[ending], (2, 6), share_out.at[ending], stat_out.at[ending])
            for copy in send_share(ending):
                copy.start()
            finish(ending, *attend_more((6, 7), ending))

        @pl.when(jnp.logical_and(is_tail, is_near))
        def _():
            pl.when(ending == last)(lambda: arrive(5, ending))
            hold(ending, *attend_more((5, 6), ending))

        @pl.when(jnp.logical_and(is_tail, is_host))
        def _():
            hold(ending, *attend_more((7,), ending))

        @pl.when(jnp.logical_and(is_cut_row, is_tail))
        def _():
            index = ending - tail
            for copy in send_pal_share(index):
                copy.wait_recv()
            finish(ending, *merge(ending, pal_share_in.at[index], pal_stat_in.at[index]))

    pl.when(is_corner)(lambda: send_att(last).start())
    for columns, value in half_mix(0, early_heads, heads):
        mixed_s[:, columns] += value
    recv_att(early_heads, heads, 2)
    for columns, value in half_mix(1, early_heads, heads):
        out_ref[:, columns] = (mixed_s[:, columns] + value).astype(out_ref.dtype)

    def drain(way, count):
        tiles_sent = kv.at[pl.ds(0, count)]
        pltpu.make_async_remote_copy(
            src_ref=tiles_sent,
            dst_ref=tiles_sent,
            send_sem=send_sem.at[way],
            recv_sem=recv_sem.at[0, 0],
            device_id={"tm": pal_device},
            device_id_type=MESH,
        ).wait_send()

    def drain_rows(sent, sem):
        pltpu.make_async_remote_copy(
            src_ref=sent,
            dst_ref=sent,
            send_sem=sem,
            recv_sem=recv_sem.at[0, 0],
            device_id={"tm": pal_device},
            device_id_type=MESH,
        ).wait_send()

    pl.when(is_outer_row)(lambda: drain(0, 2))

    @pl.when(is_cut_row)
    def _():
        drain(0, 1)
        drain_rows(kv.at[0, pl.ds(0, tail)], send_sem.at[3])
        drain_rows(pal_q, pal_send_sem.at[0])
        drain_rows(pal_share_out, pal_send_sem.at[1])
        drain_rows(pal_stat_out, pal_send_sem.at[2])

    drain(1, 1)
    drain_rows(other_s, att_send_sem)
    pl.when(role == 0)(lambda: drain_rows(kv.at[0, 0], send_sem.at[3]))
    pl.when(role == 0)(lambda: drain_rows(guest_q.at[0], q_send_sem))
    pl.when(is_host)(lambda: drain_rows(guest_q.at[pl.ds(0, NEAR - 1)], q_send_sem))
    pl.when(jnp.logical_or(is_corner, is_near))(lambda: drain_rows(q_s, q_send_sem))
    pl.when(is_cut_row)(lambda: drain(2, 2))
    for count, sender in ((heads, role == 0), (heads - NEAR, is_host), (NEAR, is_near)):
        pl.when(sender)(lambda count=count: drain_rows(share_out.at[pl.ds(0, count)], share_send_sem.at[0]))
        pl.when(sender)(lambda count=count: drain_rows(stat_out.at[pl.ds(0, count)], share_send_sem.at[1]))


def balanced_call(query_states, key_states, value_states, out_weight):
    rows, half_width = query_states.shape[1:]
    heads = half_width // HD
    depth, width = out_weight.shape
    tiles = lax.axis_size("tm") // 2
    dma = pltpu.SemaphoreType.DMA
    return pl.pallas_call(
        functools.partial(balanced_kernel, tiles),
        out_shape=jax.ShapeDtypeStruct((rows // 2, width), jnp.bfloat16),
        in_specs=[pl.BlockSpec(memory_space=pl.ANY)] * 4,
        out_specs=pl.BlockSpec(memory_space=pltpu.VMEM),
        scratch_shapes=[
            pltpu.VMEM((heads, rows, HD), jnp.bfloat16),
            pltpu.VMEM((heads, rows, HD), jnp.bfloat16),
            pltpu.VMEM((tiles, heads, 2, rows, HD), jnp.bfloat16),
            pltpu.VMEM((depth, width), jnp.bfloat16),
            pltpu.VMEM((heads, rows, HD), jnp.float32),
            pltpu.VMEM((heads, rows, HD), jnp.float32),
            pltpu.VMEM((heads, rows, HD), jnp.float32),
            pltpu.VMEM((rows // 2, width), jnp.float32),
            pltpu.VMEM((heads, rows, HD), jnp.bfloat16),
            pltpu.VMEM((heads, rows // 2, HD), jnp.bfloat16),
            pltpu.VMEM((heads, rows, HD), jnp.bfloat16),
            pltpu.VMEM((heads, rows, HD), jnp.bfloat16),
            pltpu.VMEM((heads, 8, rows), jnp.float32),
            pltpu.VMEM((heads, 8, rows), jnp.float32),
            pltpu.VMEM((NEAR, rows, HD), jnp.bfloat16),
            pltpu.VMEM((NEAR, rows, HD), jnp.bfloat16),
            pltpu.VMEM((NEAR, rows, HD), jnp.bfloat16),
            pltpu.VMEM((NEAR, 8, rows), jnp.float32),
            pltpu.VMEM((NEAR, 8, rows), jnp.float32),
            dma((heads,)),
            dma,
            dma,
            dma((4,)),
            dma((tiles, heads)),
            dma,
            dma((heads,)),
            dma((2,)),
            dma((2, heads)),
            dma((3,)),
            dma((3, NEAR)),
            dma,
            dma((3,)),
        ],
        compiler_params=pltpu.CompilerParams(
            collective_id=0, has_side_effects=True, vmem_limit_bytes=40 * 1024 * 1024
        ),
    )(*(pltpu.with_memory_space_constraint(x, pltpu.HBM) for x in (query_states, key_states, value_states, out_weight)))


def general_call(query_states, key_states, value_states, out_weight):
    rows, half_width = query_states.shape[1:]
    heads = half_width // HD
    depth, width = out_weight.shape
    time_count = lax.axis_size("tm") // (2 * TCOLS)
    return pl.pallas_call(
        functools.partial(general_kernel, time_count, heads),
        out_shape=jax.ShapeDtypeStruct((rows // 2, width), jnp.bfloat16),
        in_specs=[pl.BlockSpec(memory_space=pl.ANY)] * 4,
        out_specs=pl.BlockSpec(memory_space=pltpu.VMEM),
        scratch_shapes=[
            pltpu.VMEM((heads, rows, HD), jnp.bfloat16),
            pltpu.VMEM((11, heads, 2, rows, HD), jnp.bfloat16),
            pltpu.VMEM((depth, width), jnp.bfloat16),
            pltpu.VMEM((heads, rows, HD), jnp.float32),
            pltpu.VMEM((heads, rows, HD), jnp.float32),
            pltpu.VMEM((heads, rows, HD), jnp.float32),
            pltpu.VMEM((heads, rows // 2, HD), jnp.bfloat16),
            pltpu.VMEM((2, heads, rows // 2, HD), jnp.bfloat16),
            pltpu.SemaphoreType.DMA((3, heads)),
            pltpu.SemaphoreType.DMA,
            pltpu.SemaphoreType.DMA((13, heads)),
            pltpu.SemaphoreType.DMA((11, heads)),
            pltpu.SemaphoreType.DMA((heads,)),
            pltpu.SemaphoreType.DMA((heads,)),
        ],
        compiler_params=pltpu.CompilerParams(
            collective_id=0, has_side_effects=True, vmem_limit_bytes=56 * 1024 * 1024
        ),
    )(query_states, key_states, value_states, out_weight)


def per_device(query_states, key_states, value_states, out_weight):
    two_times = lax.axis_size("tm") == 4 * TCOLS and query_states.shape[2] >= 5 * HD
    call = balanced_call if two_times else general_call
    return call(query_states, key_states, value_states, out_weight)


def solution(mesh):
    in_specs = (
        P(("parts", "tm"), None, None),
        P(("parts", "tm"), None, None),
        P(("parts", "tm"), None, None),
        P(),
    )
    out_specs = P(("parts", "tm"), None)
    return jax.shard_map(
        per_device, mesh=mesh, in_specs=in_specs, out_specs=out_specs, check_vma=False
    )
```

```python
import functools

import jax
import jax.numpy as jnp
from jax import lax
from jax.experimental import pallas as pl
from jax.experimental.pallas import tpu as pltpu
from jax.sharding import PartitionSpec as P

TCOLS = 4
HD = 128
MESH = pl.DeviceIdType.MESH
LOG2E = 1.4426950408889634

DIRECT_OWN = 2
DIRECT_CORNER = 1
AHEAD = 2
LAG_TIME = 2
LAG_CORNER = 3
LAG_MIDDLE = 5

NEAR = 2
OUT_CHUNK = 512
FIRST_OWN, FIRST_CROSSED = range(2)


def slot_of(time_step, col_step):
    return (time_step + 1) * 3 + col_step + 1


def general_kernel(
    time_count,
    heads,
    q_hbm,
    k_hbm,
    v_hbm,
    w_hbm,
    out_ref,
    q_s,
    kv,
    w_s,
    m_s,
    l_s,
    acc_s,
    outgoing,
    attended,
    load_sem,
    w_sem,
    send_sem,
    recv_sem,
    att_send_sem,
    att_recv_sem,
):
    rows = q_s.shape[1]
    half = rows // 2
    me = lax.axis_index("tm")
    group = lax.rem(me, 2)
    tile = lax.div(me, 2)
    col = lax.rem(tile, TCOLS)
    time = lax.div(tile, TCOLS)
    has_time = {-1: time > 0, 1: time < time_count - 1}
    has_col = {-1: col > 0, 1: col < TCOLS - 1}
    outer = 1 - 2 * lax.rem(col, 2)
    is_edge = jnp.logical_or(col == 0, col == TCOLS - 1)
    is_middle = jnp.logical_not(is_edge)
    outer_device = me + 2 * outer
    middle_device = me - 2 * outer
    relay_device = me + 4 * outer
    other_core = me + 1 - 2 * group
    own_slot = slot_of(0, 0)
    stride = TCOLS
    has_hop = {-1: tile >= stride // 2, 1: tile + stride // 2 < time_count * TCOLS}
    is_hop = jnp.logical_and(has_hop[-1], has_hop[1])

    def hop_slot(step):
        return 9 if step < 0 else 10

    def load(h):
        columns = pl.ds(pl.multiple_of(h * HD, HD), HD)
        return (
            pltpu.make_async_copy(k_hbm.at[0, :, columns], kv.at[own_slot, h, 0], load_sem.at[0, h]),
            pltpu.make_async_copy(v_hbm.at[0, :, columns], kv.at[own_slot, h, 1], load_sem.at[1, h]),
            pltpu.make_async_copy(q_hbm.at[0, :, columns], q_s.at[h], load_sem.at[2, h]),
        )

    for h in range(heads):
        for copy in load(jnp.int32(h)):
            copy.start()
    w_copy = pltpu.make_async_copy(w_hbm, w_s, w_sem)
    w_copy.start()

    barrier = pltpu.get_barrier_semaphore()

    def greet(device):
        pl.semaphore_signal(barrier, inc=1, device_id={"tm": device}, device_id_type=MESH)

    greetings = jnp.int32(2)
    greet(other_core)
    greet(outer_device)
    for step in (-1, 1):
        pl.when(has_hop[step])(lambda step=step: greet(me + stride * step))
        greetings = greetings + has_hop[step].astype(jnp.int32)
    pl.when(is_middle)(lambda: greet(middle_device))
    greetings = greetings + is_middle.astype(jnp.int32)
    pl.semaphore_wait(barrier, greetings)

    def transfer(kind, h, source, target, device):
        return pltpu.make_async_remote_copy(
            src_ref=kv.at[source, h],
            dst_ref=kv.at[target, h],
            send_sem=send_sem.at[kind, h],
            recv_sem=recv_sem.at[target, h],
            device_id={"tm": device},
            device_id_type=MESH,
        )

    def arrive(slot, h):
        transfer(0, h, slot, slot, other_core).wait_recv()

    def send_time(step, h):
        return transfer(0 if step < 0 else 1, h, own_slot, hop_slot(step), me + stride * step)

    def send_hop(step, h):
        return transfer(11 if step < 0 else 12, h, hop_slot(step), slot_of(-step, 0), me + stride * step)

    def send_outer(step, h):
        return transfer(3 + step, h, slot_of(step, 0), slot_of(step, 0) - outer, outer_device)

    def send_middle(step, h):
        return transfer(6 + step, h, slot_of(step, 0), slot_of(step, 0) + outer, middle_device)

    def send_relay(step, h):
        return transfer(9 + step, h, slot_of(step, 0) + outer, slot_of(step, 0) - outer, relay_device)

    def straight(step, h):
        return h >= heads - (DIRECT_OWN if step == 0 else DIRECT_CORNER)

    def send_att(h):
        return pltpu.make_async_remote_copy(
            src_ref=outgoing.at[h],
            dst_ref=attended.at[group, h],
            send_sem=att_send_sem.at[h],
            recv_sem=att_recv_sem.at[h],
            device_id={"tm": other_core},
            device_id_type=MESH,
        )

    def recv_att(h):
        return pltpu.make_async_remote_copy(
            src_ref=outgoing.at[h],
            dst_ref=attended.at[1 - group, h],
            send_sem=att_send_sem.at[h],
            recv_sem=att_recv_sem.at[h],
            device_id={"tm": other_core},
            device_id_type=MESH,
        )

    def send_own(h):
        for copy in load(h):
            copy.wait()
        for step in (-1, 1):
            pl.when(has_time[step])(lambda step=step: send_time(step, h).start())
        send_outer(0, h).start()
        if DIRECT_OWN:
            pl.when(jnp.logical_and(is_middle, straight(0, h)))(lambda: send_middle(0, h).start())

    for h in range(AHEAD):
        send_own(jnp.int32(h))

    exponent_scale = (HD ** (-0.5)) * LOG2E

    def attend(slot, h, first=False):
        scores = lax.dot_general(
            q_s[h], kv[slot, h, 0], (((1,), (1,)), ((), ())), preferred_element_type=jnp.float32
        )
        row_max = jnp.max(scores, axis=1, keepdims=True)
        if not first:
            old_max = m_s[h][:, :1]
            row_max = jnp.maximum(row_max, old_max)
        weights = jnp.exp2((scores - row_max) * exponent_scale)
        total = jnp.sum(weights, axis=1, keepdims=True)
        result = jnp.dot(weights.astype(jnp.bfloat16), kv[slot, h, 1], preferred_element_type=jnp.float32)
        if not first:
            keep = jnp.exp2((old_max - row_max) * exponent_scale)
            total = total + keep * l_s[h][:, :1]
            result = result + keep * acc_s[h]
        m_s[h] = jnp.broadcast_to(row_max, (rows, HD))
        l_s[h] = jnp.broadcast_to(total, (rows, HD))
        acc_s[h] = result

    def finish(h):
        acc_s[h] = acc_s[h] / l_s[h]
        attended[group, h] = acc_s[h, pl.ds(pl.multiple_of(group * half, 16), half), :].astype(jnp.bfloat16)
        outgoing[h] = acc_s[h, pl.ds(pl.multiple_of((1 - group) * half, 16), half), :].astype(jnp.bfloat16)

    def ready(h):
        return jnp.logical_and(h >= 0, h < heads)

    @pl.loop(0, heads + LAG_MIDDLE)
    def _(i):
        pl.when(i + AHEAD < heads)(lambda: send_own(i + AHEAD))

        @pl.when(jnp.logical_and(i < heads, is_edge))
        def _():
            arrive(own_slot + outer, i)
            pl.when(jnp.logical_not(straight(0, i)))(lambda: send_relay(0, i).start())

        @pl.when(jnp.logical_and(i < heads, is_hop))
        def _():
            for step in (-1, 1):
                arrive(hop_slot(step), i)
                send_hop(step, i).start()

        crossed = i - LAG_TIME

        @pl.when(ready(crossed))
        def _():
            for step in (-1, 1):

                @pl.when(has_time[step])
                def _():
                    arrive(slot_of(step, 0), crossed)
                    send_outer(step, crossed).start()
                    if DIRECT_CORNER:
                        pl.when(jnp.logical_and(is_middle, straight(step, crossed)))(
                            lambda: send_middle(step, crossed).start()
                        )

        back = i - LAG_CORNER

        @pl.when(jnp.logical_and(ready(back), is_edge))
        def _():
            for step in (-1, 1):

                @pl.when(has_time[step])
                def _():
                    arrive(slot_of(step, 0) + outer, back)
                    pl.when(jnp.logical_not(straight(step, back)))(lambda: send_relay(step, back).start())

        pl.when(i < heads)(lambda: attend(own_slot, i, first=True))

        @pl.when(ready(crossed))
        def _():
            for step in (-1, 1):
                pl.when(has_time[step])(lambda: attend(slot_of(step, 0), crossed))

        @pl.when(ready(back))
        def _():
            pl.when(is_middle)(lambda: arrive(own_slot + outer, back))
            attend(own_slot + outer, back)
            for step in (-1, 1):

                @pl.when(has_time[step])
                def _():
                    pl.when(is_middle)(lambda: arrive(slot_of(step, 0) + outer, back))
                    attend(slot_of(step, 0) + outer, back)

        last = i - LAG_MIDDLE

        @pl.when(last >= 1)
        def _():
            send_att(last - 1).start()

        @pl.when(last >= 0)
        def _():
            @pl.when(is_middle)
            def _():
                arrive(own_slot - outer, last)
                attend(own_slot - outer, last)
                for step in (-1, 1):

                    @pl.when(has_time[step])
                    def _():
                        arrive(slot_of(step, 0) - outer, last)
                        attend(slot_of(step, 0) - outer, last)

            finish(last)

    send_att(heads - 1).start()
    w_copy.wait()

    for h in range(heads):
        recv_att(h).wait_recv()

    width = out_ref.shape[1]
    chunk = 512
    lhs = jnp.concatenate([attended[part, h] for part in range(2) for h in range(heads)], axis=1)

    @pl.loop(0, width // chunk, unroll=True)
    def _(n):
        columns = pl.ds(pl.multiple_of(n * chunk, chunk), chunk)
        out_ref[:, columns] = jnp.dot(lhs, w_s[:, columns], preferred_element_type=jnp.float32).astype(
            out_ref.dtype
        )

    @pl.loop(0, heads)
    def _(h):
        send_att(h).wait_send()
        send_outer(0, h).wait_send()

        @pl.when(is_hop)
        def _():
            for step in (-1, 1):
                send_hop(step, h).wait_send()

        if DIRECT_OWN:
            pl.when(jnp.logical_and(is_middle, straight(0, h)))(lambda: send_middle(0, h).wait_send())
        pl.when(jnp.logical_and(is_edge, jnp.logical_not(straight(0, h))))(
            lambda: send_relay(0, h).wait_send()
        )
        for step in (-1, 1):

            @pl.when(has_time[step])
            def _():
                send_time(step, h).wait_send()
                send_outer(step, h).wait_send()
                if DIRECT_CORNER:
                    pl.when(jnp.logical_and(is_middle, straight(step, h)))(
                        lambda: send_middle(step, h).wait_send()
                    )
                pl.when(jnp.logical_and(is_edge, jnp.logical_not(straight(step, h))))(
                    lambda: send_relay(step, h).wait_send()
                )


def crossing_order(heads):
    order = [(from_pal, h) for h in range(heads - 4) for from_pal in (True, False)]
    order += [(True, heads - 4), (True, heads - 3), (False, heads - 4), (True, heads - 2)]
    return order + [(False, h) for h in range(heads - 3, heads)]


def balanced_kernel(
    tiles,
    q_hbm,
    k_hbm,
    v_hbm,
    w_hbm,
    out_ref,
    q_s,
    guest_q,
    kv,
    w_s,
    m_s,
    l_s,
    acc_s,
    mixed_s,
    done_s,
    other_s,
    share_out,
    share_in,
    stat_out,
    stat_in,
    pal_q,
    pal_share_out,
    pal_share_in,
    pal_stat_out,
    pal_stat_in,
    load_sem,
    q_sem,
    w_sem,
    send_sem,
    recv_sem,
    q_send_sem,
    q_recv_sem,
    share_send_sem,
    share_recv_sem,
    pal_send_sem,
    pal_recv_sem,
    att_send_sem,
    att_recv_sem,
):
    heads, rows = q_s.shape[:2]
    half = rows // 2
    last = heads - 1
    early_heads = heads - 3
    first_heads = heads - 4
    tail = heads - NEAR
    me = lax.axis_index("tm")
    group = lax.rem(me, 2)
    tile = lax.div(me, 2)
    lower = tile < tiles // 2
    role = jnp.where(lower, tile, tiles - 1 - tile)
    side = lax.rem(role, 2)
    is_cut_row = role >= 2
    is_outer_row = jnp.logical_not(is_cut_row)
    is_corner = role == 1
    is_near = role == 2
    is_host = role == 3
    pal = role + 1 - 2 * side
    row_base = role - side
    swapped = 5 - side
    straight = 4 + side
    far = 6 + side
    pal_far = 7 - side
    other_core = me + 1 - 2 * group

    def device_of(slot):
        return 2 * jnp.where(lower, slot, tiles - 1 - slot) + group

    pal_device = device_of(pal)
    up_down_device = device_of(jnp.where(is_cut_row, role - 2, role + 2))
    cut_device = device_of(role + 2)
    corner_device = device_of(1)

    def load(h):
        columns = pl.ds(pl.multiple_of(h * HD, HD), HD)
        return (
            pltpu.make_async_copy(k_hbm.at[0, :, columns], kv.at[role, h, 0], load_sem.at[h]),
            pltpu.make_async_copy(v_hbm.at[0, :, columns], kv.at[role, h, 1], load_sem.at[h]),
            pltpu.make_async_copy(q_hbm.at[0, :, columns], q_s.at[h], q_sem),
        )

    def load_w(h, which):
        owner = group if which == 0 else 1 - group
        source = pl.ds(pl.multiple_of((owner * heads + h) * HD, HD), HD)
        target = pl.ds(pl.multiple_of((which * heads + h) * HD, HD), HD)
        return pltpu.make_async_copy(w_hbm.at[source], w_s.at[target], w_sem)

    barrier = pltpu.get_barrier_semaphore()

    def greet(device):
        pl.semaphore_signal(barrier, inc=1, device_id={"tm": device}, device_id_type=MESH)

    greet(other_core)
    greet(pal_device)
    greet(up_down_device)
    pl.when(is_cut_row)(lambda: greet(cut_device))
    pl.when(is_corner)(lambda: greet(device_of(2)))
    for h in (last, *range(last)):
        for copy in load(jnp.int32(h)):
            copy.start()
    pl.semaphore_wait(barrier, 3 + is_cut_row.astype(jnp.int32) + is_near.astype(jnp.int32))

    def row_of(slot):
        return jnp.where(slot < 4, lax.div(slot, 2), slot - 2)

    def transfer(way, slot, h, target, device, part=None, kind=0, landing=0):
        slot, target = jnp.int32(slot), jnp.int32(target)
        return pltpu.make_async_remote_copy(
            src_ref=kv.at[slot, h] if part is None else kv.at[slot, h, part],
            dst_ref=kv.at[target, h] if part is None else kv.at[target, h, part],
            send_sem=send_sem.at[way],
            recv_sem=recv_sem.at[landing, kind] if part == 1 else recv_sem.at[row_of(target), h],
            device_id={"tm": device},
            device_id_type=MESH,
        )

    def arrive(slot, h, part=None, kind=0):
        transfer(0, slot, h, slot, pal_device, part, kind, 2 + side).wait_recv()

    def to_pal(slot, h, part=None, kind=0, way=0):
        return transfer(way, slot, h, slot, pal_device, part, kind, 3 - side)

    def up_down(slot, h, way=1):
        return transfer(way, slot, h, slot, up_down_device)

    def cross(slot, h, part=None, kind=0):
        return transfer(2, slot, h, tiles - 1 - slot, cut_device, part, kind, 3 - side)

    def split_or_whole(is_split, act):
        pl.when(jnp.logical_not(is_split))(lambda: act(None))

        @pl.when(is_split)
        def _():
            for part in range(2):
                act(part)

    def send_q(h, source=q_s, device=up_down_device):
        return pltpu.make_async_remote_copy(
            src_ref=source.at[h],
            dst_ref=guest_q.at[h],
            send_sem=q_send_sem,
            recv_sem=q_recv_sem.at[h],
            device_id={"tm": device},
            device_id_type=MESH,
        )

    def lend_q(h):
        return pltpu.make_async_remote_copy(
            src_ref=q_s.at[h],
            dst_ref=share_in.at[h],
            send_sem=q_send_sem,
            recv_sem=share_recv_sem.at[0, h],
            device_id={"tm": up_down_device},
            device_id_type=MESH,
        )

    def send_share(h, device=corner_device):
        return tuple(
            pltpu.make_async_remote_copy(
                src_ref=source.at[h],
                dst_ref=target.at[h],
                send_sem=share_send_sem.at[which],
                recv_sem=share_recv_sem.at[which, h],
                device_id={"tm": device},
                device_id_type=MESH,
            )
            for which, (source, target) in enumerate(((share_out, share_in), (stat_out, stat_in)))
        )

    def send_pal(source, target, which, index):
        return pltpu.make_async_remote_copy(
            src_ref=source,
            dst_ref=target,
            send_sem=pal_send_sem.at[which],
            recv_sem=pal_recv_sem.at[which, index],
            device_id={"tm": pal_device},
            device_id_type=MESH,
        )

    def send_pal_share(index):
        return (
            send_pal(pal_share_out.at[index], pal_share_in.at[index], 1, index),
            send_pal(pal_stat_out.at[index], pal_stat_in.at[index], 2, index),
        )

    own_half = pl.ds(pl.multiple_of(group * half, 16), half)
    their_half = pl.ds(pl.multiple_of((1 - group) * half, 16), half)

    def send_att(h):
        return pltpu.make_async_remote_copy(
            src_ref=done_s.at[h, their_half],
            dst_ref=other_s.at[h],
            send_sem=att_send_sem,
            recv_sem=att_recv_sem.at[jnp.where(h < first_heads, 0, jnp.where(h < early_heads, 1, 2))],
            device_id={"tm": other_core},
            device_id_type=MESH,
        )

    def recv_att(first, stop, which):
        rows_in = other_s.at[pl.ds(first, stop - first)]
        pltpu.make_async_copy(rows_in, rows_in, att_recv_sem.at[which]).wait()

    def send_own(h):
        if h == 0:
            split_or_whole(is_cut_row, lambda part: to_pal(role, 0, part, FIRST_OWN).start())
        else:
            to_pal(role, h).start()
        pl.when(is_outer_row)(lambda: up_down(role, h).start())

    for h in (last, *range(last)):
        pltpu.make_async_copy(kv.at[role, h], kv.at[role, h], load_sem.at[h]).wait()
        if h == last:
            pl.when(is_cut_row)(lambda: cross(role, last).start())
        else:
            send_own(h)
        if h == 1:
            pltpu.make_async_copy(q_s, q_s, q_sem).wait()

            @pl.when(is_corner)
            def _():
                send_q(last, device=pal_device).start()
    send_own(last)

    @pl.when(is_corner)
    def _():
        for h in (*range(tail, last), *range(tail)):
            send_q(h).start()

    @pl.when(is_near)
    def _():
        for h in range(heads):
            lend_q(h).start()

    @pl.when(is_cut_row)
    def _():
        for h in range(tail, heads):
            send_pal(q_s.at[h], pal_q.at[h - tail], 0, h - tail).start()

    exponent_scale = (HD ** (-0.5)) * LOG2E

    def attend(queries, slots, h, old_max=None):
        scores = [
            lax.dot_general(queries, kv[slot, h, 0], (((1,), (1,)), ((), ())), preferred_element_type=jnp.float32)
            for slot in slots
        ]
        row_max = functools.reduce(jnp.maximum, [jnp.max(s, axis=1, keepdims=True) for s in scores])
        if old_max is not None:
            row_max = jnp.maximum(row_max, old_max)
        weights = [jnp.exp2((s - row_max) * exponent_scale) for s in scores]
        total = sum(jnp.sum(w, axis=1, keepdims=True) for w in weights)
        result = sum(
            jnp.dot(w.astype(jnp.bfloat16), kv[slot, h, 1], preferred_element_type=jnp.float32)
            for w, slot in zip(weights, slots)
        )
        return row_max, total, result

    def attend_more(slots, h):
        old_max = m_s[h][:, :1]
        row_max, total, result = attend(q_s[h], slots, h, old_max)
        keep = jnp.exp2((old_max - row_max) * exponent_scale)
        return row_max, total + keep * l_s[h][:, :1], result + keep * acc_s[h]

    def hold(h, row_max, total, result):
        m_s[h] = jnp.broadcast_to(row_max, (rows, HD))
        l_s[h] = jnp.broadcast_to(total, (rows, HD))
        acc_s[h] = result

    def finish(h, row_max, total, result):
        done_s[h] = (result / total).astype(jnp.bfloat16)

    def share(h, queries, slots, share_to, stat_to):
        row_max, total, result = attend(queries, slots, h)
        share_to[...] = (result / total).astype(jnp.bfloat16)
        lane = lax.broadcasted_iota(jnp.int32, (rows, HD), 1)
        stats = jnp.where(lax.rem(lane, 8) < 4, row_max, total)
        stat_to[...] = jnp.transpose(stats)[:8]

    def merge(h, shared, stats):
        row_max, total, result = m_s[h], l_s[h], acc_s[h]
        their_max = jnp.transpose(jnp.broadcast_to(stats[0:1, :], (HD, rows)))
        their_total = jnp.transpose(jnp.broadcast_to(stats[4:5, :], (HD, rows)))
        top = jnp.maximum(row_max, their_max)
        keep = jnp.exp2((row_max - top) * exponent_scale)
        weight = their_total * jnp.exp2((their_max - top) * exponent_scale)
        return top, keep * total + weight, keep * result + weight * shared[...].astype(jnp.float32)

    width = out_ref.shape[1]
    chunk = OUT_CHUNK

    def half_mix(which, first, stop):
        lhs = jnp.concatenate(
            [other_s[h] if which else done_s[h, own_half, :] for h in range(first, stop)], axis=1
        )
        depth = slice((which * heads + first) * HD, (which * heads + stop) * HD)

        def product(n):
            columns = pl.ds(n * chunk, chunk)
            return columns, jnp.dot(lhs, w_s[depth, columns], preferred_element_type=jnp.float32)

        return (product(n) for n in range(width // chunk))

    def mix(first, stop):
        for (columns, own), (_, other) in zip(half_mix(0, first, stop), half_mix(1, first, stop)):
            yield columns, own + other

    def ready(h):
        return jnp.logical_and(h >= 0, h < heads)

    is_slow = jnp.logical_and(is_cut_row, group == 0)
    mix_at = 2 * heads - jnp.where(is_slow, 3, 1)
    mix_gap = is_cut_row.astype(jnp.int32)

    @pl.loop(0, 2 * heads + 2)
    def _(i):
        settled = jnp.where(
            jnp.logical_and(role == 0, i == heads + 1), last, i - heads - jnp.where(is_corner, 3, 2)
        )
        settles = jnp.logical_and(ready(settled), jnp.logical_or(role != 0, i <= 2 * heads))
        held = jnp.logical_and(is_near, settled == tail - 1)
        pl.when(jnp.logical_and(settles, jnp.logical_not(held)))(lambda: send_att(settled).start())
        pl.when(jnp.logical_and(is_near, i == 2 * heads))(lambda: send_att(tail - 1).start())

        @pl.when(i == mix_at)
        def _():
            pltpu.make_async_copy(w_hbm, w_s, w_sem).wait()
            recv_att(0, first_heads, 0)
            for columns, value in mix(0, first_heads):
                mixed_s[:, columns] = value

        @pl.when(i == mix_at + mix_gap)
        def _():
            recv_att(first_heads, early_heads, 1)
            for columns, value in mix(first_heads, early_heads):
                mixed_s[:, columns] += value

        @pl.when(jnp.logical_and(i < heads, jnp.logical_or(is_outer_row, i > 0)))
        def _():
            arrive(pal, i)
            pl.when(jnp.logical_and(is_cut_row, i < last))(lambda: cross(pal, i).start())

        @pl.when(is_cut_row)
        def _():
            @pl.when(i == 0)
            def _():
                for part in range(2):
                    arrive(pal, 0, part, FIRST_OWN)
                    cross(pal, 0, part, FIRST_CROSSED).start()
                arrive(side, 0)
                cross(side, 0).start()
                arrive(straight, last)
                up_down(straight, last).start()

            def pass_on(h):
                arrive(side, h)
                cross(side, h).start()

            def take(from_pal, h):
                if from_pal:
                    for part in range(2) if h == 0 else (None,):
                        arrive(swapped, h, part, FIRST_CROSSED)
                    up_down(swapped, h).start()
                else:
                    arrive(far, h)
                    if h < tail:
                        to_pal(far, h, way=3).start()

            at = 0
            for place, (from_pal, h) in enumerate(crossing_order(heads)):
                at = max(at, h)
                if not from_pal and h > 0:
                    pl.when(i == at)(lambda h=h: pass_on(h))
            for place, (from_pal, h) in enumerate(crossing_order(heads)):
                pl.when(i == place + 1)(lambda from_pal=from_pal, h=h: take(from_pal, h))

        @pl.when(is_outer_row)
        def _():
            @pl.when(i == 1)
            def _():
                arrive(straight, last)
                to_pal(straight, last).start()

            def relay(j):
                arrive(swapped, j)
                to_pal(swapped, j).start()

            for place, (from_pal, h) in enumerate(crossing_order(heads)):
                if from_pal:
                    at = place + (3 if h < heads - 3 else 2)
                    pl.when(i == at)(lambda h=h: relay(h))

        nearby = i - heads

        @pl.when(jnp.logical_and(is_near, jnp.logical_and(nearby >= heads - NEAR, nearby < heads)))
        def _():
            send_q(nearby).wait_recv()
            share(nearby, guest_q[nearby], (2, 6), share_out.at[nearby], stat_out.at[nearby])
            for copy in send_share(nearby):
                copy.start()

        @pl.when(jnp.logical_and(is_cut_row, jnp.logical_and(nearby >= tail, nearby < heads)))
        def _():
            index = nearby - tail
            send_pal(q_s.at[nearby], pal_q.at[index], 0, index).wait_recv()
            share(nearby, pal_q[index], (far,), pal_share_out.at[index], pal_stat_out.at[index])
            for copy in send_pal_share(index):
                copy.start()

        @pl.when(jnp.logical_and(i >= 1, i <= heads))
        def _():
            for which in range(2):
                load_w(i - 1, which).start()

        @pl.when(i < heads)
        def _():
            hold(i, *attend(q_s[i], (row_base, row_base + 1), i))

        @pl.when(jnp.logical_and(i < heads, role == 0))
        def _():
            lend_q(i).wait_recv()
            share(i, share_in[i], (1,), share_out.at[i], stat_out.at[i])
            for copy in send_share(i, up_down_device):
                copy.start()

        @pl.when(jnp.logical_and(ready(i - last), is_near))
        def _():
            h = i - last
            for copy in send_share(h):
                copy.wait_recv()
            hold(h, *merge(h, share_in.at[h], stat_in.at[h]))

        @pl.when(jnp.logical_and(role == 0, i == 2))
        def _():
            send_q(last).wait_recv()
            send_q(last, source=guest_q).start()

        @pl.when(jnp.logical_and(is_host, i == heads))
        def _():
            for h in range(tail, last):
                send_q(h).wait_recv()
                send_q(h, source=guest_q, device=pal_device).start()

        @pl.when(is_outer_row)
        def _():
            ending = i - heads - 2

            @pl.when(jnp.logical_and(ready(ending), is_corner))
            def _():
                for copy in send_share(ending):
                    copy.wait_recv()
                finish(ending, *merge(ending, share_in.at[ending], stat_in.at[ending]))

            h = jnp.where(i == heads, last, i - heads - 1)

            @pl.when(jnp.logical_and(i >= heads, i < 2 * heads))
            def _():
                arrive(jnp.where(h == last, swapped, straight), h)
                pl.when(jnp.logical_and(role == 0, h == last))(lambda: up_down(swapped, h, way=3).start())
                state = attend_more((4, 5), h)
                pl.when(role == 0)(lambda: finish(h, *state))
                pl.when(is_corner)(lambda: hold(h, *state))

        ending = i - heads - 1

        is_whole = jnp.logical_and(ending >= 0, ending < tail)
        is_tail = jnp.logical_and(ending >= tail, ending < heads)

        waiting = jnp.where(i == 2 * heads - 1, tail - 1, ending)

        @pl.when(jnp.logical_and(jnp.logical_and(waiting >= 0, waiting < tail), jnp.logical_and(is_near, i != heads + tail)))
        def _():
            arrive(7, waiting)
            finish(waiting, *attend_more((5, 6, 7), waiting))

        @pl.when(jnp.logical_and(is_whole, is_host))
        def _():
            send_q(ending).wait_recv()
            arrive(6, ending)
            share(ending, guest_q[ending], (2, 6), share_out.at[ending], stat_out.at[ending])
            for copy in send_share(ending):
                copy.start()
            finish(ending, *attend_more((6, 7), ending))

        @pl.when(jnp.logical_and(is_tail, is_near))
        def _():
            pl.when(ending == last)(lambda: arrive(5, ending))
            hold(ending, *attend_more((5, 6), ending))

        @pl.when(jnp.logical_and(is_tail, is_host))
        def _():
            hold(ending, *attend_more((7,), ending))

        @pl.when(jnp.logical_and(is_cut_row, is_tail))
        def _():
            index = ending - tail
            for copy in send_pal_share(index):
                copy.wait_recv()
            finish(ending, *merge(ending, pal_share_in.at[index], pal_stat_in.at[index]))

    pl.when(is_corner)(lambda: send_att(last).start())
    for columns, value in half_mix(0, early_heads, heads):
        mixed_s[:, columns] += value
    recv_att(early_heads, heads, 2)
    for columns, value in half_mix(1, early_heads, heads):
        out_ref[:, columns] = (mixed_s[:, columns] + value).astype(out_ref.dtype)

    def drain(way, count):
        tiles_sent = kv.at[pl.ds(0, count)]
        pltpu.make_async_remote_copy(
            src_ref=tiles_sent,
            dst_ref=tiles_sent,
            send_sem=send_sem.at[way],
            recv_sem=recv_sem.at[0, 0],
            device_id={"tm": pal_device},
            device_id_type=MESH,
        ).wait_send()

    def drain_rows(sent, sem):
        pltpu.make_async_remote_copy(
            src_ref=sent,
            dst_ref=sent,
            send_sem=sem,
            recv_sem=recv_sem.at[0, 0],
            device_id={"tm": pal_device},
            device_id_type=MESH,
        ).wait_send()

    pl.when(is_outer_row)(lambda: drain(0, 2))

    @pl.when(is_cut_row)
    def _():
        drain(0, 1)
        drain_rows(kv.at[0, pl.ds(0, tail)], send_sem.at[3])
        drain_rows(pal_q, pal_send_sem.at[0])
        drain_rows(pal_share_out, pal_send_sem.at[1])
        drain_rows(pal_stat_out, pal_send_sem.at[2])

    drain(1, 1)
    drain_rows(other_s, att_send_sem)
    pl.when(role == 0)(lambda: drain_rows(kv.at[0, 0], send_sem.at[3]))
    pl.when(role == 0)(lambda: drain_rows(guest_q.at[0], q_send_sem))
    pl.when(is_host)(lambda: drain_rows(guest_q.at[pl.ds(0, NEAR - 1)], q_send_sem))
    pl.when(jnp.logical_or(is_corner, is_near))(lambda: drain_rows(q_s, q_send_sem))
    pl.when(is_cut_row)(lambda: drain(2, 2))
    for count, sender in ((heads, role == 0), (heads - NEAR, is_host), (NEAR, is_near)):
        pl.when(sender)(lambda count=count: drain_rows(share_out.at[pl.ds(0, count)], share_send_sem.at[0]))
        pl.when(sender)(lambda count=count: drain_rows(stat_out.at[pl.ds(0, count)], share_send_sem.at[1]))


def balanced_call(query_states, key_states, value_states, out_weight):
    rows, half_width = query_states.shape[1:]
    heads = half_width // HD
    depth, width = out_weight.shape
    tiles = lax.axis_size("tm") // 2
    dma = pltpu.SemaphoreType.DMA
    return pl.pallas_call(
        functools.partial(balanced_kernel, tiles),
        out_shape=jax.ShapeDtypeStruct((rows // 2, width), jnp.bfloat16),
        in_specs=[pl.BlockSpec(memory_space=pl.ANY)] * 4,
        out_specs=pl.BlockSpec(memory_space=pltpu.VMEM),
        scratch_shapes=[
            pltpu.VMEM((heads, rows, HD), jnp.bfloat16),
            pltpu.VMEM((heads, rows, HD), jnp.bfloat16),
            pltpu.VMEM((tiles, heads, 2, rows, HD), jnp.bfloat16),
            pltpu.VMEM((depth, width), jnp.bfloat16),
            pltpu.VMEM((heads, rows, HD), jnp.float32),
            pltpu.VMEM((heads, rows, HD), jnp.float32),
            pltpu.VMEM((heads, rows, HD), jnp.float32),
            pltpu.VMEM((rows // 2, width), jnp.float32),
            pltpu.VMEM((heads, rows, HD), jnp.bfloat16),
            pltpu.VMEM((heads, rows // 2, HD), jnp.bfloat16),
            pltpu.VMEM((heads, rows, HD), jnp.bfloat16),
            pltpu.VMEM((heads, rows, HD), jnp.bfloat16),
            pltpu.VMEM((heads, 8, rows), jnp.float32),
            pltpu.VMEM((heads, 8, rows), jnp.float32),
            pltpu.VMEM((NEAR, rows, HD), jnp.bfloat16),
            pltpu.VMEM((NEAR, rows, HD), jnp.bfloat16),
            pltpu.VMEM((NEAR, rows, HD), jnp.bfloat16),
            pltpu.VMEM((NEAR, 8, rows), jnp.float32),
            pltpu.VMEM((NEAR, 8, rows), jnp.float32),
            dma((heads,)),
            dma,
            dma,
            dma((4,)),
            dma((tiles - 2, heads)),
            dma,
            dma((heads,)),
            dma((2,)),
            dma((2, heads)),
            dma((3,)),
            dma((3, NEAR)),
            dma,
            dma((3,)),
        ],
        compiler_params=pltpu.CompilerParams(
            collective_id=0, has_side_effects=True, vmem_limit_bytes=40 * 1024 * 1024
        ),
    )(*(pltpu.with_memory_space_constraint(x, pltpu.HBM) for x in (query_states, key_states, value_states, out_weight)))


def general_call(query_states, key_states, value_states, out_weight):
    rows, half_width = query_states.shape[1:]
    heads = half_width // HD
    depth, width = out_weight.shape
    time_count = lax.axis_size("tm") // (2 * TCOLS)
    return pl.pallas_call(
        functools.partial(general_kernel, time_count, heads),
        out_shape=jax.ShapeDtypeStruct((rows // 2, width), jnp.bfloat16),
        in_specs=[pl.BlockSpec(memory_space=pl.ANY)] * 4,
        out_specs=pl.BlockSpec(memory_space=pltpu.VMEM),
        scratch_shapes=[
            pltpu.VMEM((heads, rows, HD), jnp.bfloat16),
            pltpu.VMEM((11, heads, 2, rows, HD), jnp.bfloat16),
            pltpu.VMEM((depth, width), jnp.bfloat16),
            pltpu.VMEM((heads, rows, HD), jnp.float32),
            pltpu.VMEM((heads, rows, HD), jnp.float32),
            pltpu.VMEM((heads, rows, HD), jnp.float32),
            pltpu.VMEM((heads, rows // 2, HD), jnp.bfloat16),
            pltpu.VMEM((2, heads, rows // 2, HD), jnp.bfloat16),
            pltpu.SemaphoreType.DMA((3, heads)),
            pltpu.SemaphoreType.DMA,
            pltpu.SemaphoreType.DMA((13, heads)),
            pltpu.SemaphoreType.DMA((11, heads)),
            pltpu.SemaphoreType.DMA((heads,)),
            pltpu.SemaphoreType.DMA((heads,)),
        ],
        compiler_params=pltpu.CompilerParams(
            collective_id=0, has_side_effects=True, vmem_limit_bytes=56 * 1024 * 1024
        ),
    )(query_states, key_states, value_states, out_weight)


def per_device(query_states, key_states, value_states, out_weight):
    two_times = lax.axis_size("tm") == 4 * TCOLS and query_states.shape[2] >= 5 * HD
    call = balanced_call if two_times else general_call
    return call(query_states, key_states, value_states, out_weight)


def solution(mesh):
    in_specs = (
        P(("parts", "tm"), None, None),
        P(("parts", "tm"), None, None),
        P(("parts", "tm"), None, None),
        P(),
    )
    out_specs = P(("parts", "tm"), None)
    return jax.shard_map(
        per_device, mesh=mesh, in_specs=in_specs, out_specs=out_specs, check_vma=False
    )
```
